256 devices in a mesh: dp: 32 (over x, z), feat: 8 (over y, core).
Axes of the slice: x: 4, y: 4, z: 8, core: 2. Of those that a mesh axis runs over, the one named last changes fastest.
Arguments:
- hidden_first: bfloat16 [2048, 4096], P('dp', 'feat'), may hold values from -6 to 6
- hidden_second: bfloat16 [2048, 4096], P('dp', 'feat'), may hold values from -11 to 11
- weight: bfloat16 [4096, 8192], P('dp', 'feat'), may hold values from -0.09375 to 0.09375
Outputs:
- total_loss: float32 [], replicated
- grad_weight: bfloat16 [4096, 8192], P('dp', 'feat')
- grad_first: bfloat16 [2048, 4096], P('dp', 'feat')
- grad_second: bfloat16 [2048, 4096], P('dp', 'feat')
The draws below stay inside these ranges and needn't reach their ends.
All inputs are finite; a program needn't handle non-finite values.
Results may differ from the reference program's by a relative error of at most 0.015.
Values may be sent and summed in bfloat16 or wider, within the bound.
No kernel may reach another device: no remote copies, remote signals or barrier semaphores. Data moves between devices by JAX's collectives and lax.ppermute only.
A program may use at most 64 MiB of HBM per device.

```python
import jax
import jax.numpy as jnp
from jax import lax

D_IN = 4096
E = 8192
PAIRS_DEV = 64
PAIRS = 2048
N_DP = 32


def draw_hidden_second(key, part):
    position = jnp.arange(PAIRS, dtype=jnp.float32) / max(PAIRS - 1, 1)
    row_scale = 0.6 * jnp.exp(position * jnp.log(3.0))
    values = jnp.clip(jax.random.normal(key, (PAIRS, D_IN), jnp.float32), -6.0, 6.0)
    return (values * row_scale[:, None]).astype(jnp.bfloat16)


def spiked(array, stream_key, source, target, parts, factor):
    def block_of(dim):
        return (jnp.arange(array.shape[dim]) // (array.shape[dim] // parts)).reshape((-1,) + (1,) * (array.ndim - 1 - dim))

    near = jax.random.permutation(stream_key, parts)[block_of(target)]
    second = (block_of(target) + parts // 2) % parts
    return jnp.where((block_of(source) == near) | (block_of(source) == second), factor * array, array)


def block_scale(stream_key, extent, shards, low, top_value):
    gain = 1.0
    for dim, parts in shards:
        steps = jax.random.uniform(jax.random.fold_in(jax.random.fold_in(stream_key, 6), dim), (parts,), jnp.float32, low / len(shards), top_value / len(shards))
        gain = gain * jnp.repeat(jnp.exp(steps), extent[dim] // parts).reshape((-1,) + (1,) * (len(extent) - 1 - dim))
    return gain


def bell_draw(own_key, extent, width, reach, shards=(), kind=jnp.bfloat16):
    drawn = width * jax.random.normal(own_key, extent, jnp.float32)
    if shards:
        drawn = drawn * block_scale(own_key, extent, shards, -0.22, 0.18)
    return jnp.clip(drawn, -reach, reach).astype(kind)


def noise_with(stream_key, extent, width, most, cuts, heavy, held_as=jnp.bfloat16):
    array = width * jax.random.normal(stream_key, extent, jnp.float32)
    if cuts:
        array = array * block_scale(stream_key, extent, cuts, -0.22, 0.18)
    return jnp.clip(spiked(array, jax.random.fold_in(stream_key, 3), *heavy), -most, most).astype(held_as)


def setup_inputs(seed: int = 0) -> dict:
    streams_of = jax.random.split(jax.random.key(seed), 4)
    hidden_first = noise_with(streams_of[0], (PAIRS, D_IN), 0.95, 6.0, ((0, 32), (1, 8)), (0, 1, 32, 2.75))
    hidden_second = draw_hidden_second(jax.random.fold_in(streams_of[3], 71), 0)
    weight = bell_draw(streams_of[2], (D_IN, E), D_IN ** -0.5, 0.09375, ((0, 32), (1, 8)))
    return {"hidden_first": hidden_first, "hidden_second": hidden_second, "weight": weight}


def reference(hidden_first, hidden_second, weight):
    total_rows = PAIRS * 1.0
    full_width = E * 1.0
    first_out = jnp.dot(hidden_first, weight, preferred_element_type=jnp.float32)
    second_out = jnp.dot(hidden_second, weight, preferred_element_type=jnp.float32)
    views = jnp.stack([first_out, second_out])
    col_mean = lax.optimization_barrier(jnp.mean(views, axis=1, keepdims=True))
    centered = views - col_mean
    variance = lax.optimization_barrier(jnp.sum(centered * centered, axis=1)) / (total_rows - 1.0)
    deviation = jnp.sqrt(variance + 0.0001)
    centered_half = centered.astype(jnp.bfloat16)
    wide_half = centered_half.astype(jnp.float32)

    def gram_block(group):
        block = lax.dynamic_slice_in_dim(wide_half, (group * PAIRS_DEV).astype(jnp.int32), PAIRS_DEV, 1)
        gram_part = jnp.einsum('vrc,vnc->vrn', block, wide_half, precision=lax.Precision.HIGHEST)
        squares = jnp.sum(gram_part * gram_part)
        gram_half = lax.optimization_barrier(gram_part.astype(jnp.bfloat16))
        spread_part = jnp.einsum('vrn,vnc->vrc', gram_half.astype(jnp.float32), wide_half, precision=lax.Precision.HIGHEST)
        return (squares, spread_part)
    squares, spread = lax.map(gram_block, jnp.arange(N_DP, dtype=jnp.int32))
    spread = jnp.transpose(spread, (1, 0, 2, 3)).reshape(2, PAIRS, E)
    frobenius = jnp.sum(squares)
    difference = views[0] - views[1]
    total_loss = 25.0 * jnp.sum(difference * difference) / (total_rows * full_width) + 25.0 * jnp.sum(jax.nn.relu(1.0 - deviation)) / full_width + (frobenius / (total_rows - 1.0) ** 2 - jnp.sum(variance * variance)) / full_width
    inv_grad = 50.0 / 256.0 * jnp.stack([difference, -difference])
    binding = (deviation < 1.0).astype(jnp.float32)
    hinge_grad = -(25.0 * total_rows / (256.0 * (total_rows - 1.0))) * (binding / deviation)[:, None, :] * centered
    cov_grad = 4.0 * total_rows / 256.0 * (spread / (total_rows - 1.0) ** 2 - variance[:, None, :] * centered / (total_rows - 1.0))
    grad_views = (inv_grad + hinge_grad + cov_grad).astype(jnp.bfloat16)
    grad_first = jnp.dot(grad_views[0], weight.T, preferred_element_type=jnp.float32).astype(jnp.bfloat16)
    grad_second = jnp.dot(grad_views[1], weight.T, preferred_element_type=jnp.float32).astype(jnp.bfloat16)

    def weight_step(running, group):
        offset = (group * PAIRS_DEV).astype(jnp.int32)
        first_rows = lax.dynamic_slice_in_dim(hidden_first, offset, PAIRS_DEV, 0)
        second_rows = lax.dynamic_slice_in_dim(hidden_second, offset, PAIRS_DEV, 0)
        first_grads = lax.dynamic_slice_in_dim(grad_views[0], offset, PAIRS_DEV, 0)
        second_grads = lax.dynamic_slice_in_dim(grad_views[1], offset, PAIRS_DEV, 0)
        term = jnp.dot(first_rows.T, first_grads, preferred_element_type=jnp.float32) + jnp.dot(second_rows.T, second_grads, preferred_element_type=jnp.float32)
        return (running + term.astype(jnp.bfloat16).astype(jnp.float32), None)
    summed, _ = lax.scan(weight_step, jnp.zeros((D_IN, E), jnp.float32), jnp.arange(N_DP, dtype=jnp.int32))
    grad_weight = summed.astype(jnp.bfloat16)
    return (total_loss, grad_weight, grad_first, grad_second)
```

```python
import jax
import jax.numpy as jnp
from jax import lax
from jax.sharding import Mesh, PartitionSpec as P

BF = jnp.bfloat16
F32 = jnp.float32
NX, NZ, NY, NC = 4, 8, 4, 2
FEAT = ("y", "c")
CHIPS = ("x", "y")


def swap_xy(v):
    pairs = [(a * NY + b, b * NX + a) for a in range(NX) for b in range(NY)]
    return lax.ppermute(v, ("x", "y"), pairs)


def swap_core(v):
    return lax.ppermute(v, "c", [(0, 1), (1, 0)])


def split3(v):
    hi = v.astype(BF)
    rest = v - hi.astype(F32)
    mid = rest.astype(BF)
    low = (rest - mid.astype(F32)).astype(BF)
    return hi, mid, low


def dot(a, b, ca, cb):
    return lax.dot_general(a, b, (((ca,), (cb,)), ((), ())), preferred_element_type=F32)


def on_device(hidden_first, hidden_second, weight):
    core = lax.axis_index("c")
    rows, kpart = hidden_first.shape
    cols = weight.shape[1]
    total_rows = rows * NX * NZ * 1.0
    full_width = cols * NY * NC * 1.0
    blk = rows * NX
    kq = kpart * NC
    sub = cols // NX

    wq = lax.all_gather(weight, "z", axis=0, tiled=True)
    moved = swap_xy(jnp.stack([hidden_first, hidden_second]))

    def whole_quarter(v):
        got = lax.all_gather(v, FEAT, axis=0, tiled=False)
        got = got.reshape(NY, NC, rows, kpart)
        return jnp.transpose(got, (0, 2, 1, 3)).reshape(blk, kq)

    hq = jnp.concatenate([whole_quarter(moved[0]), whole_quarter(moved[1])], axis=0)

    row_sum = lax.psum(jnp.sum(hq.reshape(2, blk, kq).astype(F32), axis=1), "z")
    mean_in = row_sum / total_rows
    mean_rows = jnp.concatenate(split3(mean_in), axis=0)
    mean_terms = dot(mean_rows, wq, 1, 0)
    mean_part = mean_terms[0:2] + mean_terms[2:4] + mean_terms[4:6]

    part = dot(hq, wq, 1, 0).reshape(2, blk, cols) - mean_part[:, None, :]
    part = part.astype(BF).reshape(2 * blk, NX, sub)
    part = jnp.transpose(part, (1, 0, 2))
    parts = lax.all_to_all(part, "x", split_axis=0, concat_axis=0, tiled=True)
    centered = jnp.sum(parts.astype(F32), axis=0).reshape(2, blk, sub)

    half = centered.astype(BF)
    mine = jnp.where(core == 0, half[0], half[1])
    theirs = jnp.where(core == 0, half[1], half[0])
    own_rows = jnp.concatenate([mine, swap_core(theirs)], axis=1)
    gathered = lax.all_gather(own_rows, "z", axis=0, tiled=True)

    mean_cols = lax.psum_scatter(
        mean_part.reshape(2, NX, sub).transpose(1, 0, 2), "x", scatter_dimension=0, tiled=True
    )[0]
    difference = centered[0] - centered[1] + (mean_cols[0] - mean_cols[1])[None, :]

    wide = gathered.astype(F32)
    var_view = jnp.sum(wide * wide, axis=0) / (total_rows - 1.0)
    dev_view = jnp.sqrt(var_view + 0.0001)
    var_own = var_view[:sub]
    var_back = swap_core(var_view[sub:].reshape(1, sub))[0]

    gram_part = dot(own_rows, gathered, 1, 1).astype(BF)
    pieces = lax.all_to_all(
        gram_part.reshape(NX * NY, blk // (NX * NY), -1), CHIPS, split_axis=0, concat_axis=0, tiled=True
    )
    gram_rows = jnp.sum(pieces.astype(F32), axis=0)
    gram_half = lax.all_gather(gram_rows.astype(BF), CHIPS, axis=0, tiled=True)
    spread_view = dot(gram_half, gathered, 1, 0)
    spread_own = spread_view[:, :sub]
    spread_back = swap_core(spread_view[:, sub:])

    first = core == 0
    spread = jnp.stack(
        [jnp.where(first, spread_own, spread_back), jnp.where(first, spread_back, spread_own)]
    )
    variance = jnp.stack([jnp.where(first, var_own, var_back), jnp.where(first, var_back, var_own)])
    deviation = jnp.sqrt(variance + 0.0001)

    inv_grad = 50.0 / 256.0 * jnp.stack([difference, -difference])
    binding = (deviation < 1.0).astype(F32)
    hinge_grad = (
        -(25.0 * total_rows / (256.0 * (total_rows - 1.0)))
        * (binding / deviation)[:, None, :]
        * centered
    )
    cov_grad = (
        4.0
        * total_rows
        / 256.0
        * (spread / (total_rows - 1.0) ** 2 - variance[:, None, :] * centered / (total_rows - 1.0))
    )
    grad_views = (inv_grad + hinge_grad + cov_grad).astype(BF).reshape(2 * blk, sub)
    grads = lax.all_gather(grad_views, "x", axis=1, tiled=True)

    weight_part = dot(hq, grads, 0, 0).astype(BF)
    grad_weight = lax.psum_scatter(weight_part, "z", scatter_dimension=0, tiled=True)

    input_part = dot(grads, wq, 1, 1).astype(BF)
    input_part = input_part.reshape(2, NX, rows, NC, kpart).transpose(1, 3, 0, 2, 4)
    input_part = input_part.reshape(NX * NC, 2, rows, kpart)
    input_parts = lax.all_to_all(input_part, FEAT, split_axis=0, concat_axis=0, tiled=True)
    input_grads = swap_xy(jnp.sum(input_parts.astype(F32), axis=0).astype(BF))

    share = (
        25.0 * jnp.sum(difference * difference) / (total_rows * full_width)
        + 25.0 * jnp.sum(jax.nn.relu(1.0 - dev_view)) / (full_width * NZ)
        + (
            jnp.sum(gram_rows * gram_rows) / (total_rows - 1.0) ** 2
            - jnp.sum(var_view * var_view) / NZ
        )
        / full_width
    )
    total_loss = lax.psum(lax.psum(lax.psum(share, "x"), FEAT), "z")
    return (total_loss, grad_weight, input_grads[0], input_grads[1])


def solution(mesh):
    grid = Mesh(mesh.devices.reshape(NX, NZ, NY, NC), ("x", "z", "y", "c"))
    placed = P(("x", "z"), ("y", "c"))
    return jax.shard_map(
        on_device,
        mesh=grid,
        in_specs=(placed, placed, placed),
        out_specs=(P(), placed, placed, placed),
        check_vma=False,
    )
```

```python
import jax
import jax.numpy as jnp
from jax import lax
from jax.sharding import Mesh, PartitionSpec as P

BF = jnp.bfloat16
F32 = jnp.float32
NX, NZ, NY, NC = 4, 8, 4, 2
CHIPS = ("x", "y")


def swap_xy(v):
    pairs = [(a * NY + b, b * NX + a) for a in range(NX) for b in range(NY)]
    return lax.ppermute(v, ("x", "y"), pairs)


def swap_core(v):
    return lax.ppermute(v, "c", [(0, 1), (1, 0)])


def shift(v, axis, n, k):
    return lax.ppermute(v, axis, [(i, (i + k) % n) for i in range(n)])


def butterfly(v, axis, n):
    step = 1
    while step < n:
        v = v + lax.ppermute(v, axis, [(i, i ^ step) for i in range(n)])
        step *= 2
    return v


def ring_gather(pieces, axis, n):
    h = n // 2
    got = [[None, None] for _ in range(n)]
    got[0] = list(pieces)
    for k in range(1, h + 1):
        for p in (0, 1):
            if k < h or p == 0:
                got[-k % n][p] = shift(got[(1 - k) % n][p], axis, n, 1)
            if k < h or p == 1:
                got[k][p] = shift(got[k - 1][p], axis, n, -1)
    return got


def ring_scatter(parts, axis, n):
    h = n // 2
    run = {}
    for d in range(h, 0, -1):
        for p in (0, 1):
            for way in (1, -1):
                if d == h and (p == 0) != (way == 1):
                    continue
                term = parts[(way * d) % n][p]
                if (p, way) in run:
                    term = term + run[(p, way)].astype(F32)
                run[(p, way)] = shift(term.astype(BF), axis, n, way)
    return [parts[0][p] + run[(p, 1)].astype(F32) + run[(p, -1)].astype(F32) for p in (0, 1)]


def split3(v):
    hi = v.astype(BF)
    rest = v - hi.astype(F32)
    mid = rest.astype(BF)
    low = (rest - mid.astype(F32)).astype(BF)
    return hi, mid, low


def roll_left(v, axis, amount):
    size = v.shape[axis]
    return lax.dynamic_slice_in_dim(jnp.concatenate([v, v], axis=axis), amount, size, axis)


def dot(a, b, ca, cb):
    return lax.dot_general(a, b, (((ca,), (cb,)), ((), ())), preferred_element_type=F32)


def on_device(hidden_first, hidden_second, weight):
    xi = lax.axis_index("x")
    zi = lax.axis_index("z")
    yi = lax.axis_index("y")
    core = lax.axis_index("c")
    first = core == 0
    rows, kpart = hidden_first.shape
    kz, cols = weight.shape
    total_rows = rows * NX * NZ * 1.0
    full_width = cols * NY * NC * 1.0
    blk = rows * NX
    kq = kpart * NC
    sub = cols // NX
    half = kz // 2

    shard = roll_left(weight, 1, xi * sub)
    wgot = ring_gather((shard[:half], shard[half:]), "z", NZ)
    w_near = jnp.concatenate([q for k in (0, 1, 2, 3, 5, 6, 7) for q in wgot[k]], axis=0)
    w_far = jnp.concatenate(wgot[4], axis=0)
    w_rel = jnp.concatenate([w_near[: 4 * kz], w_far, w_near[4 * kz :]], axis=0)
    w_abs = roll_left(w_rel, 0, (NZ - zi) % NZ * kz)

    moved = swap_xy(jnp.stack([hidden_first, hidden_second]))

    def both_cores(v):
        other = swap_core(v)
        return jnp.concatenate([jnp.where(first, v, other), jnp.where(first, other, v)], axis=-1)

    wide_rows = roll_left(both_cores(moved), 2, zi * kz)
    hgot = ring_gather((wide_rows[0], wide_rows[1]), "y", NY)

    def in_order(p):
        out = jnp.zeros((NY, rows, kq), BF)
        for k in range(NY):
            out = lax.dynamic_update_slice_in_dim(out, hgot[k][p][None], (yi + k) % NY, 0)
        return out.reshape(blk, kq)

    hq = jnp.concatenate([in_order(0), in_order(1)], axis=0)

    sums = butterfly(butterfly(jnp.sum(moved.astype(F32), axis=1), "y", NY), "z", NZ)
    mean_in = roll_left(both_cores(sums), 1, zi * kz) / total_rows
    mean_rows = jnp.concatenate(split3(mean_in), axis=0)
    mean_terms = dot(mean_rows, w_rel, 1, 0)
    mean_part = mean_terms[0:2] + mean_terms[2:4] + mean_terms[4:6]

    h_near = jnp.concatenate([hq[:, : 4 * kz], hq[:, 5 * kz :]], axis=1)
    h_far = hq[:, 4 * kz : 5 * kz]
    part = (dot(h_near, w_near, 1, 0) + dot(h_far, w_far, 1, 0)).reshape(2, blk, cols) - mean_part[:, None, :]
    terms = [[part[p, :, k * sub : (k + 1) * sub] for p in (0, 1)] for k in range(NX)]
    centered = jnp.stack(ring_scatter(terms, "x", NX))

    rounded = centered.astype(BF)
    mine = jnp.where(first, rounded[0], rounded[1])
    theirs = jnp.where(first, rounded[1], rounded[0])
    own_rows = jnp.concatenate([mine, swap_core(theirs)], axis=1)
    cgot = ring_gather((own_rows[: blk // 2], own_rows[blk // 2 :]), "z", NZ)
    c_near = jnp.concatenate([q for k in (0, 1, 2, 3, 5, 6, 7) for q in cgot[k]], axis=0)
    c_far = jnp.concatenate(cgot[4], axis=0)

    mean_cols = mean_part[:, :sub]
    for k in range(1, NX):
        mean_cols = mean_cols + shift(mean_part[:, k * sub : (k + 1) * sub], "x", NX, k)
    difference = centered[0] - centered[1] + (mean_cols[0] - mean_cols[1])[None, :]

    gram_part = jnp.concatenate(
        [dot(own_rows, c_near, 1, 1).astype(BF), dot(own_rows, c_far, 1, 1).astype(BF)], axis=1
    )
    pieces = lax.all_to_all(
        gram_part.reshape(NX * NY, blk // (NX * NY), -1), CHIPS, split_axis=0, concat_axis=0, tiled=True
    )
    gram_rows = jnp.sum(pieces.astype(F32), axis=0)
    spare = jnp.broadcast_to(gram_rows.astype(BF)[None], pieces.shape)
    gram_half = lax.all_to_all(spare, CHIPS, split_axis=0, concat_axis=0, tiled=True).reshape(blk, -1)

    near_wide = c_near.astype(F32)
    far_wide = c_far.astype(F32)
    var_view = (jnp.sum(near_wide * near_wide, axis=0) + jnp.sum(far_wide * far_wide, axis=0)) / (
        total_rows - 1.0
    )
    dev_view = jnp.sqrt(var_view + 0.0001)
    var_own = var_view[:sub]
    var_back = swap_core(var_view[sub:].reshape(1, sub))[0]

    near = c_near.shape[0]
    spread_view = dot(gram_half[:, :near], c_near, 1, 0) + dot(gram_half[:, near:], c_far, 1, 0)
    spread_own = spread_view[:, :sub]
    spread_back = swap_core(spread_view[:, sub:])
    spread = jnp.stack(
        [jnp.where(first, spread_own, spread_back), jnp.where(first, spread_back, spread_own)]
    )
    variance = jnp.stack([jnp.where(first, var_own, var_back), jnp.where(first, var_back, var_own)])
    deviation = jnp.sqrt(variance + 0.0001)

    inv_grad = 50.0 / 256.0 * jnp.stack([difference, -difference])
    binding = (deviation < 1.0).astype(F32)
    hinge_grad = (
        -(25.0 * total_rows / (256.0 * (total_rows - 1.0)))
        * (binding / deviation)[:, None, :]
        * centered
    )
    cov_grad = (
        4.0
        * total_rows
        / 256.0
        * (spread / (total_rows - 1.0) ** 2 - variance[:, None, :] * centered / (total_rows - 1.0))
    )
    grad_views = (inv_grad + hinge_grad + cov_grad).astype(BF)
    ggot = ring_gather((grad_views[0], grad_views[1]), "x", NX)
    grads = jnp.concatenate(
        [jnp.concatenate([ggot[k][p] for k in range(NX)], axis=1) for p in (0, 1)], axis=0
    )

    weight_terms = []
    for k in range(NZ):
        term = dot(hq[:, k * kz : (k + 1) * kz], grads, 0, 0)
        weight_terms.append((term[:half], term[half:]))
    grad_weight = jnp.concatenate(ring_scatter(weight_terms, "z", NZ), axis=0).astype(BF)
    grad_weight = roll_left(grad_weight, 1, (NX - xi) % NX * sub)

    input_part = dot(grads, w_abs, 1, 1)
    kept = jnp.where(first, input_part[:, :kpart], input_part[:, kpart:])
    sent = jnp.where(first, input_part[:, kpart:], input_part[:, :kpart])
    input_sum = (kept + swap_core(sent.astype(BF)).astype(F32)).reshape(2, NY, rows, kpart)
    input_terms = []
    for k in range(NY):
        term = lax.dynamic_slice_in_dim(input_sum, (yi + k) % NY, 1, 1)[:, 0]
        input_terms.append((term[0], term[1]))
    input_grads = swap_xy(jnp.stack(ring_scatter(input_terms, "y", NY)).astype(BF))

    share = (
        25.0 * jnp.sum(difference * difference) / (total_rows * full_width)
        + 25.0 * jnp.sum(jax.nn.relu(1.0 - dev_view)) / (full_width * NZ)
        + (
            jnp.sum(gram_rows * gram_rows) / (total_rows - 1.0) ** 2
            - jnp.sum(var_view * var_view) / NZ
        )
        / full_width
    )
    total_loss = share.reshape(1, 1)
    for axis, n in (("c", NC), ("x", NX), ("y", NY), ("z", NZ)):
        total_loss = butterfly(total_loss, axis, n)
    return (total_loss[0, 0], grad_weight, input_grads[0], input_grads[1])


def solution(mesh):
    grid = Mesh(mesh.devices.reshape(NX, NZ, NY, NC), ("x", "z", "y", "c"))
    placed = P(("x", "z"), ("y", "c"))
    return jax.shard_map(
        on_device,
        mesh=grid,
        in_specs=(placed, placed, placed),
        out_specs=(P(), placed, placed, placed),
        check_vma=False,
    )
```

```python
import jax
import jax.numpy as jnp
from jax import lax
from jax.experimental import pallas as pl
from jax.experimental.pallas import tpu as pltpu
from jax.sharding import Mesh, PartitionSpec as P

BF = jnp.bfloat16
F32 = jnp.float32
NX, NZ, NY, NC = 4, 8, 4, 2
FEAT = ("y", "c")
CHIPS = ("x", "y")
EXTRA = 16


def swap_xy(v):
    pairs = [(a * NY + b, b * NX + a) for a in range(NX) for b in range(NY)]
    return lax.ppermute(v, ("x", "y"), pairs)


def swap_core(v):
    return lax.ppermute(v, "c", [(0, 1), (1, 0)])


def spread_out(v, axes, n):
    return lax.all_to_all(
        jnp.broadcast_to(v[None], (n,) + v.shape), axes, split_axis=0, concat_axis=0, tiled=True
    )


def split3(v):
    hi = v.astype(BF)
    rest = v - hi.astype(F32)
    mid = rest.astype(BF)
    low = (rest - mid.astype(F32)).astype(BF)
    return hi, mid, low


def dot(a, b, ca, cb):
    return lax.dot_general(a, b, (((ca,), (cb,)), ((), ())), preferred_element_type=F32)


def whole(shape):
    return pl.BlockSpec(shape, lambda j: (0,) * len(shape))


def views_kernel(h_ref, m_ref, w_ref, out_ref):
    ny, nc, nv, rows, kpart = h_ref.shape
    flat = ny * nv * rows
    acc = dot(h_ref[:, 0].reshape(flat, kpart), w_ref[:kpart], 1, 0)
    acc = acc + dot(h_ref[:, 1].reshape(flat, kpart), w_ref[kpart:], 1, 0)
    terms = dot(m_ref[...], w_ref[...], 1, 0)
    mean = terms[0:2] + terms[2:4] + terms[4:6]
    for a in range(ny):
        for v in range(nv):
            lo = (a * nv + v) * rows
            out_ref[0, lo : lo + rows] = (acc[lo : lo + rows] - mean[v : v + 1]).astype(BF)
    hi, mid, low = split3(mean)
    pad = jnp.zeros((EXTRA - 6, mean.shape[1]), F32)
    tail = jnp.concatenate([hi.astype(F32), mid.astype(F32), low.astype(F32), pad], axis=0)
    out_ref[0, flat : flat + EXTRA] = tail.astype(BF)


def weight_kernel(h_ref, g_ref, out_ref):
    ny, nc, nv, rows, kpart = h_ref.shape
    flat = ny * nv * rows
    for c in range(nc):
        out_ref[c * kpart : (c + 1) * kpart] = dot(
            h_ref[:, c].reshape(flat, kpart), g_ref[0], 0, 0
        ).astype(BF)


def input_kernel(g_ref, w_ref, out_ref):
    ny, _, nv, rows, kpart = out_ref.shape
    nx, _, sub = g_ref.shape
    acc = dot(g_ref[0], w_ref[:, :sub], 1, 1)
    for k in range(1, nx):
        acc = acc + dot(g_ref[k], w_ref[:, k * sub : (k + 1) * sub], 1, 1)
    out_ref[:, 0] = acc.astype(BF).reshape(ny, nv, rows, kpart)


def on_device(hidden_first, hidden_second, weight):
    core = lax.axis_index("c")
    first = core == 0
    rows, kpart = hidden_first.shape
    cols = weight.shape[1]
    total_rows = rows * NX * NZ * 1.0
    full_width = cols * NY * NC * 1.0
    blk = rows * NX
    kq = kpart * NC
    sub = cols // NX
    flat = 2 * blk

    wq = lax.all_gather(weight, "z", axis=0, tiled=True)
    moved = swap_xy(jnp.stack([hidden_first, hidden_second]))
    hq = spread_out(moved, FEAT, NY * NC).reshape(NY, NC, 2, rows, kpart)
    row_sum = jnp.sum(hq.astype(F32), axis=(0, 3)).transpose(1, 0, 2).reshape(2, kq)
    mean_in = lax.psum(row_sum, "z") / total_rows
    mean_rows = jnp.concatenate(split3(mean_in) + (jnp.zeros((EXTRA - 6, kq), BF),), axis=0)

    part = pl.pallas_call(
        views_kernel,
        grid=(NX,),
        in_specs=[
            whole(hq.shape),
            whole(mean_rows.shape),
            pl.BlockSpec((kq, sub), lambda j: (0, j)),
        ],
        out_specs=pl.BlockSpec((1, flat + EXTRA, sub), lambda j: (j, 0, 0)),
        out_shape=jax.ShapeDtypeStruct((NX, flat + EXTRA, sub), BF),
        name="views",
    )(hq, mean_rows, wq)
    parts = lax.all_to_all(part, "x", split_axis=0, concat_axis=0, tiled=True)
    summed = jnp.sum(parts.astype(F32), axis=0)
    centered = summed[:flat].reshape(NX, 2, rows, sub).transpose(1, 0, 2, 3).reshape(2, blk, sub)
    mean_cols = summed[flat : flat + 2] + summed[flat + 2 : flat + 4] + summed[flat + 4 : flat + 6]

    half = centered.astype(BF)
    mine = jnp.where(first, half[0], half[1])
    theirs = jnp.where(first, half[1], half[0])
    own_rows = jnp.concatenate([mine, swap_core(theirs)], axis=1)
    gathered = lax.all_gather(own_rows, "z", axis=0, tiled=True)

    variance = lax.psum(jnp.sum(centered * centered, axis=1), "z") / (total_rows - 1.0)
    deviation = jnp.sqrt(variance + 0.0001)
    difference = centered[0] - centered[1] + (mean_cols[0] - mean_cols[1])[None, :]
    share = (
        25.0 * jnp.sum(difference * difference) / (total_rows * full_width)
        + 25.0 * jnp.sum(jax.nn.relu(1.0 - deviation)) / (full_width * NZ)
        - jnp.sum(variance * variance) / (full_width * NZ)
    )
    share = lax.psum(lax.psum(share, "x"), "y")
    gathered, share, difference = lax.optimization_barrier((gathered, share, difference))

    gram_part = dot(own_rows, gathered, 1, 1).astype(BF)
    pieces = lax.all_to_all(
        gram_part.reshape(NX * NY, blk // (NX * NY), -1), CHIPS, split_axis=0, concat_axis=0, tiled=True
    )
    gram_rows = jnp.sum(pieces.astype(F32), axis=0).astype(BF)
    gram_half = spread_out(gram_rows, CHIPS, NX * NY).reshape(blk, -1)
    spread_view = dot(gram_half, gathered, 1, 0)
    spread_own = spread_view[:, :sub]
    spread_back = swap_core(spread_view[:, sub:])
    spread = jnp.stack(
        [jnp.where(first, spread_own, spread_back), jnp.where(first, spread_back, spread_own)]
    )

    inv_grad = 50.0 / 256.0 * jnp.stack([difference, -difference])
    binding = (deviation < 1.0).astype(F32)
    hinge_grad = (
        -(25.0 * total_rows / (256.0 * (total_rows - 1.0)))
        * (binding / deviation)[:, None, :]
        * centered
    )
    cov_grad = (
        4.0
        * total_rows
        / 256.0
        * (spread / (total_rows - 1.0) ** 2 - variance[:, None, :] * centered / (total_rows - 1.0))
    )
    grad_views = (inv_grad + hinge_grad + cov_grad).astype(BF)
    grad_views = grad_views.reshape(2, NX, rows, sub).transpose(1, 0, 2, 3).reshape(flat, sub)
    grads = spread_out(grad_views, "x", NX)

    weight_part = pl.pallas_call(
        weight_kernel,
        grid=(NX,),
        in_specs=[whole(hq.shape), pl.BlockSpec((1, flat, sub), lambda j: (j, 0, 0))],
        out_specs=pl.BlockSpec((kq, sub), lambda j: (0, j)),
        out_shape=jax.ShapeDtypeStruct((kq, cols), BF),
        name="weight_terms",
    )(hq, grads)
    grad_weight = lax.psum_scatter(weight_part, "z", scatter_dimension=0, tiled=True)

    input_part = pl.pallas_call(
        input_kernel,
        grid=(NC,),
        in_specs=[whole(grads.shape), pl.BlockSpec((kpart, cols), lambda j: (j, 0))],
        out_specs=pl.BlockSpec((NY, 1, 2, rows, kpart), lambda j: (0, j, 0, 0, 0)),
        out_shape=jax.ShapeDtypeStruct((NY, NC, 2, rows, kpart), BF),
        name="input_terms",
    )(grads, wq)
    input_parts = lax.all_to_all(
        input_part.reshape(NY * NC, 2, rows, kpart), FEAT, split_axis=0, concat_axis=0, tiled=True
    )
    input_grads = swap_xy(jnp.sum(input_parts.astype(F32), axis=0).astype(BF))

    wide = gram_half.astype(F32)
    share = share + jnp.sum(wide * wide) / ((total_rows - 1.0) ** 2 * full_width)
    share = share.reshape(1, 1)
    total_loss = lax.psum(share + swap_core(share), "z")
    return (total_loss[0, 0], grad_weight, input_grads[0], input_grads[1])


def solution(mesh):
    grid = Mesh(mesh.devices.reshape(NX, NZ, NY, NC), ("x", "z", "y", "c"))
    placed = P(("x", "z"), ("y", "c"))
    return jax.shard_map(
        on_device,
        mesh=grid,
        in_specs=(placed, placed, placed),
        out_specs=(P(), placed, placed, placed),
        check_vma=False,
    )
```

```python
import jax
import jax.numpy as jnp
from jax import lax
from jax.experimental import pallas as pl
from jax.experimental.pallas import tpu as pltpu
from jax.sharding import Mesh, PartitionSpec as P

BF = jnp.bfloat16
F32 = jnp.float32
NX, NZ, NY, NC = 4, 8, 4, 2
CHIPS = ("x", "y")
SMEM = pltpu.SMEM


def swap_core(v):
    return lax.ppermute(v, "c", [(0, 1), (1, 0)])


def exchange(v, axes):
    return lax.all_to_all(v, axes, split_axis=0, concat_axis=0, tiled=True)


def spread_out(v, axes, n):
    return exchange(jnp.broadcast_to(v[None], (n,) + v.shape), axes)


def split3(v):
    hi = v.astype(BF)
    rest = v - hi.astype(F32)
    mid = rest.astype(BF)
    low = (rest - mid.astype(F32)).astype(BF)
    return hi, mid, low


def dot(a, b, ca, cb):
    return lax.dot_general(a, b, (((ca,), (cb,)), ((), ())), preferred_element_type=F32)


def fixed(shape):
    return pl.BlockSpec(shape, lambda j: (0,) * len(shape))


def at_dim(shape, dim):
    return pl.BlockSpec(shape, lambda j: tuple(j if d == dim else 0 for d in range(len(shape))))


def flat_rows(ref):
    nx, _, nv, rows, width = ref.shape
    return ref[:, 0].reshape(nx * nv * rows, width)


def views_kernel(core_ref, own_ref, oth_ref, m_ref, w_ref, cen_ref, mine_ref, theirs_ref, stat_ref, acc, macc):
    step = pl.program_id(0)
    core = core_ref[0]
    nx, _, nv, rows, _ = own_ref.shape
    w_own = w_ref[0, core]
    w_oth = w_ref[0, 1 - core]
    term = dot(flat_rows(own_ref), w_own, 1, 0) + dot(flat_rows(oth_ref), w_oth, 1, 0)
    mterm = dot(m_ref[0, 0], w_own, 1, 0) + dot(m_ref[0, 1], w_oth, 1, 0)

    @pl.when(step == 0)
    def _():
        acc[...] = term
        macc[...] = mterm

    @pl.when(step > 0)
    def _():
        acc[...] += term
        macc[...] += mterm

    @pl.when(step == pl.num_programs(0) - 1)
    def _():
        terms = macc[...]
        mean = terms[0:2] + terms[2:4] + terms[4:6]
        sums = []
        for v in range(nv):
            total = jnp.zeros((1, mean.shape[1]), F32)
            for a in range(nx):
                lo = (a * nv + v) * rows
                block = acc[lo : lo + rows] - mean[v : v + 1]
                cen_ref[v, a * rows : (a + 1) * rows] = block
                total = total + jnp.sum(block * block, axis=0, keepdims=True)
            sums.append(total)
        stat_ref[...] = jnp.concatenate(sums + [mean, jnp.zeros((4, mean.shape[1]), F32)], axis=0)
        zero = cen_ref[0].astype(BF)
        one = cen_ref[1].astype(BF)
        mine_ref[...] = jnp.where(core == 0, zero, one)
        theirs_ref[...] = jnp.where(core == 0, one, zero)


def weight_kernel(core_ref, own_ref, oth_ref, g_ref, out_ref):
    core = core_ref[0]
    out_ref[0, core] = dot(flat_rows(own_ref), g_ref[...], 0, 0).astype(BF)
    out_ref[0, 1 - core] = dot(flat_rows(oth_ref), g_ref[...], 0, 0).astype(BF)


def input_kernel(core_ref, g_ref, w_ref, out_ref):
    nx, _, nv, rows, width = out_ref.shape
    out_ref[:, 0] = dot(g_ref[...], w_ref[0, core_ref[0]], 1, 1).astype(BF).reshape(nx, nv, rows, width)


def on_device(hidden_first, hidden_second, weight):
    core = lax.axis_index("c")
    core_own = core.astype(jnp.int32).reshape(1)
    first = core == 0
    rows, kpart = hidden_first.shape
    kz, cols = weight.shape
    total_rows = rows * NX * NZ * 1.0
    full_width = cols * NY * NC * 1.0
    blk = rows * NX
    flat = 2 * blk
    sub = cols // NX
    hshape = (NX, NY, 2, rows, kpart)
    hblock = (NX, 1, 2, rows, kpart)
    wblock = (1, NC, kpart, sub)

    w_parts = exchange(jnp.stack([weight[:, k * sub : (k + 1) * sub] for k in range(NX)]), "x")
    moved, w_parts = lax.optimization_barrier((jnp.stack([hidden_first, hidden_second]), w_parts))
    w_all = lax.all_gather(w_parts, "z", axis=1, tiled=True).reshape(NY, NC, kpart, sub)
    h_own = spread_out(moved, CHIPS, NX * NY).reshape(hshape)
    h_oth = swap_core(h_own)

    row_sum = jnp.sum(h_own.astype(F32), axis=(0, 3)).reshape(2 * NY, kpart)
    mean_own = (jnp.sum(spread_out(row_sum, "z", NZ), axis=0) / total_rows).reshape(NY, 2, kpart)
    pad = jnp.zeros((NY, 10, kpart), BF)
    m_own = jnp.concatenate(split3(mean_own) + (pad,), axis=1)
    m_rows = jnp.stack([m_own, swap_core(m_own)], axis=1)

    centered, mine, theirs, stats = pl.pallas_call(
        views_kernel,
        grid=(NY,),
        in_specs=[
            pl.BlockSpec(memory_space=SMEM),
            at_dim(hblock, 1),
            at_dim(hblock, 1),
            at_dim((1, 2, 16, kpart), 0),
            at_dim(wblock, 0),
        ],
        out_specs=[fixed((2, blk, sub)), fixed((blk, sub)), fixed((blk, sub)), fixed((8, sub))],
        out_shape=[
            jax.ShapeDtypeStruct((2, blk, sub), F32),
            jax.ShapeDtypeStruct((blk, sub), BF),
            jax.ShapeDtypeStruct((blk, sub), BF),
            jax.ShapeDtypeStruct((8, sub), F32),
        ],
        scratch_shapes=[pltpu.VMEM((flat, sub), F32), pltpu.VMEM((16, sub), F32)],
        name="views",
    )(core_own, h_own, h_oth, m_rows, w_all)
    mean_cols = stats[2:4]

    own_rows = jnp.concatenate([mine, swap_core(theirs)], axis=1)
    gathered = lax.all_gather(own_rows, "z", axis=0, tiled=True)

    variance = jnp.sum(spread_out(stats, "z", NZ), axis=0)[:2] / (total_rows - 1.0)
    deviation = jnp.sqrt(variance + 0.0001)
    difference = centered[0] - centered[1] + (mean_cols[0] - mean_cols[1])[None, :]
    share = (
        25.0 * jnp.sum(difference * difference) / (total_rows * full_width)
        + 25.0 * jnp.sum(jax.nn.relu(1.0 - deviation)) / (full_width * NZ)
        - jnp.sum(variance * variance) / (full_width * NZ)
    )
    share = jnp.sum(spread_out(jnp.broadcast_to(share, (8, 128)), CHIPS, NX * NY), axis=0)
    gathered, share, difference = lax.optimization_barrier((gathered, share, difference))

    gram_part = dot(own_rows, gathered, 1, 1).astype(BF)
    pieces = exchange(gram_part.reshape(NX * NY, blk // (NX * NY), -1), CHIPS)
    gram_rows = jnp.sum(pieces.astype(F32), axis=0).astype(BF)
    gram_half = spread_out(gram_rows, CHIPS, NX * NY).reshape(blk, -1)
    spread_view = dot(gram_half, gathered, 1, 0)
    spread_own = spread_view[:, :sub]
    spread_back = swap_core(spread_view[:, sub:])
    spread = jnp.stack(
        [jnp.where(first, spread_own, spread_back), jnp.where(first, spread_back, spread_own)]
    )

    inv_grad = 50.0 / 256.0 * jnp.stack([difference, -difference])
    binding = (deviation < 1.0).astype(F32)
    hinge_grad = (
        -(25.0 * total_rows / (256.0 * (total_rows - 1.0)))
        * (binding / deviation)[:, None, :]
        * centered
    )
    cov_grad = (
        4.0
        * total_rows
        / 256.0
        * (spread / (total_rows - 1.0) ** 2 - variance[:, None, :] * centered / (total_rows - 1.0))
    )
    grad_views = (inv_grad + hinge_grad + cov_grad).astype(BF)
    grads = grad_views.reshape(2, NX, rows, sub).transpose(1, 0, 2, 3).reshape(flat, sub)

    weight_part = pl.pallas_call(
        weight_kernel,
        grid=(NY,),
        in_specs=[
            pl.BlockSpec(memory_space=SMEM),
            at_dim(hblock, 1),
            at_dim(hblock, 1),
            fixed((flat, sub)),
        ],
        out_specs=at_dim(wblock, 0),
        out_shape=jax.ShapeDtypeStruct((NY, NC, kpart, sub), BF),
        name="weight_terms",
    )(core_own, h_own, h_oth, grads)
    weight_sum = lax.psum_scatter(
        weight_part.reshape(NX, NZ * kz, sub), "z", scatter_dimension=1, tiled=True
    )

    def input_terms(which):
        return pl.pallas_call(
            input_kernel,
            grid=(NY,),
            in_specs=[pl.BlockSpec(memory_space=SMEM), fixed((flat, sub)), at_dim(wblock, 0)],
            out_specs=at_dim(hblock, 1),
            out_shape=jax.ShapeDtypeStruct(hshape, BF),
            name="input_terms",
        )(which, grads, w_all)

    from_other = swap_core(input_terms(1 - core_own))
    input_sum = (input_terms(core_own).astype(F32) + from_other.astype(F32)).astype(BF)
    input_parts = exchange(input_sum.reshape(NX * NY, 2, rows, kpart), CHIPS)
    input_grads = jnp.sum(input_parts.astype(F32), axis=0).astype(BF)

    wide = gram_half.astype(F32)
    share = share + jnp.sum(wide * wide) / ((total_rows - 1.0) ** 2 * full_width)
    total_loss = jnp.sum(spread_out(share, ("z", "c"), NZ * NC), axis=0)[0, 0]

    blocks = exchange(weight_sum, "x")
    grad_weight = jnp.concatenate([blocks[k] for k in range(NX)], axis=1)
    return (total_loss, grad_weight, input_grads[0], input_grads[1])


def solution(mesh):
    grid = Mesh(mesh.devices.reshape(NX, NZ, NY, NC), ("x", "z", "y", "c"))
    placed = P(("x", "z"), ("y", "c"))
    return jax.shard_map(
        on_device,
        mesh=grid,
        in_specs=(placed, placed, placed),
        out_specs=(P(), placed, placed, placed),
        check_vma=False,
    )
```

```python
import jax
import jax.numpy as jnp
from jax import lax
from jax.experimental import pallas as pl
from jax.experimental.pallas import tpu as pltpu
from jax.sharding import Mesh, PartitionSpec as P

BF = jnp.bfloat16
F32 = jnp.float32
NX, NZ, NY, NC = 4, 8, 4, 2
CHIPS = ("x", "y")
SMEM = pltpu.SMEM


def swap_core(v):
    return lax.ppermute(v, "c", [(0, 1), (1, 0)])


def exchange(v, axes):
    return lax.all_to_all(v, axes, split_axis=0, concat_axis=0, tiled=True)


def spread_out(v, axes, n):
    return exchange(jnp.broadcast_to(v[None], (n,) + v.shape), axes)


def split3(v):
    hi = v.astype(BF)
    rest = v - hi.astype(F32)
    mid = rest.astype(BF)
    low = (rest - mid.astype(F32)).astype(BF)
    return hi, mid, low


def dot(a, b, ca, cb):
    return lax.dot_general(a, b, (((ca,), (cb,)), ((), ())), preferred_element_type=F32)


def fixed(shape):
    return pl.BlockSpec(shape, lambda j: (0,) * len(shape))


def at_dim(shape, dim):
    return pl.BlockSpec(shape, lambda j: tuple(j if d == dim else 0 for d in range(len(shape))))


def flat_rows(ref):
    nx, _, nv, rows, width = ref.shape
    return ref[:, 0].reshape(nx * nv * rows, width)


def views_kernel(core_ref, own_ref, oth_ref, w_ref, cen_ref, mine_ref, theirs_ref, stat_ref, acc):
    step = pl.program_id(0)
    core = core_ref[0]
    nx, _, nv, rows, _ = own_ref.shape
    term = dot(flat_rows(own_ref), w_ref[0, core], 1, 0) + dot(flat_rows(oth_ref), w_ref[0, 1 - core], 1, 0)

    @pl.when(step == 0)
    def _():
        acc[...] = term

    @pl.when(step > 0)
    def _():
        acc[...] += term

    @pl.when(step == pl.num_programs(0) - 1)
    def _():
        squares, means = [], []
        for v in range(nv):
            blocks = [acc[(a * nv + v) * rows : (a * nv + v + 1) * rows] for a in range(nx)]
            mean = sum(jnp.sum(block, axis=0, keepdims=True) for block in blocks) / (nx * rows * 1.0)
            means.append(mean)
            total = jnp.zeros_like(mean)
            for a in range(nx):
                block = blocks[a] - mean
                cen_ref[v, a * rows : (a + 1) * rows] = block
                total = total + jnp.sum(block * block, axis=0, keepdims=True)
            squares.append(total)
        stat_ref[...] = jnp.concatenate(squares + means + [jnp.zeros((4, mean.shape[1]), F32)], axis=0)
        zero = cen_ref[0].astype(BF)
        one = cen_ref[1].astype(BF)
        mine_ref[...] = jnp.where(core == 0, zero, one)
        theirs_ref[...] = jnp.where(core == 0, one, zero)


def weight_kernel(core_ref, own_ref, oth_ref, g_ref, out_ref):
    core = core_ref[0]
    out_ref[0, core] = dot(flat_rows(own_ref), g_ref[...], 0, 0).astype(BF)
    out_ref[0, 1 - core] = dot(flat_rows(oth_ref), g_ref[...], 0, 0).astype(BF)


def sent_kernel(core_ref, g_ref, w_ref, out_ref):
    nx, _, nv, rows, width = out_ref.shape
    term = dot(g_ref[...], w_ref[0, 1 - core_ref[0]], 1, 1)
    out_ref[:, 0] = term.astype(BF).reshape(nx, nv, rows, width)


def kept_kernel(core_ref, g_ref, w_ref, recv_ref, out_ref):
    nx, _, nv, rows, width = out_ref.shape
    term = dot(g_ref[...], w_ref[0, core_ref[0]], 1, 1) + flat_rows(recv_ref).astype(F32)
    out_ref[:, 0] = term.astype(BF).reshape(nx, nv, rows, width)


def on_device(hidden_first, hidden_second, weight):
    core = lax.axis_index("c")
    core_own = core.astype(jnp.int32).reshape(1)
    first = core == 0
    rows, kpart = hidden_first.shape
    kz, cols = weight.shape
    total_rows = rows * NX * NZ * 1.0
    full_width = cols * NY * NC * 1.0
    blk = rows * NX
    flat = 2 * blk
    sub = cols // NX
    hshape = (NX, NY, 2, rows, kpart)
    hblock = (NX, 1, 2, rows, kpart)
    wblock = (1, NC, kpart, sub)

    w_parts = exchange(jnp.stack([weight[:, k * sub : (k + 1) * sub] for k in range(NX)]), "x")
    moved, w_parts = lax.optimization_barrier((jnp.stack([hidden_first, hidden_second]), w_parts))
    w_all = lax.all_gather(w_parts, "z", axis=1, tiled=True).reshape(NY, NC, kpart, sub)
    h_own = spread_out(moved, CHIPS, NX * NY).reshape(hshape)
    h_oth = swap_core(h_own)

    cen, mine, theirs, stats = pl.pallas_call(
        views_kernel,
        grid=(NY,),
        in_specs=[
            pl.BlockSpec(memory_space=SMEM),
            at_dim(hblock, 1),
            at_dim(hblock, 1),
            at_dim(wblock, 0),
        ],
        out_specs=[fixed((2, blk, sub)), fixed((blk, sub)), fixed((blk, sub)), fixed((8, sub))],
        out_shape=[
            jax.ShapeDtypeStruct((2, blk, sub), F32),
            jax.ShapeDtypeStruct((blk, sub), BF),
            jax.ShapeDtypeStruct((blk, sub), BF),
            jax.ShapeDtypeStruct((8, sub), F32),
        ],
        scratch_shapes=[pltpu.VMEM((flat, sub), F32)],
        name="views",
    )(core_own, h_own, h_oth, w_all)

    local_rows = jnp.concatenate([mine, swap_core(theirs)], axis=1)
    local = lax.all_gather(local_rows, "z", axis=0, tiled=False)

    block_stats = spread_out(stats, "z", NZ)
    block_mean = block_stats[:, 2:4]
    shift = block_mean - jnp.mean(block_mean, axis=0, keepdims=True)
    own_shift = stats[2:4] - jnp.mean(block_mean, axis=0)
    variance = (jnp.sum(block_stats[:, :2], axis=0) + blk * jnp.sum(shift * shift, axis=0)) / (total_rows - 1.0)
    deviation = jnp.sqrt(variance + 0.0001)
    centered = cen + own_shift[:, None, :]
    difference = cen[0] - cen[1] + (stats[2] - stats[3])[None, :]

    def view_shift(v):
        kept = jnp.where(first, v[:, 0], v[:, 1])
        sent = jnp.where(first, v[:, 1], v[:, 0])
        return jnp.concatenate([kept, swap_core(sent)], axis=1)

    shift_rows = view_shift(jnp.concatenate([shift, own_shift[None]], axis=0))
    share = (
        25.0 * jnp.sum(difference * difference) / (total_rows * full_width)
        + 25.0 * jnp.sum(jax.nn.relu(1.0 - deviation)) / (full_width * NZ)
        - jnp.sum(variance * variance) / (full_width * NZ)
    )
    share = jnp.sum(spread_out(jnp.broadcast_to(share, (8, 128)), CHIPS, NX * NY), axis=0)
    local, share, difference, centered, shift_rows = lax.optimization_barrier(
        (local, share, difference, centered, shift_rows)
    )
    own_rows = (local_rows.astype(F32) + shift_rows[NZ:]).astype(BF)
    gathered = (local.astype(F32) + shift_rows[:NZ, None]).astype(BF).reshape(NZ * blk, 2 * sub)

    gram_part = dot(own_rows, gathered, 1, 1).astype(BF)
    pieces = exchange(gram_part.reshape(NX * NY, blk // (NX * NY), -1), CHIPS)
    gram_rows = jnp.sum(pieces.astype(F32), axis=0).astype(BF)
    gram_half = spread_out(gram_rows, CHIPS, NX * NY).reshape(blk, -1)
    spread_view = dot(gram_half, gathered, 1, 0)
    spread_own = spread_view[:, :sub]
    spread_back = swap_core(spread_view[:, sub:])
    spread = jnp.stack(
        [jnp.where(first, spread_own, spread_back), jnp.where(first, spread_back, spread_own)]
    )

    inv_grad = 50.0 / 256.0 * jnp.stack([difference, -difference])
    binding = (deviation < 1.0).astype(F32)
    hinge_grad = (
        -(25.0 * total_rows / (256.0 * (total_rows - 1.0)))
        * (binding / deviation)[:, None, :]
        * centered
    )
    cov_grad = (
        4.0
        * total_rows
        / 256.0
        * (spread / (total_rows - 1.0) ** 2 - variance[:, None, :] * centered / (total_rows - 1.0))
    )
    grad_views = (inv_grad + hinge_grad + cov_grad).astype(BF)
    grads = grad_views.reshape(2, NX, rows, sub).transpose(1, 0, 2, 3).reshape(flat, sub)

    weight_part = pl.pallas_call(
        weight_kernel,
        grid=(NY,),
        in_specs=[
            pl.BlockSpec(memory_space=SMEM),
            at_dim(hblock, 1),
            at_dim(hblock, 1),
            fixed((flat, sub)),
        ],
        out_specs=at_dim(wblock, 0),
        out_shape=jax.ShapeDtypeStruct((NY, NC, kpart, sub), BF),
        name="weight_terms",
    )(core_own, h_own, h_oth, grads)
    weight_sum = lax.psum_scatter(
        weight_part.reshape(NX, NZ * kz, sub), "z", scatter_dimension=1, tiled=True
    )

    later, weight_part = lax.optimization_barrier((grads, weight_part))
    smem = pl.BlockSpec(memory_space=SMEM)
    from_other = swap_core(
        pl.pallas_call(
            sent_kernel,
            grid=(NY,),
            in_specs=[smem, fixed((flat, sub)), at_dim(wblock, 0)],
            out_specs=at_dim(hblock, 1),
            out_shape=jax.ShapeDtypeStruct(hshape, BF),
            name="input_sent",
        )(core_own, later, w_all)
    )
    input_sum = pl.pallas_call(
        kept_kernel,
        grid=(NY,),
        in_specs=[smem, fixed((flat, sub)), at_dim(wblock, 0), at_dim(hblock, 1)],
        out_specs=at_dim(hblock, 1),
        out_shape=jax.ShapeDtypeStruct(hshape, BF),
        name="input_kept",
    )(core_own, later, w_all, from_other)
    input_parts = exchange(input_sum.reshape(NX * NY, 2, rows, kpart), CHIPS)
    input_grads = jnp.sum(input_parts.astype(F32), axis=0).astype(BF)

    wide = gram_half.astype(F32)
    share = share + jnp.sum(wide * wide) / ((total_rows - 1.0) ** 2 * full_width)
    total_loss = jnp.sum(spread_out(share, ("z", "c"), NZ * NC), axis=0)[0, 0]

    blocks = exchange(weight_sum, "x")
    grad_weight = jnp.concatenate([blocks[k] for k in range(NX)], axis=1)
    return (total_loss, grad_weight, input_grads[0], input_grads[1])


def solution(mesh):
    grid = Mesh(mesh.devices.reshape(NX, NZ, NY, NC), ("x", "z", "y", "c"))
    placed = P(("x", "z"), ("y", "c"))
    return jax.shard_map(
        on_device,
        mesh=grid,
        in_specs=(placed, placed, placed),
        out_specs=(P(), placed, placed, placed),
        check_vma=False,
    )
```

```python
import jax
import jax.numpy as jnp
from jax import lax
from jax.experimental import pallas as pl
from jax.experimental.pallas import tpu as pltpu
from jax.sharding import Mesh, PartitionSpec as P

BF = jnp.bfloat16
F32 = jnp.float32
NX, NZ, NY, NC = 4, 8, 4, 2
CHIPS = ("x", "y")
SMEM = pltpu.SMEM


def swap_core(v):
    return lax.ppermute(v, "c", [(0, 1), (1, 0)])


def butterfly(v, axis, n):
    step = 1
    while step < n:
        v = v + lax.ppermute(v, axis, [(i, i ^ step) for i in range(n)])
        step *= 2
    return v


def exchange(v, axes):
    return lax.all_to_all(v, axes, split_axis=0, concat_axis=0, tiled=True)


def spread_out(v, axes, n):
    return exchange(jnp.broadcast_to(v[None], (n,) + v.shape), axes)


def split3(v):
    hi = v.astype(BF)
    rest = v - hi.astype(F32)
    mid = rest.astype(BF)
    low = (rest - mid.astype(F32)).astype(BF)
    return hi, mid, low


def dot(a, b, ca, cb):
    return lax.dot_general(a, b, (((ca,), (cb,)), ((), ())), preferred_element_type=F32)


def fixed(shape):
    return pl.BlockSpec(shape, lambda j: (0,) * len(shape))


def at_dim(shape, dim):
    return pl.BlockSpec(shape, lambda j: tuple(j if d == dim else 0 for d in range(len(shape))))


def flat_rows(ref):
    nx, _, nv, rows, width = ref.shape
    return ref[:, 0].reshape(nx * nv * rows, width)


def views_kernel(core_ref, own_ref, oth_ref, w_ref, cen_ref, mine_ref, theirs_ref, stat_ref, acc):
    step = pl.program_id(0)
    core = core_ref[0]
    nx, _, nv, rows, _ = own_ref.shape
    term = dot(flat_rows(own_ref), w_ref[0, core], 1, 0) + dot(flat_rows(oth_ref), w_ref[0, 1 - core], 1, 0)

    @pl.when(step == 0)
    def _():
        acc[...] = term

    @pl.when(step > 0)
    def _():
        acc[...] += term

    @pl.when(step == pl.num_programs(0) - 1)
    def _():
        squares, means = [], []
        for v in range(nv):
            blocks = [acc[(a * nv + v) * rows : (a * nv + v + 1) * rows] for a in range(nx)]
            mean = sum(jnp.sum(block, axis=0, keepdims=True) for block in blocks) / (nx * rows * 1.0)
            means.append(mean)
            total = jnp.zeros_like(mean)
            for a in range(nx):
                block = blocks[a] - mean
                cen_ref[v, a * rows : (a + 1) * rows] = block
                total = total + jnp.sum(block * block, axis=0, keepdims=True)
            squares.append(total)
        stat_ref[...] = jnp.concatenate(squares + means + [jnp.zeros((4, mean.shape[1]), F32)], axis=0)
        zero = cen_ref[0].astype(BF)
        one = cen_ref[1].astype(BF)
        mine_ref[...] = jnp.where(core == 0, zero, one)
        theirs_ref[...] = jnp.where(core == 0, one, zero)


def weight_kernel(core_ref, own_ref, oth_ref, g_ref, out_ref):
    core = core_ref[0]
    out_ref[0, core] = dot(flat_rows(own_ref), g_ref[...], 0, 0).astype(BF)
    out_ref[0, 1 - core] = dot(flat_rows(oth_ref), g_ref[...], 0, 0).astype(BF)


def on_device(hidden_first, hidden_second, weight):
    core = lax.axis_index("c")
    core_own = core.astype(jnp.int32).reshape(1)
    first = core == 0
    rows, kpart = hidden_first.shape
    kz, cols = weight.shape
    total_rows = rows * NX * NZ * 1.0
    full_width = cols * NY * NC * 1.0
    blk = rows * NX
    flat = 2 * blk
    sub = cols // NX
    hshape = (NX, NY, 2, rows, kpart)
    hblock = (NX, 1, 2, rows, kpart)
    wblock = (1, NC, kpart, sub)

    w_parts = exchange(jnp.stack([weight[:, k * sub : (k + 1) * sub] for k in range(NX)]), "x")
    moved, w_parts = lax.optimization_barrier((jnp.stack([hidden_first, hidden_second]), w_parts))
    w_all = lax.all_gather(w_parts, "z", axis=1, tiled=True).reshape(NY, NC, kpart, sub)
    h_own = spread_out(moved, CHIPS, NX * NY).reshape(hshape)
    h_oth = swap_core(h_own)

    cen, mine, theirs, stats = pl.pallas_call(
        views_kernel,
        grid=(NY,),
        in_specs=[
            pl.BlockSpec(memory_space=SMEM),
            at_dim(hblock, 1),
            at_dim(hblock, 1),
            at_dim(wblock, 0),
        ],
        out_specs=[fixed((2, blk, sub)), fixed((blk, sub)), fixed((blk, sub)), fixed((8, sub))],
        out_shape=[
            jax.ShapeDtypeStruct((2, blk, sub), F32),
            jax.ShapeDtypeStruct((blk, sub), BF),
            jax.ShapeDtypeStruct((blk, sub), BF),
            jax.ShapeDtypeStruct((8, sub), F32),
        ],
        scratch_shapes=[pltpu.VMEM((flat, sub), F32)],
        name="views",
    )(core_own, h_own, h_oth, w_all)

    local_rows = jnp.concatenate([mine, swap_core(theirs)], axis=1)
    local = lax.all_gather(local_rows, "z", axis=0, tiled=False)

    block_stats = spread_out(stats, "z", NZ)
    block_mean = block_stats[:, 2:4]
    shift = block_mean - jnp.mean(block_mean, axis=0, keepdims=True)
    own_shift = stats[2:4] - jnp.mean(block_mean, axis=0)
    variance = (jnp.sum(block_stats[:, :2], axis=0) + blk * jnp.sum(shift * shift, axis=0)) / (total_rows - 1.0)
    deviation = jnp.sqrt(variance + 0.0001)
    centered = cen + own_shift[:, None, :]
    difference = cen[0] - cen[1] + (stats[2] - stats[3])[None, :]

    def view_shift(v):
        kept = jnp.where(first, v[:, 0], v[:, 1])
        sent = jnp.where(first, v[:, 1], v[:, 0])
        return jnp.concatenate([kept, swap_core(sent)], axis=1)

    shift_rows = view_shift(jnp.concatenate([shift, own_shift[None]], axis=0))
    share = (
        25.0 * jnp.sum(difference * difference) / (total_rows * full_width)
        + 25.0 * jnp.sum(jax.nn.relu(1.0 - deviation)) / (full_width * NZ)
        - jnp.sum(variance * variance) / (full_width * NZ)
    )
    share = jnp.sum(spread_out(jnp.broadcast_to(share, (8, 128)), CHIPS, NX * NY), axis=0)
    w_kept = jnp.where(first, w_all[:, 0], w_all[:, 1])
    w_sent = jnp.where(first, w_all[:, 1], w_all[:, 0])
    w_half = jnp.concatenate([w_kept, swap_core(w_sent)], axis=2)
    local, share, difference, centered, shift_rows, w_half = lax.optimization_barrier(
        (local, share, difference, centered, shift_rows, w_half)
    )
    own_rows = (local_rows.astype(F32) + shift_rows[NZ:]).astype(BF)
    gathered = (local.astype(F32) + shift_rows[:NZ, None]).astype(BF).reshape(NZ * blk, 2 * sub)

    gram_part = dot(own_rows, gathered, 1, 1).astype(BF)
    pieces = exchange(gram_part.reshape(NX * NY, blk // (NX * NY), -1), CHIPS)
    gram_rows = jnp.sum(pieces.astype(F32), axis=0).astype(BF)
    gram_half = spread_out(gram_rows, CHIPS, NX * NY).reshape(blk, -1)
    spread_view = dot(gram_half, gathered, 1, 0)
    spread_own = spread_view[:, :sub]
    spread_back = swap_core(spread_view[:, sub:])
    spread = jnp.stack(
        [jnp.where(first, spread_own, spread_back), jnp.where(first, spread_back, spread_own)]
    )

    inv_grad = 50.0 / 256.0 * jnp.stack([difference, -difference])
    binding = (deviation < 1.0).astype(F32)
    hinge_grad = (
        -(25.0 * total_rows / (256.0 * (total_rows - 1.0)))
        * (binding / deviation)[:, None, :]
        * centered
    )
    cov_grad = (
        4.0
        * total_rows
        / 256.0
        * (spread / (total_rows - 1.0) ** 2 - variance[:, None, :] * centered / (total_rows - 1.0))
    )
    grad_views = (inv_grad + hinge_grad + cov_grad).astype(BF)
    grads = grad_views.reshape(2, NX, rows, sub).transpose(1, 0, 2, 3).reshape(flat, sub)

    weight_part = pl.pallas_call(
        weight_kernel,
        grid=(NY,),
        in_specs=[
            pl.BlockSpec(memory_space=SMEM),
            at_dim(hblock, 1),
            at_dim(hblock, 1),
            fixed((flat, sub)),
        ],
        out_specs=at_dim(wblock, 0),
        out_shape=jax.ShapeDtypeStruct((NY, NC, kpart, sub), BF),
        name="weight_terms",
    )(core_own, h_own, h_oth, grads)
    both = jnp.concatenate([grads, swap_core(grads)], axis=1)
    weight_sum = lax.psum_scatter(
        weight_part.reshape(NX, NZ * kz, sub), "z", scatter_dimension=1, tiled=True
    )
    input_part = lax.dot_general(
        jnp.broadcast_to(both[None], (NY,) + both.shape),
        w_half,
        (((2,), (2,)), ((0,), (0,))),
        preferred_element_type=F32,
    ).astype(BF)
    input_parts = exchange(input_part.reshape(NX * NY, 2, rows, kpart), ("y", "x"))
    input_grads = jnp.sum(input_parts.astype(F32), axis=0).astype(BF)

    wide = gram_half.astype(F32)
    share = share + jnp.sum(wide * wide) / ((total_rows - 1.0) ** 2 * full_width)
    total_loss = butterfly(butterfly(share[:1], "c", NC), "z", NZ)[0, 0]

    blocks = exchange(weight_sum, "x")
    grad_weight = jnp.concatenate([blocks[k] for k in range(NX)], axis=1)
    return (total_loss, grad_weight, input_grads[0], input_grads[1])


def solution(mesh):
    grid = Mesh(mesh.devices.reshape(NX, NZ, NY, NC), ("x", "z", "y", "c"))
    placed = P(("x", "z"), ("y", "c"))
    return jax.shard_map(
        on_device,
        mesh=grid,
        in_specs=(placed, placed, placed),
        out_specs=(P(), placed, placed, placed),
        check_vma=False,
    )
```

```python
import jax
import jax.numpy as jnp
from jax import lax
from jax.experimental import pallas as pl
from jax.experimental.pallas import tpu as pltpu
from jax.sharding import Mesh, PartitionSpec as P

BF = jnp.bfloat16
F32 = jnp.float32
NX, NZ, NY, NC = 4, 8, 4, 2
HALF = NZ // 2
CHIPS = ("x", "y")
SMEM = pltpu.SMEM
STAT = 16


def swap_core(v):
    return lax.ppermute(v, "c", [(0, 1), (1, 0)])


def hop(v, k):
    return lax.ppermute(v, "z", [(i, (i + k) % NZ) for i in range(NZ)])


def butterfly(v, axis, n):
    step = 1
    while step < n:
        v = v + lax.ppermute(v, axis, [(i, i ^ step) for i in range(n)])
        step *= 2
    return v


def exchange(v, axes):
    return lax.all_to_all(v, axes, split_axis=0, concat_axis=0, tiled=True)


def spread_out(v, axes, n):
    return exchange(jnp.broadcast_to(v[None], (n,) + v.shape), axes)


def ring_blocks(v):
    right, left = [v], [v]
    for _ in range(1, HALF):
        right.append(hop(right[-1], 1))
        left.append(hop(left[-1], -1))
    half = v.shape[0] // 2
    far = (hop(right[-1][:half], 1), hop(left[-1][half:], -1))
    return left[1:], right[:0:-1], far


def ring_pieces(first, second):
    got = [[None, None] for _ in range(NZ)]
    got[0] = [first, second]
    for k in range(1, HALF + 1):
        for p in (0, 1):
            if k < HALF or p == 0:
                got[-k % NZ][p] = hop(got[(1 - k) % NZ][p], 1)
            if k < HALF or p == 1:
                got[k][p] = hop(got[k - 1][p], -1)
    return got


def ring_sum(terms):
    half = terms.shape[1] // 2
    right = hop(terms[HALF][:half], 1)
    left = hop(terms[HALF][half:], -1)
    blank = jnp.zeros(right.shape, F32)
    for d in range(HALF - 1, 0, -1):
        right, left = lax.optimization_barrier((right, left))
        right, left = right.astype(F32), left.astype(F32)
        if d == HALF - 1:
            right = jnp.concatenate([right, blank], axis=0)
            left = jnp.concatenate([blank, left], axis=0)
        right = hop((terms[d].astype(F32) + right).astype(BF), 1)
        left = hop((terms[NZ - d].astype(F32) + left).astype(BF), -1)
    return terms[0].astype(F32) + right.astype(F32) + left.astype(F32)


def split3(v):
    hi = v.astype(BF).astype(F32)
    mid = (v - hi).astype(BF).astype(F32)
    return [hi, mid, v - hi - mid]


def dot(a, b, ca, cb):
    return lax.dot_general(a, b, (((ca,), (cb,)), ((), ())), preferred_element_type=F32)


def fixed(shape):
    return pl.BlockSpec(shape, lambda j: (0,) * len(shape))


def at_dim(shape, dim):
    return pl.BlockSpec(shape, lambda j: tuple(j if d == dim else 0 for d in range(len(shape))))


def flat_rows(ref):
    nx, _, nv, rows, width = ref.shape
    return ref[:, 0].reshape(nx * nv * rows, width)


def views_kernel(place_ref, own_ref, oth_ref, *refs):
    w_refs, (far_a, far_b, wout_ref, cen_ref, mine_ref, theirs_ref, stat_ref, acc) = refs[:7], refs[7:]
    step = pl.program_id(0)
    core = place_ref[0]
    zi = place_ref[1]
    nx, _, nv, rows, kpart = own_ref.shape
    sub = acc.shape[1]
    for k, ref in zip((0, 1, 2, 3, 5, 6, 7), w_refs):
        wout_ref[0, lax.rem(zi + k, NZ)] = ref[0]
    wout_ref[0, lax.rem(zi + HALF, NZ)] = jnp.where(step < NY // 2, far_a[0], far_b[0])
    w_own = wout_ref[0, pl.ds(core * HALF, HALF)].reshape(kpart, sub)
    w_oth = wout_ref[0, pl.ds((1 - core) * HALF, HALF)].reshape(kpart, sub)
    term = dot(flat_rows(own_ref), w_own, 1, 0) + dot(flat_rows(oth_ref), w_oth, 1, 0)

    @pl.when(step == 0)
    def _():
        acc[...] = term

    @pl.when(step > 0)
    def _():
        acc[...] += term

    @pl.when(step == pl.num_programs(0) - 1)
    def _():
        means, tails = [], []
        for v in range(nv):
            blocks = [acc[(a * nv + v) * rows : (a * nv + v + 1) * rows] for a in range(nx)]
            mean = sum(jnp.sum(block, axis=0, keepdims=True) for block in blocks) / (nx * rows * 1.0)
            means.append(mean)
            total = jnp.zeros_like(mean)
            for a in range(nx):
                block = blocks[a] - mean
                cen_ref[v, a * rows : (a + 1) * rows] = block
                total = total + jnp.sum(block * block, axis=0, keepdims=True)
            pad = jnp.zeros((STAT - 6, sub), F32)
            tails.append(jnp.concatenate(split3(mean) + split3(total) + [pad], axis=0).astype(BF))
        stat_ref[...] = jnp.concatenate(means + [jnp.zeros((6, sub), F32)], axis=0)
        data = [cen_ref[v].astype(BF) for v in range(nv)]
        for ref, same in ((mine_ref, core == 0), (theirs_ref, core == 1)):
            ref[:STAT] = jnp.where(same, tails[0], tails[1])
            ref[STAT:] = jnp.where(same, data[0], data[1])


def gram_kernel(*refs):
    pieces, (all_ref, gram_ref, stat_ref) = refs[: 2 * NZ], refs[2 * NZ :]
    top = pieces[0].shape[0] - STAT
    blk = top + pieces[1].shape[0]
    stats = [pieces[2 * k][:STAT].astype(F32) for k in range(NZ)]
    means = [s[0:1] + s[1:2] + s[2:3] for s in stats]
    center = sum(means) / (NZ * 1.0)
    total = sum(s[3:4] + s[4:5] + s[5:6] for s in stats)
    for k in range(NZ):
        move = means[k] - center
        total = total + blk * (move * move)
        all_ref[k * blk : k * blk + top] = (pieces[2 * k][STAT:].astype(F32) + move).astype(BF)
        all_ref[k * blk + top : (k + 1) * blk] = (pieces[2 * k + 1][...].astype(F32) + move).astype(BF)
        gram_ref[:, k * blk : (k + 1) * blk] = dot(
            all_ref[:blk], all_ref[k * blk : (k + 1) * blk], 1, 1
        ).astype(BF)
    pad = jnp.zeros((6, total.shape[1]), F32)
    stat_ref[...] = jnp.concatenate([total / (NZ * blk - 1.0), means[0] - center, pad], axis=0)


def weight_kernel(place_ref, own_ref, oth_ref, g_ref, out_ref):
    core = place_ref[0]
    zi = place_ref[1]
    kz = out_ref.shape[2]
    for ref, lead in ((own_ref, core), (oth_ref, 1 - core)):
        term = dot(flat_rows(ref), g_ref[...], 0, 0).astype(BF)
        for q in range(HALF):
            out_ref[lax.rem(lead * HALF + q - zi + NZ, NZ), 0] = term[q * kz : (q + 1) * kz]


def on_device(hidden_first, hidden_second, weight):
    core = lax.axis_index("c")
    place = jnp.stack([core, lax.axis_index("z")]).astype(jnp.int32)
    first = core == 0
    rows, kpart = hidden_first.shape
    kz, cols = weight.shape
    total_rows = rows * NX * NZ * 1.0
    full_width = cols * NY * NC * 1.0
    blk = rows * NX
    flat = 2 * blk
    sub = cols // NX
    hshape = (NX, NY, 2, rows, kpart)
    hblock = (NX, 1, 2, rows, kpart)
    smem = pl.BlockSpec(memory_space=SMEM)
    shape = jax.ShapeDtypeStruct

    w_parts = exchange(jnp.stack([weight[:, k * sub : (k + 1) * sub] for k in range(NX)]), "x")
    moved, w_parts = lax.optimization_barrier((jnp.stack([hidden_first, hidden_second]), w_parts))
    h_own = spread_out(moved, CHIPS, NX * NY).reshape(hshape)
    after, before, (far_a, far_b) = ring_blocks(w_parts)
    h_own, _, _ = lax.optimization_barrier((h_own, after[-1], before[0]))
    h_oth = swap_core(h_own)

    block_spec = at_dim((1, kz, sub), 0)
    w_all, cen, mine, theirs, stats = pl.pallas_call(
        views_kernel,
        grid=(NY,),
        in_specs=[smem, at_dim(hblock, 1), at_dim(hblock, 1)]
        + [block_spec] * 7
        + [
            pl.BlockSpec((1, kz, sub), lambda j: (jnp.minimum(j, NX // 2 - 1), 0, 0)),
            pl.BlockSpec((1, kz, sub), lambda j: (jnp.maximum(j - NX // 2, 0), 0, 0)),
        ],
        out_specs=[
            at_dim((1, NZ, kz, sub), 0),
            fixed((2, blk, sub)),
            fixed((blk + STAT, sub)),
            fixed((blk + STAT, sub)),
            fixed((8, sub)),
        ],
        out_shape=[
            shape((NY, NZ, kz, sub), BF),
            shape((2, blk, sub), F32),
            shape((blk + STAT, sub), BF),
            shape((blk + STAT, sub), BF),
            shape((8, sub), F32),
        ],
        scratch_shapes=[pltpu.VMEM((flat, sub), F32)],
        name="views",
    )(place, h_own, h_oth, w_parts, *after, *before, far_a, far_b)

    local = jnp.concatenate([mine, swap_core(theirs)], axis=1)
    got = ring_pieces(local[: STAT + blk // 2], local[STAT + blk // 2 :])

    w_pair = w_all.reshape(NY, NC, kpart, sub)
    w_kept = jnp.where(first, w_pair[:, 0], w_pair[:, 1])
    w_sent = jnp.where(first, w_pair[:, 1], w_pair[:, 0])
    w_half = jnp.concatenate([w_kept, swap_core(w_sent)], axis=2)
    difference = cen[0] - cen[1] + (stats[0] - stats[1])[None, :]
    share = 25.0 * jnp.sum(difference * difference) / (total_rows * full_width)

    flat_got = [piece for pair in got for piece in pair]
    whole = lambda s: pl.BlockSpec(s, lambda: (0,) * len(s))
    gathered, gram_part, view_stats = pl.pallas_call(
        gram_kernel,
        in_specs=[whole(piece.shape) for piece in flat_got],
        out_specs=[whole((NZ * blk, 2 * sub)), whole((blk, NZ * blk)), whole((8, 2 * sub))],
        out_shape=[
            shape((NZ * blk, 2 * sub), BF),
            shape((blk, NZ * blk), BF),
            shape((8, 2 * sub), F32),
        ],
        name="gram",
    )(*flat_got)

    var_view = view_stats[0]
    share = (
        share
        + 25.0 * jnp.sum(jax.nn.relu(1.0 - jnp.sqrt(var_view + 0.0001))) / (full_width * NZ)
        - jnp.sum(var_view * var_view) / (full_width * NZ)
    )
    share = butterfly(butterfly(share.reshape(1, 1), "x", NX), "y", NY)
    stats_own = view_stats[:, :sub]
    stats_back = swap_core(view_stats[:, sub:])
    both_stats = jnp.stack(
        [jnp.where(first, stats_own, stats_back), jnp.where(first, stats_back, stats_own)]
    )
    variance = both_stats[:, 0]
    centered = cen + both_stats[:, 1][:, None, :]
    deviation = jnp.sqrt(variance + 0.0001)

    pieces = exchange(gram_part.reshape(NX * NY, blk // (NX * NY), -1), CHIPS)
    gram_rows = jnp.sum(pieces.astype(F32), axis=0).astype(BF)
    gram_rows, share, variance, w_half = lax.optimization_barrier((gram_rows, share, variance, w_half))
    gram_half = spread_out(gram_rows, CHIPS, NX * NY).reshape(blk, -1)
    spread_view = dot(gram_half, gathered, 1, 0)
    spread_own = spread_view[:, :sub]
    spread_back = swap_core(spread_view[:, sub:])
    spread = jnp.stack(
        [jnp.where(first, spread_own, spread_back), jnp.where(first, spread_back, spread_own)]
    )

    inv_grad = 50.0 / 256.0 * jnp.stack([difference, -difference])
    binding = (deviation < 1.0).astype(F32)
    hinge_grad = (
        -(25.0 * total_rows / (256.0 * (total_rows - 1.0)))
        * (binding / deviation)[:, None, :]
        * centered
    )
    cov_grad = (
        4.0
        * total_rows
        / 256.0
        * (spread / (total_rows - 1.0) ** 2 - variance[:, None, :] * centered / (total_rows - 1.0))
    )
    grad_views = (inv_grad + hinge_grad + cov_grad).astype(BF)
    grads = grad_views.reshape(2, NX, rows, sub).transpose(1, 0, 2, 3).reshape(flat, sub)

    weight_part = pl.pallas_call(
        weight_kernel,
        grid=(NY,),
        in_specs=[smem, at_dim(hblock, 1), at_dim(hblock, 1), fixed((flat, sub))],
        out_specs=at_dim((NZ, 1, kz, sub), 1),
        out_shape=shape((NZ, NY, kz, sub), BF),
        name="weight_terms",
    )(place, h_own, h_oth, grads)

    both = jnp.concatenate([grads, swap_core(grads)], axis=1)
    input_part = lax.dot_general(
        jnp.broadcast_to(both[None], (NY,) + both.shape),
        w_half,
        (((2,), (2,)), ((0,), (0,))),
        preferred_element_type=F32,
    ).astype(BF)
    input_parts = exchange(input_part.reshape(NX * NY, 2, rows, kpart), ("y", "x"))
    input_grads = jnp.sum(input_parts.astype(F32), axis=0).astype(BF)

    weight_sum, input_grads = lax.optimization_barrier((ring_sum(weight_part).astype(BF), input_grads))
    blocks = exchange(weight_sum, "x")
    grad_weight = jnp.concatenate([blocks[k] for k in range(NX)], axis=1)

    wide = gram_half.astype(F32)
    share = share + jnp.sum(wide * wide) / ((total_rows - 1.0) ** 2 * full_width)
    total_loss = butterfly(butterfly(share, "c", NC), "z", NZ)[0, 0]
    return (total_loss, grad_weight, input_grads[0], input_grads[1])


def solution(mesh):
    grid = Mesh(mesh.devices.reshape(NX, NZ, NY, NC), ("x", "z", "y", "c"))
    placed = P(("x", "z"), ("y", "c"))
    return jax.shard_map(
        on_device,
        mesh=grid,
        in_specs=(placed, placed, placed),
        out_specs=(P(), placed, placed, placed),
        check_vma=False,
    )
```

```python
import functools

import jax
import jax.numpy as jnp
from jax import lax
from jax.experimental import pallas as pl
from jax.experimental.pallas import tpu as pltpu
from jax.sharding import Mesh, PartitionSpec as P

BF = jnp.bfloat16
F32 = jnp.float32
NX, NZ, NY, NC = 4, 8, 4, 2
HALF = NZ // 2
CHIPS = ("x", "y")
SMEM = pltpu.SMEM
STAT = 16


def swap_core(v):
    return lax.ppermute(v, "c", [(0, 1), (1, 0)])


def hop(v, k):
    return lax.ppermute(v, "z", [(i, (i + k) % NZ) for i in range(NZ)])


def exchange(v, axes):
    return lax.all_to_all(v, axes, split_axis=0, concat_axis=0, tiled=True)


def copies(v, n):
    return jnp.broadcast_to(v[None], (n,) + v.shape)


def ring_blocks(v):
    right, left = [v], [v]
    for _ in range(1, HALF):
        right.append(hop(right[-1], 1))
        left.append(hop(left[-1], -1))
    half = v.shape[0] // 2
    far = (hop(right[-1][:half], 1), hop(left[-1][half:], -1))
    return left[1:], right[:0:-1], far


def ring_pieces(first, second):
    got = [[None, None] for _ in range(NZ)]
    got[0] = [first, second]
    for k in range(1, HALF + 1):
        for p in (0, 1):
            if k < HALF or p == 0:
                got[-k % NZ][p] = hop(got[(1 - k) % NZ][p], 1)
            if k < HALF or p == 1:
                got[k][p] = hop(got[k - 1][p], -1)
    return got


def ring_sum(terms, half):
    right = hop(terms[HALF][:half], 1)
    left = hop(terms[HALF][half:], -1)
    for d in range(HALF - 1, 0, -1):
        right, left = lax.optimization_barrier((right, left))
        right, left = right.astype(F32), left.astype(F32)
        if d == HALF - 1:
            low, high = jnp.zeros(left.shape, F32), jnp.zeros(right.shape, F32)
            right = jnp.concatenate([right, low], axis=0)
            left = jnp.concatenate([high, left], axis=0)
        right = hop((terms[d].astype(F32) + right).astype(BF), 1)
        left = hop((terms[NZ - d].astype(F32) + left).astype(BF), -1)
    return terms[0].astype(F32) + right.astype(F32) + left.astype(F32)


def split3(v):
    hi = v.astype(BF).astype(F32)
    mid = (v - hi).astype(BF).astype(F32)
    return [hi, mid, v - hi - mid]


def dot(a, b, ca, cb):
    return lax.dot_general(a, b, (((ca,), (cb,)), ((), ())), preferred_element_type=F32)


def fixed(shape):
    return pl.BlockSpec(shape, lambda j: (0,) * len(shape))


def at_dim(shape, dim):
    return pl.BlockSpec(shape, lambda j: tuple(j if d == dim else 0 for d in range(len(shape))))


def flat_rows(ref):
    nx, _, nv, rows, width = ref.shape
    return ref[:, 0].reshape(nx * nv * rows, width)


def views_kernel(place_ref, own_ref, oth_ref, *refs):
    w_refs, refs = refs[:7], refs[7:]
    far_a, far_b, kept_ref, sent_ref, cen_ref, mine_ref, theirs_ref, stat_ref, w_ref, acc = refs
    step = pl.program_id(0)
    core = place_ref[0]
    zi = place_ref[1]
    nx, _, nv, rows, kpart = own_ref.shape
    sub = acc.shape[1]
    for k, ref in zip((0, 1, 2, 3, 5, 6, 7), w_refs):
        w_ref[lax.rem(zi + k, NZ)] = ref[0]
    w_ref[lax.rem(zi + HALF, NZ)] = jnp.where(step < NY // 2, far_a[0], far_b[0])
    w_own = w_ref[pl.ds(core * HALF, HALF)].reshape(kpart, sub)
    w_oth = w_ref[pl.ds((1 - core) * HALF, HALF)].reshape(kpart, sub)
    kept_ref[0] = w_own
    sent_ref[0] = w_oth
    term = dot(flat_rows(own_ref), w_own, 1, 0) + dot(flat_rows(oth_ref), w_oth, 1, 0)

    @pl.when(step == 0)
    def _():
        acc[...] = term

    @pl.when(step > 0)
    def _():
        acc[...] += term

    @pl.when(step == pl.num_programs(0) - 1)
    def _():
        means, tails = [], []
        for v in range(nv):
            blocks = [acc[(a * nv + v) * rows : (a * nv + v + 1) * rows] for a in range(nx)]
            mean = sum(jnp.sum(block, axis=0, keepdims=True) for block in blocks) / (nx * rows * 1.0)
            means.append(mean)
            total = jnp.zeros_like(mean)
            for a in range(nx):
                block = blocks[a] - mean
                cen_ref[v, a * rows : (a + 1) * rows] = block
                total = total + jnp.sum(block * block, axis=0, keepdims=True)
            pad = jnp.zeros((STAT - 6, sub), F32)
            tails.append(jnp.concatenate(split3(mean) + split3(total) + [pad], axis=0).astype(BF))
        stat_ref[...] = jnp.concatenate(means + [jnp.zeros((6, sub), F32)], axis=0)
        data = [cen_ref[v].astype(BF) for v in range(nv)]
        for ref, same in ((mine_ref, core == 0), (theirs_ref, core == 1)):
            ref[:STAT] = jnp.where(same, tails[0], tails[1])
            ref[STAT:] = jnp.where(same, data[0], data[1])


def gram_kernel(scale_each, diff_ref, *refs):
    pieces, (all_ref, gram_ref, stat_ref) = refs[: 2 * NZ], refs[2 * NZ :]
    top = pieces[0].shape[0] - STAT
    blk = top + pieces[1].shape[0]
    stats = [pieces[2 * k][:STAT].astype(F32) for k in range(NZ)]
    means = [s[0:1] + s[1:2] + s[2:3] for s in stats]
    center = sum(means) / (NZ * 1.0)
    total = sum(s[3:4] + s[4:5] + s[5:6] for s in stats)
    for k in range(NZ):
        move = means[k] - center
        total = total + blk * (move * move)
        all_ref[k * blk : k * blk + top] = (pieces[2 * k][STAT:].astype(F32) + move).astype(BF)
        all_ref[k * blk + top : (k + 1) * blk] = (pieces[2 * k + 1][...].astype(F32) + move).astype(BF)
        gram_ref[:, k * blk : (k + 1) * blk] = dot(
            all_ref[:blk], all_ref[k * blk : (k + 1) * blk], 1, 1
        ).astype(BF)
    variance = total / (NZ * blk - 1.0)
    pad = jnp.zeros((6, total.shape[1]), F32)
    stat_ref[...] = jnp.concatenate([variance, means[0] - center, pad], axis=0)
    hinge = jnp.maximum(1.0 - jnp.sqrt(variance + 0.0001), 0.0)
    share = diff_ref[...] + scale_each * jnp.sum(25.0 * hinge - variance * variance, axis=1, keepdims=True)
    extra = gram_ref.shape[1] - NZ * blk
    row = lax.broadcasted_iota(jnp.int32, (blk, extra), 0)
    lane = lax.broadcasted_iota(jnp.int32, (blk, extra), 1)
    lead = lax.rem(row, blk // (NX * NY)) == 0
    gram_ref[:, NZ * blk :] = in_lanes(share, lane, 0, lead).astype(BF)


def in_lanes(value, lane, start, keep):
    out = jnp.zeros(lane.shape, F32)
    for n, term in enumerate(split3(value)):
        out = jnp.where(keep & (lane == start + n), term, out)
    return out


def weight_kernel(place_ref, own_ref, oth_ref, g_ref, share_ref, out_ref):
    step = pl.program_id(0)
    core = place_ref[0]
    zi = place_ref[1]
    rows = NY * (own_ref.shape[4] // HALF)
    kz = rows // NY
    for ref, lead in ((own_ref, core), (oth_ref, 1 - core)):
        term = dot(flat_rows(ref), g_ref[...], 0, 0).astype(BF)
        for q in range(HALF):
            k = lax.rem(lead * HALF + q - zi + NZ, NZ)
            out_ref[k, pl.ds(pl.multiple_of(step * kz, kz), kz)] = term[q * kz : (q + 1) * kz]

    @pl.when(step == 0)
    def _():
        row = lax.broadcasted_iota(jnp.int32, (STAT, out_ref.shape[2]), 0)
        lane = lax.broadcasted_iota(jnp.int32, (STAT, out_ref.shape[2]), 1)
        tail = in_lanes(share_ref[...], lane, 3 * zi, row == 0).astype(BF)
        for k in range(NZ):
            out_ref[k, rows:] = tail


def input_kernel(own_ref, oth_ref, kept_ref, recv_ref, out_ref):
    term = dot(own_ref[...], kept_ref[0], 1, 1) + dot(oth_ref[...], recv_ref[0], 1, 1)
    out_ref[0] = term.astype(BF)


def on_device(hidden_first, hidden_second, weight):
    core = lax.axis_index("c")
    place = jnp.stack([core, lax.axis_index("z")]).astype(jnp.int32)
    first = core == 0
    rows, kpart = hidden_first.shape
    kz, cols = weight.shape
    total_rows = rows * NX * NZ * 1.0
    full_width = cols * NY * NC * 1.0
    blk = rows * NX
    flat = 2 * blk
    sub = cols // NX
    hshape = (NX, NY, 2, rows, kpart)
    hblock = (NX, 1, 2, rows, kpart)
    smem = pl.BlockSpec(memory_space=SMEM)
    shape = jax.ShapeDtypeStruct

    w_parts = exchange(jnp.stack([weight[:, k * sub : (k + 1) * sub] for k in range(NX)]), "x")
    moved = copies(jnp.stack([hidden_first, hidden_second]), NX * NY)
    moved, w_parts = lax.optimization_barrier((moved, w_parts))
    h_own = exchange(moved, CHIPS).reshape(hshape)
    after, before, (far_a, far_b) = ring_blocks(w_parts)
    h_own, _, _ = lax.optimization_barrier((h_own, after[-1], before[0]))
    h_oth = swap_core(h_own)

    block_spec = at_dim((1, kz, sub), 0)
    w_kept, w_sent, cen, mine, theirs, stats = pl.pallas_call(
        views_kernel,
        grid=(NY,),
        in_specs=[smem, at_dim(hblock, 1), at_dim(hblock, 1)]
        + [block_spec] * 7
        + [
            pl.BlockSpec((1, kz, sub), lambda j: (jnp.minimum(j, NX // 2 - 1), 0, 0)),
            pl.BlockSpec((1, kz, sub), lambda j: (jnp.maximum(j - NX // 2, 0), 0, 0)),
        ],
        out_specs=[
            at_dim((1, kpart, sub), 0),
            at_dim((1, kpart, sub), 0),
            fixed((2, blk, sub)),
            fixed((blk + STAT, sub)),
            fixed((blk + STAT, sub)),
            fixed((8, sub)),
        ],
        out_shape=[
            shape((NY, kpart, sub), BF),
            shape((NY, kpart, sub), BF),
            shape((2, blk, sub), F32),
            shape((blk + STAT, sub), BF),
            shape((blk + STAT, sub), BF),
            shape((8, sub), F32),
        ],
        scratch_shapes=[pltpu.VMEM((NZ, kz, sub), BF), pltpu.VMEM((flat, sub), F32)],
        name="views",
    )(place, h_own, h_oth, w_parts, *after, *before, far_a, far_b)

    local = jnp.concatenate([mine, swap_core(theirs)], axis=1)
    got = ring_pieces(local[: STAT + blk // 2], local[STAT + blk // 2 :])

    w_recv = swap_core(w_sent)
    difference = cen[0] - cen[1] + (stats[0] - stats[1])[None, :]
    diff_share = (25.0 * jnp.sum(difference * difference) / (total_rows * full_width)).reshape(1, 1)

    wide = NZ * blk + 128
    flat_got = [piece for pair in got for piece in pair]
    whole = lambda s: pl.BlockSpec(s, lambda: (0,) * len(s))
    gathered, gram_part, view_stats = pl.pallas_call(
        functools.partial(gram_kernel, 1.0 / (full_width * NZ)),
        in_specs=[whole((1, 1))] + [whole(piece.shape) for piece in flat_got],
        out_specs=[whole((NZ * blk, 2 * sub)), whole((blk, wide)), whole((8, 2 * sub))],
        out_shape=[
            shape((NZ * blk, 2 * sub), BF),
            shape((blk, wide), BF),
            shape((8, 2 * sub), F32),
        ],
        name="gram",
    )(diff_share, *flat_got)

    stats_own = view_stats[:, :sub]
    stats_back = swap_core(view_stats[:, sub:])
    both_stats = jnp.stack(
        [jnp.where(first, stats_own, stats_back), jnp.where(first, stats_back, stats_own)]
    )
    variance = both_stats[:, 0]
    centered = cen + both_stats[:, 1][:, None, :]
    deviation = jnp.sqrt(variance + 0.0001)

    pieces = exchange(gram_part.reshape(NX * NY, blk // (NX * NY), wide), CHIPS)
    gram_rows = jnp.sum(pieces[:, :, : NZ * blk].astype(F32), axis=0).astype(BF)
    share = jnp.sum(pieces[:, :, NZ * blk :].astype(F32))
    gram_rows, share, variance, w_recv = lax.optimization_barrier((gram_rows, share, variance, w_recv))
    gram_half = exchange(copies(gram_rows, NX * NY), CHIPS).reshape(blk, NZ * blk)
    squares = gram_half.astype(F32)
    share = (share + jnp.sum(squares * squares) / ((total_rows - 1.0) ** 2 * full_width)).reshape(1, 1)
    spread_view = dot(gram_half, gathered, 1, 0)
    spread_own = spread_view[:, :sub]
    spread_back = swap_core(spread_view[:, sub:])
    spread = jnp.stack(
        [jnp.where(first, spread_own, spread_back), jnp.where(first, spread_back, spread_own)]
    )

    inv_grad = 50.0 / 256.0 * jnp.stack([difference, -difference])
    binding = (deviation < 1.0).astype(F32)
    hinge_grad = (
        -(25.0 * total_rows / (256.0 * (total_rows - 1.0)))
        * (binding / deviation)[:, None, :]
        * centered
    )
    cov_grad = (
        4.0
        * total_rows
        / 256.0
        * (spread / (total_rows - 1.0) ** 2 - variance[:, None, :] * centered / (total_rows - 1.0))
    )
    grad_views = (inv_grad + hinge_grad + cov_grad).astype(BF)
    grads = grad_views.reshape(2, NX, rows, sub).transpose(1, 0, 2, 3).reshape(flat, sub)

    terms = NX * kz + STAT
    weight_part = pl.pallas_call(
        weight_kernel,
        grid=(NY,),
        in_specs=[smem, at_dim(hblock, 1), at_dim(hblock, 1), fixed((flat, sub)), fixed((1, 1))],
        out_specs=fixed((NZ, terms, sub)),
        out_shape=shape((NZ, terms, sub), BF),
        name="weight_terms",
    )(place, h_own, h_oth, grads, share)

    input_part = pl.pallas_call(
        input_kernel,
        grid=(NY,),
        in_specs=[fixed((flat, sub)), fixed((flat, sub)), at_dim((1, kpart, sub), 0), at_dim((1, kpart, sub), 0)],
        out_specs=at_dim((1, flat, kpart), 0),
        out_shape=shape((NY, flat, kpart), BF),
        name="input_terms",
    )(grads, swap_core(grads), w_kept, w_recv)
    input_parts = exchange(input_part.reshape(NX * NY, 2, rows, kpart), ("y", "x"))
    input_grads = jnp.sum(input_parts.astype(F32), axis=0).astype(BF)

    weight_sum = ring_sum(weight_part, NX * kz // 2)
    loss_part = jnp.sum(weight_sum[NX * kz :]).reshape(1, 1)
    weight_sum = weight_sum[: NX * kz].astype(BF).reshape(NX, kz, sub)
    weight_sum, input_grads = lax.optimization_barrier((weight_sum, input_grads))
    blocks = exchange(weight_sum, "x")
    grad_weight = jnp.concatenate([blocks[k] for k in range(NX)], axis=1)
    total_loss = (loss_part + swap_core(loss_part))[0, 0]
    return (total_loss, grad_weight, input_grads[0], input_grads[1])


def solution(mesh):
    grid = Mesh(mesh.devices.reshape(NX, NZ, NY, NC), ("x", "z", "y", "c"))
    placed = P(("x", "z"), ("y", "c"))
    return jax.shard_map(
        on_device,
        mesh=grid,
        in_specs=(placed, placed, placed),
        out_specs=(P(), placed, placed, placed),
        check_vma=False,
    )
```

```python
import functools

import jax
import jax.numpy as jnp
from jax import lax
from jax.experimental import pallas as pl
from jax.experimental.pallas import tpu as pltpu
from jax.sharding import Mesh, PartitionSpec as P


BF = jnp.bfloat16
F32 = jnp.float32
NX, NZ, NY, NC = 4, 8, 4, 2
HALF = NZ // 2
CHIPS = ("x", "y")
SMEM = pltpu.SMEM
STAT = 16


def swap_core(v):
    return lax.ppermute(v, "c", [(0, 1), (1, 0)])


def hop(v, k):
    return lax.ppermute(v, "z", [(i, (i + k) % NZ) for i in range(NZ)])


def exchange(v, axes):
    return lax.all_to_all(v, axes, split_axis=0, concat_axis=0, tiled=True)


def copies(v, n):
    return jnp.broadcast_to(v[None], (n,) + v.shape)


def ring_blocks(v):
    right, left = [v], [v]
    for _ in range(1, HALF):
        right.append(hop(right[-1], 1))
        left.append(hop(left[-1], -1))
    half = v.shape[0] // 2
    far = (hop(right[-1][:half], 1), hop(left[-1][half:], -1))
    return left[1:], right[:0:-1], far


def ring_pieces(first, second):
    got = [[None, None] for _ in range(NZ)]
    got[0] = [first, second]
    for k in range(1, HALF + 1):
        for p in (0, 1):
            if k < HALF or p == 0:
                got[-k % NZ][p] = hop(got[(1 - k) % NZ][p], 1)
            if k < HALF or p == 1:
                got[k][p] = hop(got[k - 1][p], -1)
    return got


def ring_sum(terms, half):
    right = hop(terms[HALF][:half], 1)
    left = hop(terms[HALF][half:], -1)
    for d in range(HALF - 1, 0, -1):
        right, left = lax.optimization_barrier((right, left))
        right, left = right.astype(F32), left.astype(F32)
        if d == HALF - 1:
            low, high = jnp.zeros(left.shape, F32), jnp.zeros(right.shape, F32)
            right = jnp.concatenate([right, low], axis=0)
            left = jnp.concatenate([high, left], axis=0)
        right = hop((terms[d].astype(F32) + right).astype(BF), 1)
        left = hop((terms[NZ - d].astype(F32) + left).astype(BF), -1)
    return terms[0].astype(F32) + right.astype(F32) + left.astype(F32)


def split3(v):
    hi = v.astype(BF).astype(F32)
    mid = (v - hi).astype(BF).astype(F32)
    return [hi, mid, v - hi - mid]


def dot(a, b, ca, cb):
    return lax.dot_general(a, b, (((ca,), (cb,)), ((), ())), preferred_element_type=F32)


def fixed(shape):
    return pl.BlockSpec(shape, lambda j: (0,) * len(shape))


def at_dim(shape, dim):
    return pl.BlockSpec(shape, lambda j: tuple(j if d == dim else 0 for d in range(len(shape))))


def flat_rows(ref):
    nx, _, nv, rows, width = ref.shape
    return ref[:, 0].reshape(nx * nv * rows, width)


def views_kernel(place_ref, own_ref, oth_ref, *refs):
    w_refs, refs = refs[:7], refs[7:]
    far_a, far_b, kept_ref, sent_ref, cen_ref, mine_ref, theirs_ref, stat_ref, w_ref, acc = refs
    step = pl.program_id(0)
    core = place_ref[0]
    zi = place_ref[1]
    nx, _, nv, rows, kpart = own_ref.shape
    sub = acc.shape[1]
    for k, ref in zip((0, 1, 2, 3, 5, 6, 7), w_refs):
        w_ref[lax.rem(zi + k, NZ)] = ref[0]
    w_ref[lax.rem(zi + HALF, NZ)] = jnp.where(step < NY // 2, far_a[0], far_b[0])
    w_own = w_ref[pl.ds(core * HALF, HALF)].reshape(kpart, sub)
    w_oth = w_ref[pl.ds((1 - core) * HALF, HALF)].reshape(kpart, sub)
    kept_ref[0] = w_own
    sent_ref[0] = w_oth
    term = dot(flat_rows(own_ref), w_own, 1, 0) + dot(flat_rows(oth_ref), w_oth, 1, 0)

    @pl.when(step == 0)
    def _():
        acc[...] = term

    @pl.when(step > 0)
    def _():
        acc[...] += term

    @pl.when(step == pl.num_programs(0) - 1)
    def _():
        means, tails = [], []
        for v in range(nv):
            blocks = [acc[(a * nv + v) * rows : (a * nv + v + 1) * rows] for a in range(nx)]
            mean = sum(jnp.sum(block, axis=0, keepdims=True) for block in blocks) / (nx * rows * 1.0)
            means.append(mean)
            total = jnp.zeros_like(mean)
            for a in range(nx):
                block = blocks[a] - mean
                cen_ref[v, a * rows : (a + 1) * rows] = block
                total = total + jnp.sum(block * block, axis=0, keepdims=True)
            pad = jnp.zeros((STAT - 6, sub), F32)
            tails.append(jnp.concatenate(split3(mean) + split3(total) + [pad], axis=0).astype(BF))
        stat_ref[...] = jnp.concatenate(means + [jnp.zeros((6, sub), F32)], axis=0)
        data = [cen_ref[v].astype(BF) for v in range(nv)]
        for ref, same in ((mine_ref, core == 0), (theirs_ref, core == 1)):
            ref[:STAT] = jnp.where(same, tails[0], tails[1])
            ref[STAT:] = jnp.where(same, data[0], data[1])


def gram_kernel(scale_each, diff_ref, *refs):
    pieces, (all_ref, gram_ref, stat_ref) = refs[: 2 * NZ], refs[2 * NZ :]
    top = pieces[0].shape[0] - STAT
    blk = top + pieces[1].shape[0]
    stats = [pieces[2 * k][:STAT].astype(F32) for k in range(NZ)]
    means = [s[0:1] + s[1:2] + s[2:3] for s in stats]
    center = sum(means) / (NZ * 1.0)
    total = sum(s[3:4] + s[4:5] + s[5:6] for s in stats)
    for k in range(NZ):
        move = means[k] - center
        total = total + blk * (move * move)
        all_ref[k * blk : k * blk + top] = (pieces[2 * k][STAT:].astype(F32) + move).astype(BF)
        all_ref[k * blk + top : (k + 1) * blk] = (pieces[2 * k + 1][...].astype(F32) + move).astype(BF)
        gram_ref[:, k * blk : (k + 1) * blk] = dot(
            all_ref[:blk], all_ref[k * blk : (k + 1) * blk], 1, 1
        ).astype(BF)
    variance = total / (NZ * blk - 1.0)
    pad = jnp.zeros((6, total.shape[1]), F32)
    stat_ref[...] = jnp.concatenate([variance, means[0] - center, pad], axis=0)
    hinge = jnp.maximum(1.0 - jnp.sqrt(variance + 0.0001), 0.0)
    share = diff_ref[...] + scale_each * jnp.sum(25.0 * hinge - variance * variance, axis=1, keepdims=True)
    extra = gram_ref.shape[1] - NZ * blk
    row = lax.broadcasted_iota(jnp.int32, (blk, extra), 0)
    lane = lax.broadcasted_iota(jnp.int32, (blk, extra), 1)
    lead = lax.rem(row, blk // (NX * NY)) == 0
    gram_ref[:, NZ * blk :] = in_lanes(share, lane, 0, lead).astype(BF)


def in_lanes(value, lane, start, keep):
    out = jnp.zeros(lane.shape, F32)
    for n, term in enumerate(split3(value)):
        out = jnp.where(keep & (lane == start + n), term, out)
    return out


def weight_kernel(place_ref, own_ref, oth_ref, g_ref, share_ref, out_ref):
    step = pl.program_id(0)
    core = place_ref[0]
    zi = place_ref[1]
    rows = NY * (own_ref.shape[4] // HALF)
    kz = rows // NY
    for ref, lead in ((own_ref, core), (oth_ref, 1 - core)):
        term = dot(flat_rows(ref), g_ref[...], 0, 0).astype(BF)
        for q in range(HALF):
            k = lax.rem(lead * HALF + q - zi + NZ, NZ)
            out_ref[k, pl.ds(pl.multiple_of(step * kz, kz), kz)] = term[q * kz : (q + 1) * kz]

    @pl.when(step == 0)
    def _():
        row = lax.broadcasted_iota(jnp.int32, (STAT, out_ref.shape[2]), 0)
        lane = lax.broadcasted_iota(jnp.int32, (STAT, out_ref.shape[2]), 1)
        tail = in_lanes(share_ref[...], lane, 3 * zi, row == 0).astype(BF)
        for k in range(NZ):
            out_ref[k, rows:] = tail


def input_kernel(own_ref, oth_ref, kept_ref, recv_ref, out_ref):
    term = dot(own_ref[...], kept_ref[0], 1, 1) + dot(oth_ref[...], recv_ref[0], 1, 1)
    out_ref[0] = term.astype(BF)


def on_device(hidden_first, hidden_second, weight):
    core = lax.axis_index("c")
    place = jnp.stack([core, lax.axis_index("z")]).astype(jnp.int32)
    first = core == 0
    rows, kpart = hidden_first.shape
    kz, cols = weight.shape
    total_rows = rows * NX * NZ * 1.0
    full_width = cols * NY * NC * 1.0
    blk = rows * NX
    flat = 2 * blk
    sub = cols // NX
    hshape = (NX, NY, 2, rows, kpart)
    hblock = (NX, 1, 2, rows, kpart)
    smem = pl.BlockSpec(memory_space=SMEM)
    shape = jax.ShapeDtypeStruct

    w_parts = exchange(jnp.stack([weight[:, k * sub : (k + 1) * sub] for k in range(NX)]), "x")
    moved = copies(jnp.stack([hidden_first, hidden_second]), NX * NY)
    moved, w_parts = lax.optimization_barrier((moved, w_parts))
    h_own = exchange(moved, CHIPS).reshape(hshape)
    after, before, (far_a, far_b) = ring_blocks(w_parts)
    h_own, _, _ = lax.optimization_barrier((h_own, after[-1], before[0]))
    h_oth = swap_core(h_own)

    block_spec = at_dim((1, kz, sub), 0)
    w_kept, w_sent, cen, mine, theirs, stats = pl.pallas_call(
        views_kernel,
        grid=(NY,),
        in_specs=[smem, at_dim(hblock, 1), at_dim(hblock, 1)]
        + [block_spec] * 7
        + [
            pl.BlockSpec((1, kz, sub), lambda j: (jnp.minimum(j, NX // 2 - 1), 0, 0)),
            pl.BlockSpec((1, kz, sub), lambda j: (jnp.maximum(j - NX // 2, 0), 0, 0)),
        ],
        out_specs=[
            at_dim((1, kpart, sub), 0),
            at_dim((1, kpart, sub), 0),
            fixed((2, blk, sub)),
            fixed((blk + STAT, sub)),
            fixed((blk + STAT, sub)),
            fixed((8, sub)),
        ],
        out_shape=[
            shape((NY, kpart, sub), BF),
            shape((NY, kpart, sub), BF),
            shape((2, blk, sub), F32),
            shape((blk + STAT, sub), BF),
            shape((blk + STAT, sub), BF),
            shape((8, sub), F32),
        ],
        scratch_shapes=[pltpu.VMEM((NZ, kz, sub), BF), pltpu.VMEM((flat, sub), F32)],
        name="views",
    )(place, h_own, h_oth, w_parts, *after, *before, far_a, far_b)

    local = jnp.concatenate([mine, swap_core(theirs)], axis=1)
    got = ring_pieces(local[: STAT + blk // 2], local[STAT + blk // 2 :])

    w_recv = swap_core(w_sent)
    difference = cen[0] - cen[1] + (stats[0] - stats[1])[None, :]
    diff_share = (25.0 * jnp.sum(difference * difference) / (total_rows * full_width)).reshape(1, 1)

    wide = NZ * blk + 128
    flat_got = [piece for pair in got for piece in pair]
    whole = lambda s: pl.BlockSpec(s, lambda: (0,) * len(s))
    gathered, gram_part, view_stats = pl.pallas_call(
        functools.partial(gram_kernel, 1.0 / (full_width * NZ)),
        in_specs=[whole((1, 1))] + [whole(piece.shape) for piece in flat_got],
        out_specs=[whole((NZ * blk, 2 * sub)), whole((blk, wide)), whole((8, 2 * sub))],
        out_shape=[
            shape((NZ * blk, 2 * sub), BF),
            shape((blk, wide), BF),
            shape((8, 2 * sub), F32),
        ],
        name="gram",
    )(diff_share, *flat_got)

    stats_own = view_stats[:, :sub]
    stats_back = swap_core(view_stats[:, sub:])
    both_stats = jnp.stack(
        [jnp.where(first, stats_own, stats_back), jnp.where(first, stats_back, stats_own)]
    )
    variance = both_stats[:, 0]
    centered = cen + both_stats[:, 1][:, None, :]
    deviation = jnp.sqrt(variance + 0.0001)

    inv_grad = 50.0 / 256.0 * jnp.stack([difference, -difference])
    binding = (deviation < 1.0).astype(F32)
    hinge_scale = -(25.0 * total_rows / (256.0 * (total_rows - 1.0))) * binding / deviation
    cov_scale = 4.0 * total_rows / 256.0 * variance / (total_rows - 1.0)
    base = inv_grad + (hinge_scale - cov_scale)[:, None, :] * centered

    pieces = exchange(gram_part.reshape(NX * NY, blk // (NX * NY), wide), CHIPS)
    gram_rows = jnp.sum(pieces[:, :, : NZ * blk].astype(F32), axis=0).astype(BF)
    share = jnp.sum(pieces[:, :, NZ * blk :].astype(F32))
    gram_rows, share, base, w_recv = lax.optimization_barrier((gram_rows, share, base, w_recv))
    gram_half = exchange(copies(gram_rows, NX * NY), CHIPS).reshape(blk, NZ * blk)
    squares = gram_half.astype(F32)
    share = (share + jnp.sum(squares * squares) / ((total_rows - 1.0) ** 2 * full_width)).reshape(1, 1)
    spread_view = dot(gram_half, gathered, 1, 0)
    spread_own = spread_view[:, :sub]
    spread_back = swap_core(spread_view[:, sub:])
    spread = jnp.stack(
        [jnp.where(first, spread_own, spread_back), jnp.where(first, spread_back, spread_own)]
    )

    grad_views = (base + 4.0 * total_rows / 256.0 / (total_rows - 1.0) ** 2 * spread).astype(BF)
    grads = grad_views.reshape(2, NX, rows, sub).transpose(1, 0, 2, 3).reshape(flat, sub)

    terms = NX * kz + STAT
    weight_part = pl.pallas_call(
        weight_kernel,
        grid=(NY,),
        in_specs=[smem, at_dim(hblock, 1), at_dim(hblock, 1), fixed((flat, sub)), fixed((1, 1))],
        out_specs=fixed((NZ, terms, sub)),
        out_shape=shape((NZ, terms, sub), BF),
        name="weight_terms",
    )(place, h_own, h_oth, grads, share)

    input_part = pl.pallas_call(
        input_kernel,
        grid=(NY,),
        in_specs=[fixed((flat, sub)), fixed((flat, sub)), at_dim((1, kpart, sub), 0), at_dim((1, kpart, sub), 0)],
        out_specs=at_dim((1, flat, kpart), 0),
        out_shape=shape((NY, flat, kpart), BF),
        name="input_terms",
    )(grads, swap_core(grads), w_kept, w_recv)
    input_parts = exchange(input_part.reshape(NX * NY, 2, rows, kpart), ("y", "x"))
    weight_sum = ring_sum(weight_part, NX * kz // 2)
    loss_rows = weight_sum[NX * kz :]
    weight_sum = weight_sum[: NX * kz].astype(BF).reshape(NX, kz, sub)
    weight_sum, loss_rows, input_parts = lax.optimization_barrier((weight_sum, loss_rows, input_parts))
    loss_part = jnp.sum(loss_rows).reshape(1, 1)
    blocks = exchange(weight_sum, "x")
    input_grads = jnp.sum(input_parts.astype(F32), axis=0).astype(BF)
    grad_weight = jnp.concatenate([blocks[k] for k in range(NX)], axis=1)
    total_loss = (loss_part + swap_core(loss_part))[0, 0]
    return (total_loss, grad_weight, input_grads[0], input_grads[1])


def solution(mesh):
    grid = Mesh(mesh.devices.reshape(NX, NZ, NY, NC), ("x", "z", "y", "c"))
    placed = P(("x", "z"), ("y", "c"))

    return jax.shard_map(
        on_device,
        mesh=grid,
        in_specs=(placed, placed, placed),
        out_specs=(P(), placed, placed, placed),
        check_vma=False,
    )
```

```python
import functools

import jax
import jax.numpy as jnp
from jax import lax
from jax.experimental import pallas as pl
from jax.experimental.pallas import tpu as pltpu
from jax.sharding import Mesh, PartitionSpec as P


BF = jnp.bfloat16
F32 = jnp.float32
NX, NZ, NY, NC = 4, 8, 4, 2
HALF = NZ // 2
CHIPS = ("x", "y")
SMEM = pltpu.SMEM
STAT = 16


def swap_core(v):
    return lax.ppermute(v, "c", [(0, 1), (1, 0)])


def hop(v, k):
    return lax.ppermute(v, "z", [(i, (i + k) % NZ) for i in range(NZ)])


def exchange(v, axes):
    return lax.all_to_all(v, axes, split_axis=0, concat_axis=0, tiled=True)


def copies(v, n):
    return jnp.broadcast_to(v[None], (n,) + v.shape)


def ring_blocks(v):
    right, left = [v], [v]
    for _ in range(1, HALF):
        right.append(hop(right[-1], 1))
        left.append(hop(left[-1], -1))
    half = v.shape[0] // 2
    far = (hop(right[-1][:half], 1), hop(left[-1][half:], -1))
    return left[1:], right[:0:-1], far


def ring_pieces(first, second):
    got = [[None, None] for _ in range(NZ)]
    got[0] = [first, second]
    for k in range(1, HALF + 1):
        for p in (0, 1):
            if k < HALF or p == 0:
                got[-k % NZ][p] = hop(got[(1 - k) % NZ][p], 1)
            if k < HALF or p == 1:
                got[k][p] = hop(got[k - 1][p], -1)
    return got


def ring_sum(terms, right, left):
    for d in range(HALF - 1, 0, -1):
        right, left = lax.optimization_barrier((right, left))
        right, left = right.astype(F32), left.astype(F32)
        if d == HALF - 1:
            low, high = jnp.zeros(left.shape, F32), jnp.zeros(right.shape, F32)
            right = jnp.concatenate([right, low], axis=0)
            left = jnp.concatenate([high, left], axis=0)
        right = hop((terms[d].astype(F32) + right).astype(BF), 1)
        left = hop((terms[NZ - d].astype(F32) + left).astype(BF), -1)
    return terms[0].astype(F32) + right.astype(F32) + left.astype(F32)


def split3(v):
    hi = v.astype(BF).astype(F32)
    mid = (v - hi).astype(BF).astype(F32)
    return [hi, mid, v - hi - mid]


def dot(a, b, ca, cb):
    return lax.dot_general(a, b, (((ca,), (cb,)), ((), ())), preferred_element_type=F32)


def fixed(shape):
    return pl.BlockSpec(shape, lambda j: (0,) * len(shape))


def at_dim(shape, dim):
    return pl.BlockSpec(shape, lambda j: tuple(j if d == dim else 0 for d in range(len(shape))))


def flat_rows(ref):
    nx, _, nv, rows, width = ref.shape
    return ref[:, 0].reshape(nx * nv * rows, width)


def views_kernel(place_ref, own_ref, oth_ref, *refs):
    w_refs, refs = refs[:7], refs[7:]
    far_a, far_b, kept_ref, sent_ref, cen_ref, mine_ref, theirs_ref, stat_ref, w_ref, acc = refs
    step = pl.program_id(0)
    core = place_ref[0]
    zi = place_ref[1]
    nx, _, nv, rows, kpart = own_ref.shape
    sub = acc.shape[1]
    for k, ref in zip((0, 1, 2, 3, 5, 6, 7), w_refs):
        w_ref[lax.rem(zi + k, NZ)] = ref[0]
    w_ref[lax.rem(zi + HALF, NZ)] = jnp.where(step < NY // 2, far_a[0], far_b[0])
    w_own = w_ref[pl.ds(core * HALF, HALF)].reshape(kpart, sub)
    w_oth = w_ref[pl.ds((1 - core) * HALF, HALF)].reshape(kpart, sub)
    kept_ref[0] = w_own
    sent_ref[0] = w_oth
    term = dot(flat_rows(own_ref), w_own, 1, 0) + dot(flat_rows(oth_ref), w_oth, 1, 0)

    @pl.when(step == 0)
    def _():
        acc[...] = term

    @pl.when(step > 0)
    def _():
        acc[...] += term

    @pl.when(step == pl.num_programs(0) - 1)
    def _():
        means, tails = [], []
        for v in range(nv):
            blocks = [acc[(a * nv + v) * rows : (a * nv + v + 1) * rows] for a in range(nx)]
            mean = sum(jnp.sum(block, axis=0, keepdims=True) for block in blocks) / (nx * rows * 1.0)
            means.append(mean)
            total = jnp.zeros_like(mean)
            for a in range(nx):
                block = blocks[a] - mean
                cen_ref[v, a * rows : (a + 1) * rows] = block
                total = total + jnp.sum(block * block, axis=0, keepdims=True)
            pad = jnp.zeros((STAT - 6, sub), F32)
            tails.append(jnp.concatenate(split3(mean) + split3(total) + [pad], axis=0).astype(BF))
        stat_ref[...] = jnp.concatenate(means + [jnp.zeros((6, sub), F32)], axis=0)
        data = [cen_ref[v].astype(BF) for v in range(nv)]
        for ref, same in ((mine_ref, core == 0), (theirs_ref, core == 1)):
            ref[:STAT] = jnp.where(same, tails[0], tails[1])
            ref[STAT:] = jnp.where(same, data[0], data[1])


def gram_kernel(scale_each, diff_ref, *refs):
    pieces, (all_ref, gram_ref, stat_ref) = refs[: 2 * NZ], refs[2 * NZ :]
    top = pieces[0].shape[0] - STAT
    blk = top + pieces[1].shape[0]
    stats = [pieces[2 * k][:STAT].astype(F32) for k in range(NZ)]
    means = [s[0:1] + s[1:2] + s[2:3] for s in stats]
    center = sum(means) / (NZ * 1.0)
    total = sum(s[3:4] + s[4:5] + s[5:6] for s in stats)
    for k in range(NZ):
        move = means[k] - center
        total = total + blk * (move * move)
        all_ref[k * blk : k * blk + top] = (pieces[2 * k][STAT:].astype(F32) + move).astype(BF)
        all_ref[k * blk + top : (k + 1) * blk] = (pieces[2 * k + 1][...].astype(F32) + move).astype(BF)
        gram_ref[:, k * blk : (k + 1) * blk] = dot(
            all_ref[:blk], all_ref[k * blk : (k + 1) * blk], 1, 1
        ).astype(BF)
    variance = total / (NZ * blk - 1.0)
    pad = jnp.zeros((6, total.shape[1]), F32)
    stat_ref[...] = jnp.concatenate([variance, means[0] - center, pad], axis=0)
    hinge = jnp.maximum(1.0 - jnp.sqrt(variance + 0.0001), 0.0)
    share = diff_ref[...] + scale_each * jnp.sum(25.0 * hinge - variance * variance, axis=1, keepdims=True)
    extra = gram_ref.shape[1] - NZ * blk
    row = lax.broadcasted_iota(jnp.int32, (blk, extra), 0)
    lane = lax.broadcasted_iota(jnp.int32, (blk, extra), 1)
    lead = lax.rem(row, blk // (NX * NY)) == 0
    gram_ref[:, NZ * blk :] = in_lanes(share, lane, 0, lead).astype(BF)


def in_lanes(value, lane, start, keep):
    out = jnp.zeros(lane.shape, F32)
    for n, term in enumerate(split3(value)):
        out = jnp.where(keep & (lane == start + n), term, out)
    return out


def weight_kernel(place_ref, own_ref, oth_ref, g_ref, share_ref, out_ref):
    step = pl.program_id(0)
    core = place_ref[0]
    zi = place_ref[1]
    rows = NY * (own_ref.shape[4] // HALF)
    kz = rows // NY
    for ref, lead in ((own_ref, core), (oth_ref, 1 - core)):
        term = dot(flat_rows(ref), g_ref[...], 0, 0).astype(BF)
        for q in range(HALF):
            k = lax.rem(lead * HALF + q - zi + NZ, NZ)
            out_ref[k, pl.ds(pl.multiple_of(step * kz, kz), kz)] = term[q * kz : (q + 1) * kz]

    @pl.when(step == 0)
    def _():
        row = lax.broadcasted_iota(jnp.int32, (STAT, out_ref.shape[2]), 0)
        lane = lax.broadcasted_iota(jnp.int32, (STAT, out_ref.shape[2]), 1)
        tail = in_lanes(share_ref[...], lane, 3 * zi, row == 0).astype(BF)
        for k in range(NZ):
            out_ref[k, rows:] = tail


def far_kernel(place_ref, own_ref, oth_ref, g_ref, share_ref, a_ref, b_ref):
    step = pl.program_id(0)
    core = place_ref[0]
    zi = place_ref[1]
    kz = own_ref.shape[4]
    mine = 1 - zi // HALF == core
    block = jnp.where(mine, flat_rows(own_ref).astype(F32), flat_rows(oth_ref).astype(F32)).astype(BF)
    term = dot(block, g_ref[...], 0, 0).astype(BF)
    place = pl.ds(pl.multiple_of(lax.rem(step, NY // 2) * kz, kz), kz)

    @pl.when(step < NY // 2)
    def _():
        a_ref[place] = term

    @pl.when(step >= NY // 2)
    def _():
        b_ref[place] = term

    @pl.when(step == 0)
    def _():
        row = lax.broadcasted_iota(jnp.int32, (STAT, b_ref.shape[1]), 0)
        lane = lax.broadcasted_iota(jnp.int32, (STAT, b_ref.shape[1]), 1)
        b_ref[NY // 2 * kz :] = in_lanes(share_ref[...], lane, 3 * zi, row == 0).astype(BF)


def input_kernel(own_ref, oth_ref, kept_ref, recv_ref, out_ref):
    term = dot(own_ref[...], kept_ref[0], 1, 1) + dot(oth_ref[...], recv_ref[0], 1, 1)
    out_ref[0] = term.astype(BF)


def on_device(hidden_first, hidden_second, weight):
    core = lax.axis_index("c")
    place = jnp.stack([core, lax.axis_index("z")]).astype(jnp.int32)
    first = core == 0
    rows, kpart = hidden_first.shape
    kz, cols = weight.shape
    total_rows = rows * NX * NZ * 1.0
    full_width = cols * NY * NC * 1.0
    blk = rows * NX
    flat = 2 * blk
    sub = cols // NX
    hshape = (NX, NY, 2, rows, kpart)
    hblock = (NX, 1, 2, rows, kpart)
    smem = pl.BlockSpec(memory_space=SMEM)
    shape = jax.ShapeDtypeStruct

    w_parts = exchange(jnp.stack([weight[:, k * sub : (k + 1) * sub] for k in range(NX)]), "x")
    moved = copies(jnp.stack([hidden_first, hidden_second]), NX * NY)
    moved, w_parts = lax.optimization_barrier((moved, w_parts))
    h_own = exchange(moved, CHIPS).reshape(hshape)
    after, before, (far_a, far_b) = ring_blocks(w_parts)
    h_own, _, _ = lax.optimization_barrier((h_own, after[-1], before[0]))
    h_oth = swap_core(h_own)

    block_spec = at_dim((1, kz, sub), 0)
    w_kept, w_sent, cen, mine, theirs, stats = pl.pallas_call(
        views_kernel,
        grid=(NY,),
        in_specs=[smem, at_dim(hblock, 1), at_dim(hblock, 1)]
        + [block_spec] * 7
        + [
            pl.BlockSpec((1, kz, sub), lambda j: (jnp.minimum(j, NX // 2 - 1), 0, 0)),
            pl.BlockSpec((1, kz, sub), lambda j: (jnp.maximum(j - NX // 2, 0), 0, 0)),
        ],
        out_specs=[
            at_dim((1, kpart, sub), 0),
            at_dim((1, kpart, sub), 0),
            fixed((2, blk, sub)),
            fixed((blk + STAT, sub)),
            fixed((blk + STAT, sub)),
            fixed((8, sub)),
        ],
        out_shape=[
            shape((NY, kpart, sub), BF),
            shape((NY, kpart, sub), BF),
            shape((2, blk, sub), F32),
            shape((blk + STAT, sub), BF),
            shape((blk + STAT, sub), BF),
            shape((8, sub), F32),
        ],
        scratch_shapes=[pltpu.VMEM((NZ, kz, sub), BF), pltpu.VMEM((flat, sub), F32)],
        name="views",
    )(place, h_own, h_oth, w_parts, *after, *before, far_a, far_b)

    local = jnp.concatenate([mine, swap_core(theirs)], axis=1)
    got = ring_pieces(local[: STAT + blk // 2], local[STAT + blk // 2 :])

    w_recv = swap_core(w_sent)
    difference = cen[0] - cen[1] + (stats[0] - stats[1])[None, :]
    diff_share = (25.0 * jnp.sum(difference * difference) / (total_rows * full_width)).reshape(1, 1)

    wide = NZ * blk + 128
    flat_got = [piece for pair in got for piece in pair]
    whole = lambda s: pl.BlockSpec(s, lambda: (0,) * len(s))
    gathered, gram_part, view_stats = pl.pallas_call(
        functools.partial(gram_kernel, 1.0 / (full_width * NZ)),
        in_specs=[whole((1, 1))] + [whole(piece.shape) for piece in flat_got],
        out_specs=[whole((NZ * blk, 2 * sub)), whole((blk, wide)), whole((8, 2 * sub))],
        out_shape=[
            shape((NZ * blk, 2 * sub), BF),
            shape((blk, wide), BF),
            shape((8, 2 * sub), F32),
        ],
        name="gram",
    )(diff_share, *flat_got)

    stats_own = view_stats[:, :sub]
    stats_back = swap_core(view_stats[:, sub:])
    both_stats = jnp.stack(
        [jnp.where(first, stats_own, stats_back), jnp.where(first, stats_back, stats_own)]
    )
    variance = both_stats[:, 0]
    centered = cen + both_stats[:, 1][:, None, :]
    deviation = jnp.sqrt(variance + 0.0001)

    pieces = exchange(gram_part.reshape(NX * NY, blk // (NX * NY), wide), CHIPS)
    gram_rows = jnp.sum(pieces[:, :, : NZ * blk].astype(F32), axis=0).astype(BF)
    share = jnp.sum(pieces[:, :, NZ * blk :].astype(F32))
    gram_rows, share, variance, w_recv = lax.optimization_barrier((gram_rows, share, variance, w_recv))
    gram_half = exchange(copies(gram_rows, NX * NY), CHIPS).reshape(blk, NZ * blk)
    squares = gram_half.astype(F32)
    share = (share + jnp.sum(squares * squares) / ((total_rows - 1.0) ** 2 * full_width)).reshape(1, 1)
    spread_view = dot(gram_half, gathered, 1, 0)
    spread_own = spread_view[:, :sub]
    spread_back = swap_core(spread_view[:, sub:])
    spread = jnp.stack(
        [jnp.where(first, spread_own, spread_back), jnp.where(first, spread_back, spread_own)]
    )

    inv_grad = 50.0 / 256.0 * jnp.stack([difference, -difference])
    binding = (deviation < 1.0).astype(F32)
    hinge_grad = (
        -(25.0 * total_rows / (256.0 * (total_rows - 1.0)))
        * (binding / deviation)[:, None, :]
        * centered
    )
    cov_grad = (
        4.0
        * total_rows
        / 256.0
        * (spread / (total_rows - 1.0) ** 2 - variance[:, None, :] * centered / (total_rows - 1.0))
    )
    grad_views = (inv_grad + hinge_grad + cov_grad).astype(BF)
    grads = grad_views.reshape(2, NX, rows, sub).transpose(1, 0, 2, 3).reshape(flat, sub)

    far_block = pl.BlockSpec((NX, 1, 2, rows, kz), lambda j, place: (0, j, 0, 0, lax.rem(place[1], HALF)))
    held = lambda s: pl.BlockSpec(s, lambda j, place: (0,) * len(s))
    half = NX // 2 * kz
    far_right, far_left = pl.pallas_call(
        far_kernel,
        grid_spec=pltpu.PrefetchScalarGridSpec(
            num_scalar_prefetch=1,
            grid=(NY,),
            in_specs=[far_block, far_block, held((flat, sub)), held((1, 1))],
            out_specs=[held((half, sub)), held((half + STAT, sub))],
        ),
        out_shape=[shape((half, sub), BF), shape((half + STAT, sub), BF)],
        name="far_terms",
    )(place, h_own, h_oth, grads, share)
    right = hop(far_right, 1)
    left = hop(far_left, -1)

    later, _, _ = lax.optimization_barrier((grads, far_right, far_left))
    input_part = pl.pallas_call(
        input_kernel,
        grid=(NY,),
        in_specs=[fixed((flat, sub)), fixed((flat, sub)), at_dim((1, kpart, sub), 0), at_dim((1, kpart, sub), 0)],
        out_specs=at_dim((1, flat, kpart), 0),
        out_shape=shape((NY, flat, kpart), BF),
        name="input_terms",
    )(later, swap_core(grads), w_kept, w_recv)
    input_parts = exchange(input_part.reshape(NX * NY, 2, rows, kpart), ("y", "x"))

    later, _ = lax.optimization_barrier((later, input_part))
    terms = NX * kz + STAT
    weight_part = pl.pallas_call(
        weight_kernel,
        grid=(NY,),
        in_specs=[smem, at_dim(hblock, 1), at_dim(hblock, 1), fixed((flat, sub)), fixed((1, 1))],
        out_specs=fixed((NZ, terms, sub)),
        out_shape=shape((NZ, terms, sub), BF),
        name="weight_terms",
    )(place, h_own, h_oth, later, share)

    weight_sum = ring_sum(weight_part, right, left)
    loss_rows = weight_sum[NX * kz :]
    weight_sum = weight_sum[: NX * kz].astype(BF).reshape(NX, kz, sub)
    weight_sum, loss_rows, input_parts = lax.optimization_barrier((weight_sum, loss_rows, input_parts))
    loss_part = jnp.sum(loss_rows).reshape(1, 1)
    blocks = exchange(weight_sum, "x")
    input_grads = jnp.sum(input_parts.astype(F32), axis=0).astype(BF)
    grad_weight = jnp.concatenate([blocks[k] for k in range(NX)], axis=1)
    total_loss = (loss_part + swap_core(loss_part))[0, 0]
    return (total_loss, grad_weight, input_grads[0], input_grads[1])


def solution(mesh):
    grid = Mesh(mesh.devices.reshape(NX, NZ, NY, NC), ("x", "z", "y", "c"))
    placed = P(("x", "z"), ("y", "c"))

    return jax.shard_map(
        on_device,
        mesh=grid,
        in_specs=(placed, placed, placed),
        out_specs=(P(), placed, placed, placed),
        check_vma=False,
    )
```

```python
import functools

import jax
import jax.numpy as jnp
from jax import lax
from jax.experimental import pallas as pl
from jax.experimental.pallas import tpu as pltpu
from jax.sharding import Mesh, PartitionSpec as P


BF = jnp.bfloat16
F32 = jnp.float32
NX, NZ, NY, NC = 4, 8, 4, 2
HALF = NZ // 2
CHIPS = ("x", "y")
SMEM = pltpu.SMEM
STAT = 16


def swap_core(v):
    return lax.ppermute(v, "c", [(0, 1), (1, 0)])


def hop(v, k):
    return lax.ppermute(v, "z", [(i, (i + k) % NZ) for i in range(NZ)])


def exchange(v, axes):
    return lax.all_to_all(v, axes, split_axis=0, concat_axis=0, tiled=True)


def copies(v, n):
    return jnp.broadcast_to(v[None], (n,) + v.shape)


def ring_blocks(v):
    right, left = [v], [v]
    for _ in range(1, HALF):
        right.append(hop(right[-1], 1))
        left.append(hop(left[-1], -1))
    half = v.shape[0] // 2
    far = (hop(right[-1][:half], 1), hop(left[-1][half:], -1))
    return left[1:], right[:0:-1], far


def ring_pieces(first, second):
    got = [[None, None] for _ in range(NZ)]
    got[0] = [first, second]
    for k in range(1, HALF + 1):
        for p in (0, 1):
            if k < HALF or p == 0:
                got[-k % NZ][p] = hop(got[(1 - k) % NZ][p], 1)
            if k < HALF or p == 1:
                got[k][p] = hop(got[k - 1][p], -1)
    return got


def ring_sum(terms, right, left):
    for d in range(HALF - 1, 0, -1):
        right, left = lax.optimization_barrier((right, left))
        right, left = right.astype(F32), left.astype(F32)
        if d == HALF - 1:
            low, high = jnp.zeros(left.shape, F32), jnp.zeros(right.shape, F32)
            right = jnp.concatenate([right, low], axis=0)
            left = jnp.concatenate([high, left], axis=0)
        right = hop((terms[d].astype(F32) + right).astype(BF), 1)
        left = hop((terms[NZ - d].astype(F32) + left).astype(BF), -1)
    return terms[0].astype(F32) + right.astype(F32) + left.astype(F32)


def split3(v):
    hi = v.astype(BF).astype(F32)
    mid = (v - hi).astype(BF).astype(F32)
    return [hi, mid, v - hi - mid]


def dot(a, b, ca, cb):
    return lax.dot_general(a, b, (((ca,), (cb,)), ((), ())), preferred_element_type=F32)


def fixed(shape):
    return pl.BlockSpec(shape, lambda j: (0,) * len(shape))


def at_dim(shape, dim):
    return pl.BlockSpec(shape, lambda j: tuple(j if d == dim else 0 for d in range(len(shape))))


def flat_rows(ref):
    nx, _, nv, rows, width = ref.shape
    return ref[:, 0].reshape(nx * nv * rows, width)


def views_kernel(place_ref, own_ref, oth_ref, *refs):
    w_refs, refs = refs[:7], refs[7:]
    far_a, far_b, kept_ref, sent_ref, cen_ref, mine_ref, theirs_ref, stat_ref, w_ref, acc = refs
    step = pl.program_id(0)
    core = place_ref[0]
    zi = place_ref[1]
    nx, _, nv, rows, kpart = own_ref.shape
    sub = acc.shape[1]
    for k, ref in zip((0, 1, 2, 3, 5, 6, 7), w_refs):
        w_ref[lax.rem(zi + k, NZ)] = ref[0]
    w_ref[lax.rem(zi + HALF, NZ)] = jnp.where(step < NY // 2, far_a[0], far_b[0])
    w_own = w_ref[pl.ds(core * HALF, HALF)].reshape(kpart, sub)
    w_oth = w_ref[pl.ds((1 - core) * HALF, HALF)].reshape(kpart, sub)
    kept_ref[0] = w_own
    sent_ref[0] = w_oth
    term = dot(flat_rows(own_ref), w_own, 1, 0) + dot(flat_rows(oth_ref), w_oth, 1, 0)

    @pl.when(step == 0)
    def _():
        acc[...] = term

    @pl.when(step > 0)
    def _():
        acc[...] += term

    @pl.when(step == pl.num_programs(0) - 1)
    def _():
        means, tails = [], []
        for v in range(nv):
            blocks = [acc[(a * nv + v) * rows : (a * nv + v + 1) * rows] for a in range(nx)]
            mean = sum(jnp.sum(block, axis=0, keepdims=True) for block in blocks) / (nx * rows * 1.0)
            means.append(mean)
            total = jnp.zeros_like(mean)
            for a in range(nx):
                block = blocks[a] - mean
                cen_ref[v, a * rows : (a + 1) * rows] = block
                total = total + jnp.sum(block * block, axis=0, keepdims=True)
            pad = jnp.zeros((STAT - 6, sub), F32)
            tails.append(jnp.concatenate(split3(mean) + split3(total) + [pad], axis=0).astype(BF))
        stat_ref[...] = jnp.concatenate(means + [jnp.zeros((6, sub), F32)], axis=0)
        data = [cen_ref[v].astype(BF) for v in range(nv)]
        for ref, same in ((mine_ref, core == 0), (theirs_ref, core == 1)):
            ref[:STAT] = jnp.where(same, tails[0], tails[1])
            ref[STAT:] = jnp.where(same, data[0], data[1])


def gram_kernel(scale_each, diff_ref, *refs):
    pieces, (all_ref, gram_ref, stat_ref) = refs[: 2 * NZ], refs[2 * NZ :]
    top = pieces[0].shape[0] - STAT
    blk = top + pieces[1].shape[0]
    stats = [pieces[2 * k][:STAT].astype(F32) for k in range(NZ)]
    means = [s[0:1] + s[1:2] + s[2:3] for s in stats]
    center = sum(means) / (NZ * 1.0)
    total = sum(s[3:4] + s[4:5] + s[5:6] for s in stats)
    for k in range(NZ):
        move = means[k] - center
        total = total + blk * (move * move)
        all_ref[k * blk : k * blk + top] = (pieces[2 * k][STAT:].astype(F32) + move).astype(BF)
        all_ref[k * blk + top : (k + 1) * blk] = (pieces[2 * k + 1][...].astype(F32) + move).astype(BF)
        gram_ref[:, k * blk : (k + 1) * blk] = dot(
            all_ref[:blk], all_ref[k * blk : (k + 1) * blk], 1, 1
        ).astype(BF)
    variance = total / (NZ * blk - 1.0)
    pad = jnp.zeros((6, total.shape[1]), F32)
    stat_ref[...] = jnp.concatenate([variance, means[0] - center, pad], axis=0)
    hinge = jnp.maximum(1.0 - jnp.sqrt(variance + 0.0001), 0.0)
    share = diff_ref[...] + scale_each * jnp.sum(25.0 * hinge - variance * variance, axis=1, keepdims=True)
    extra = gram_ref.shape[1] - NZ * blk
    row = lax.broadcasted_iota(jnp.int32, (blk, extra), 0)
    lane = lax.broadcasted_iota(jnp.int32, (blk, extra), 1)
    lead = lax.rem(row, blk // (NX * NY)) == 0
    gram_ref[:, NZ * blk :] = in_lanes(share, lane, 0, lead).astype(BF)


def in_lanes(value, lane, start, keep):
    out = jnp.zeros(lane.shape, F32)
    for n, term in enumerate(split3(value)):
        out = jnp.where(keep & (lane == start + n), term, out)
    return out


def turn_kernel(own_ref, oth_ref, kept_ref, recv_ref, own_out, oth_out, w_out):
    own_out[0] = flat_rows(own_ref).T
    oth_out[0] = flat_rows(oth_ref).T
    sub = kept_ref.shape[2]
    w_out[0, :sub] = kept_ref[0].T
    w_out[0, sub:] = recv_ref[0].T


def weight_kernel(place_ref, own_ref, oth_ref, g_ref, share_ref, out_ref):
    step = pl.program_id(0)
    core = place_ref[0]
    zi = place_ref[1]
    kz = own_ref.shape[1] // HALF
    rows = NY * kz
    for ref, lead in ((own_ref, core), (oth_ref, 1 - core)):
        term = dot(ref[0], g_ref[...], 1, 0).astype(BF)
        for q in range(HALF):
            k = lax.rem(lead * HALF + q - zi + NZ, NZ)
            out_ref[k, pl.ds(pl.multiple_of(step * kz, kz), kz)] = term[q * kz : (q + 1) * kz]

    @pl.when(step == 0)
    def _():
        row = lax.broadcasted_iota(jnp.int32, (STAT, out_ref.shape[2]), 0)
        lane = lax.broadcasted_iota(jnp.int32, (STAT, out_ref.shape[2]), 1)
        tail = in_lanes(share_ref[...], lane, 3 * zi, row == 0).astype(BF)
        for k in range(NZ):
            out_ref[k, rows:] = tail


def far_kernel(place_ref, own_ref, oth_ref, g_ref, share_ref, a_ref, b_ref):
    step = pl.program_id(0)
    core = place_ref[0]
    zi = place_ref[1]
    kz = own_ref.shape[1]
    mine = 1 - zi // HALF == core
    block = jnp.where(mine, own_ref[0].astype(F32), oth_ref[0].astype(F32)).astype(BF)
    term = dot(block, g_ref[...], 1, 0).astype(BF)
    place = pl.ds(pl.multiple_of(lax.rem(step, NY // 2) * kz, kz), kz)

    @pl.when(step < NY // 2)
    def _():
        a_ref[place] = term

    @pl.when(step >= NY // 2)
    def _():
        b_ref[place] = term

    @pl.when(step == 0)
    def _():
        row = lax.broadcasted_iota(jnp.int32, (STAT, b_ref.shape[1]), 0)
        lane = lax.broadcasted_iota(jnp.int32, (STAT, b_ref.shape[1]), 1)
        b_ref[NY // 2 * kz :] = in_lanes(share_ref[...], lane, 3 * zi, row == 0).astype(BF)


def input_kernel(own_ref, oth_ref, w_ref, out_ref):
    sub = own_ref.shape[1]
    term = dot(own_ref[...], w_ref[0, :sub], 1, 0) + dot(oth_ref[...], w_ref[0, sub:], 1, 0)
    out_ref[0] = term.astype(BF)


def on_device(hidden_first, hidden_second, weight):
    core = lax.axis_index("c")
    place = jnp.stack([core, lax.axis_index("z")]).astype(jnp.int32)
    first = core == 0
    rows, kpart = hidden_first.shape
    kz, cols = weight.shape
    total_rows = rows * NX * NZ * 1.0
    full_width = cols * NY * NC * 1.0
    blk = rows * NX
    flat = 2 * blk
    sub = cols // NX
    hshape = (NX, NY, 2, rows, kpart)
    hblock = (NX, 1, 2, rows, kpart)
    smem = pl.BlockSpec(memory_space=SMEM)
    shape = jax.ShapeDtypeStruct

    w_parts = exchange(jnp.stack([weight[:, k * sub : (k + 1) * sub] for k in range(NX)]), "x")
    moved = copies(jnp.stack([hidden_first, hidden_second]), NX * NY)
    moved, w_parts = lax.optimization_barrier((moved, w_parts))
    h_own = exchange(moved, CHIPS).reshape(hshape)
    after, before, (far_a, far_b) = ring_blocks(w_parts)
    h_own, _, _ = lax.optimization_barrier((h_own, after[-1], before[0]))
    h_oth = swap_core(h_own)

    block_spec = at_dim((1, kz, sub), 0)
    w_kept, w_sent, cen, mine, theirs, stats = pl.pallas_call(
        views_kernel,
        grid=(NY,),
        in_specs=[smem, at_dim(hblock, 1), at_dim(hblock, 1)]
        + [block_spec] * 7
        + [
            pl.BlockSpec((1, kz, sub), lambda j: (jnp.minimum(j, NX // 2 - 1), 0, 0)),
            pl.BlockSpec((1, kz, sub), lambda j: (jnp.maximum(j - NX // 2, 0), 0, 0)),
        ],
        out_specs=[
            at_dim((1, kpart, sub), 0),
            at_dim((1, kpart, sub), 0),
            fixed((2, blk, sub)),
            fixed((blk + STAT, sub)),
            fixed((blk + STAT, sub)),
            fixed((8, sub)),
        ],
        out_shape=[
            shape((NY, kpart, sub), BF),
            shape((NY, kpart, sub), BF),
            shape((2, blk, sub), F32),
            shape((blk + STAT, sub), BF),
            shape((blk + STAT, sub), BF),
            shape((8, sub), F32),
        ],
        scratch_shapes=[pltpu.VMEM((NZ, kz, sub), BF), pltpu.VMEM((flat, sub), F32)],
        name="views",
    )(place, h_own, h_oth, w_parts, *after, *before, far_a, far_b)

    local = jnp.concatenate([mine, swap_core(theirs)], axis=1)
    got = ring_pieces(local[: STAT + blk // 2], local[STAT + blk // 2 :])

    w_recv = swap_core(w_sent)
    difference = cen[0] - cen[1] + (stats[0] - stats[1])[None, :]
    diff_share = (25.0 * jnp.sum(difference * difference) / (total_rows * full_width)).reshape(1, 1)

    wide = NZ * blk + 128
    flat_got = [piece for pair in got for piece in pair]
    whole = lambda s: pl.BlockSpec(s, lambda: (0,) * len(s))
    gathered, gram_part, view_stats = pl.pallas_call(
        functools.partial(gram_kernel, 1.0 / (full_width * NZ)),
        in_specs=[whole((1, 1))] + [whole(piece.shape) for piece in flat_got],
        out_specs=[whole((NZ * blk, 2 * sub)), whole((blk, wide)), whole((8, 2 * sub))],
        out_shape=[
            shape((NZ * blk, 2 * sub), BF),
            shape((blk, wide), BF),
            shape((8, 2 * sub), F32),
        ],
        name="gram",
    )(diff_share, *flat_got)

    stats_own = view_stats[:, :sub]
    stats_back = swap_core(view_stats[:, sub:])
    both_stats = jnp.stack(
        [jnp.where(first, stats_own, stats_back), jnp.where(first, stats_back, stats_own)]
    )
    variance = both_stats[:, 0]
    centered = cen + both_stats[:, 1][:, None, :]
    deviation = jnp.sqrt(variance + 0.0001)

    pieces = exchange(gram_part.reshape(NX * NY, blk // (NX * NY), wide), CHIPS)
    turned = (NY, kpart, flat)
    h_own, h_oth, w_turned = pl.pallas_call(
        turn_kernel,
        grid=(NY,),
        in_specs=[at_dim(hblock, 1), at_dim(hblock, 1)] + [at_dim((1, kpart, sub), 0)] * 2,
        out_specs=[at_dim((1, kpart, flat), 0)] * 2 + [at_dim((1, 2 * sub, kpart), 0)],
        out_shape=[shape(turned, BF), shape(turned, BF), shape((NY, 2 * sub, kpart), BF)],
        name="turn",
    )(h_own, h_oth, w_kept, w_recv)
    gram_rows = jnp.sum(pieces[:, :, : NZ * blk].astype(F32), axis=0).astype(BF)
    share = jnp.sum(pieces[:, :, NZ * blk :].astype(F32))
    gram_rows, share, variance, h_own, h_oth, w_turned = lax.optimization_barrier(
        (gram_rows, share, variance, h_own, h_oth, w_turned)
    )
    gram_half = exchange(copies(gram_rows, NX * NY), CHIPS).reshape(blk, NZ * blk)
    squares = gram_half.astype(F32)
    share = (share + jnp.sum(squares * squares) / ((total_rows - 1.0) ** 2 * full_width)).reshape(1, 1)
    spread_view = dot(gram_half, gathered, 1, 0)
    spread_own = spread_view[:, :sub]
    spread_back = swap_core(spread_view[:, sub:])
    spread = jnp.stack(
        [jnp.where(first, spread_own, spread_back), jnp.where(first, spread_back, spread_own)]
    )

    inv_grad = 50.0 / 256.0 * jnp.stack([difference, -difference])
    binding = (deviation < 1.0).astype(F32)
    hinge_grad = (
        -(25.0 * total_rows / (256.0 * (total_rows - 1.0)))
        * (binding / deviation)[:, None, :]
        * centered
    )
    cov_grad = (
        4.0
        * total_rows
        / 256.0
        * (spread / (total_rows - 1.0) ** 2 - variance[:, None, :] * centered / (total_rows - 1.0))
    )
    grad_views = (inv_grad + hinge_grad + cov_grad).astype(BF)
    grads = grad_views.reshape(2, NX, rows, sub).transpose(1, 0, 2, 3).reshape(flat, sub)

    far_block = pl.BlockSpec((1, kz, flat), lambda j, place: (j, lax.rem(place[1], HALF), 0))
    held = lambda s: pl.BlockSpec(s, lambda j, place: (0,) * len(s))
    half = NX // 2 * kz
    far_right, far_left = pl.pallas_call(
        far_kernel,
        grid_spec=pltpu.PrefetchScalarGridSpec(
            num_scalar_prefetch=1,
            grid=(NY,),
            in_specs=[far_block, far_block, held((flat, sub)), held((1, 1))],
            out_specs=[held((half, sub)), held((half + STAT, sub))],
        ),
        out_shape=[shape((half, sub), BF), shape((half + STAT, sub), BF)],
        name="far_terms",
    )(place, h_own, h_oth, grads, share)
    right = hop(far_right, 1)
    left = hop(far_left, -1)

    later, _, _ = lax.optimization_barrier((grads, far_right, far_left))
    input_part = pl.pallas_call(
        input_kernel,
        grid=(NY,),
        in_specs=[fixed((flat, sub)), fixed((flat, sub)), at_dim((1, 2 * sub, kpart), 0)],
        out_specs=at_dim((1, flat, kpart), 0),
        out_shape=shape((NY, flat, kpart), BF),
        name="input_terms",
    )(later, swap_core(grads), w_turned)
    input_parts = exchange(input_part.reshape(NX * NY, 2, rows, kpart), ("y", "x"))

    later, _ = lax.optimization_barrier((later, input_part))
    terms = NX * kz + STAT
    weight_part = pl.pallas_call(
        weight_kernel,
        grid=(NY,),
        in_specs=[smem] + [at_dim((1, kpart, flat), 0)] * 2 + [fixed((flat, sub)), fixed((1, 1))],
        out_specs=fixed((NZ, terms, sub)),
        out_shape=shape((NZ, terms, sub), BF),
        name="weight_terms",
    )(place, h_own, h_oth, later, share)

    weight_sum = ring_sum(weight_part, right, left)
    loss_rows = weight_sum[NX * kz :]
    weight_sum = weight_sum[: NX * kz].astype(BF).reshape(NX, kz, sub)
    weight_sum, loss_rows, input_parts = lax.optimization_barrier((weight_sum, loss_rows, input_parts))
    loss_part = jnp.sum(loss_rows).reshape(1, 1)
    blocks = exchange(weight_sum, "x")
    input_grads = jnp.sum(input_parts.astype(F32), axis=0).astype(BF)
    grad_weight = jnp.concatenate([blocks[k] for k in range(NX)], axis=1)
    total_loss = (loss_part + swap_core(loss_part))[0, 0]
    return (total_loss, grad_weight, input_grads[0], input_grads[1])


def solution(mesh):
    grid = Mesh(mesh.devices.reshape(NX, NZ, NY, NC), ("x", "z", "y", "c"))
    placed = P(("x", "z"), ("y", "c"))

    return jax.shard_map(
        on_device,
        mesh=grid,
        in_specs=(placed, placed, placed),
        out_specs=(P(), placed, placed, placed),
        check_vma=False,
    )
```

```python
import functools

import jax
import jax.numpy as jnp
from jax import lax
from jax.experimental import pallas as pl
from jax.experimental.pallas import tpu as pltpu
from jax.sharding import Mesh, PartitionSpec as P


BF = jnp.bfloat16
F32 = jnp.float32
NX, NZ, NY, NC = 4, 8, 4, 2
HALF = NZ // 2
CHIPS = ("x", "y")
SMEM = pltpu.SMEM
STAT = 16


def swap_core(v):
    return lax.ppermute(v, "c", [(0, 1), (1, 0)])


def hop(v, k):
    return lax.ppermute(v, "z", [(i, (i + k) % NZ) for i in range(NZ)])


def exchange(v, axes):
    return lax.all_to_all(v, axes, split_axis=0, concat_axis=0, tiled=True)


def copies(v, n):
    return jnp.broadcast_to(v[None], (n,) + v.shape)


def ring_blocks(v):
    right, left = [v], [v]
    for _ in range(1, HALF):
        right.append(hop(right[-1], 1))
        left.append(hop(left[-1], -1))
    half = v.shape[0] // 2
    far = (hop(right[-1][:half], 1), hop(left[-1][half:], -1))
    return left[1:], right[:0:-1], far


def ring_pieces(first, second):
    got = [[None, None] for _ in range(NZ)]
    got[0] = [first, second]
    for k in range(1, HALF + 1):
        for p in (0, 1):
            if k < HALF or p == 0:
                got[-k % NZ][p] = hop(got[(1 - k) % NZ][p], 1)
            if k < HALF or p == 1:
                got[k][p] = hop(got[k - 1][p], -1)
    return got


def ring_sum(terms, right, left):
    for d in range(HALF - 1, 0, -1):
        right, left = lax.optimization_barrier((right, left))
        right, left = right.astype(F32), left.astype(F32)
        if d == HALF - 1:
            low, high = jnp.zeros(left.shape, F32), jnp.zeros(right.shape, F32)
            right = jnp.concatenate([right, low], axis=0)
            left = jnp.concatenate([high, left], axis=0)
        right = hop((terms[d].astype(F32) + right).astype(BF), 1)
        left = hop((terms[NZ - d].astype(F32) + left).astype(BF), -1)
    return terms[0].astype(F32) + right.astype(F32) + left.astype(F32)


def split3(v):
    hi = v.astype(BF).astype(F32)
    mid = (v - hi).astype(BF).astype(F32)
    return [hi, mid, v - hi - mid]


def dot(a, b, ca, cb):
    return lax.dot_general(a, b, (((ca,), (cb,)), ((), ())), preferred_element_type=F32)


def fixed(shape):
    return pl.BlockSpec(shape, lambda j: (0,) * len(shape))


def at_dim(shape, dim):
    return pl.BlockSpec(shape, lambda j: tuple(j if d == dim else 0 for d in range(len(shape))))


def flat_rows(ref, y=0):
    nx, _, nv, rows, width = ref.shape
    return ref[:, y].reshape(nx * nv * rows, width)


def views_kernel(place_ref, own_ref, oth_ref, *refs):
    w_refs, refs = refs[:7], refs[7:]
    far_a, far_b, kept_ref, sent_ref, cen_ref, mine_ref, theirs_ref, stat_ref, w_ref, acc = refs
    step = pl.program_id(0)
    core = place_ref[0]
    zi = place_ref[1]
    nx, _, nv, rows, kpart = own_ref.shape
    sub = acc.shape[1]
    for k, ref in zip((0, 1, 2, 3, 5, 6, 7), w_refs):
        w_ref[lax.rem(zi + k, NZ)] = ref[0]
    w_ref[lax.rem(zi + HALF, NZ)] = jnp.where(step < NY // 2, far_a[0], far_b[0])
    w_own = w_ref[pl.ds(core * HALF, HALF)].reshape(kpart, sub)
    w_oth = w_ref[pl.ds((1 - core) * HALF, HALF)].reshape(kpart, sub)
    kept_ref[0] = w_own
    sent_ref[0] = w_oth
    term = dot(flat_rows(own_ref), w_own, 1, 0) + dot(flat_rows(oth_ref), w_oth, 1, 0)

    @pl.when(step == 0)
    def _():
        acc[...] = term

    @pl.when(step > 0)
    def _():
        acc[...] += term

    @pl.when(step == pl.num_programs(0) - 1)
    def _():
        means, tails = [], []
        for v in range(nv):
            blocks = [acc[(a * nv + v) * rows : (a * nv + v + 1) * rows] for a in range(nx)]
            mean = sum(jnp.sum(block, axis=0, keepdims=True) for block in blocks) / (nx * rows * 1.0)
            means.append(mean)
            total = jnp.zeros_like(mean)
            for a in range(nx):
                block = blocks[a] - mean
                cen_ref[v, a * rows : (a + 1) * rows] = block
                total = total + jnp.sum(block * block, axis=0, keepdims=True)
            pad = jnp.zeros((STAT - 6, sub), F32)
            tails.append(jnp.concatenate(split3(mean) + split3(total) + [pad], axis=0).astype(BF))
        stat_ref[...] = jnp.concatenate(means + [jnp.zeros((6, sub), F32)], axis=0)
        data = [cen_ref[v].astype(BF) for v in range(nv)]
        for ref, same in ((mine_ref, core == 0), (theirs_ref, core == 1)):
            ref[:STAT] = jnp.where(same, tails[0], tails[1])
            ref[STAT:] = jnp.where(same, data[0], data[1])


def gram_kernel(scale_each, diff_ref, *refs):
    pieces, (all_ref, gram_ref, stat_ref) = refs[: 2 * NZ], refs[2 * NZ :]
    top = pieces[0].shape[0] - STAT
    blk = top + pieces[1].shape[0]
    stats = [pieces[2 * k][:STAT].astype(F32) for k in range(NZ)]
    means = [s[0:1] + s[1:2] + s[2:3] for s in stats]
    center = sum(means) / (NZ * 1.0)
    total = sum(s[3:4] + s[4:5] + s[5:6] for s in stats)
    for k in range(NZ):
        move = means[k] - center
        total = total + blk * (move * move)
        all_ref[k * blk : k * blk + top] = (pieces[2 * k][STAT:].astype(F32) + move).astype(BF)
        all_ref[k * blk + top : (k + 1) * blk] = (pieces[2 * k + 1][...].astype(F32) + move).astype(BF)
        gram_ref[:, k * blk : (k + 1) * blk] = dot(
            all_ref[:blk], all_ref[k * blk : (k + 1) * blk], 1, 1
        ).astype(BF)
    variance = total / (NZ * blk - 1.0)
    pad = jnp.zeros((6, total.shape[1]), F32)
    stat_ref[...] = jnp.concatenate([variance, means[0] - center, pad], axis=0)
    hinge = jnp.maximum(1.0 - jnp.sqrt(variance + 0.0001), 0.0)
    share = diff_ref[...] + scale_each * jnp.sum(25.0 * hinge - variance * variance, axis=1, keepdims=True)
    extra = gram_ref.shape[1] - NZ * blk
    row = lax.broadcasted_iota(jnp.int32, (blk, extra), 0)
    lane = lax.broadcasted_iota(jnp.int32, (blk, extra), 1)
    lead = lax.rem(row, blk // (NX * NY)) == 0
    gram_ref[:, NZ * blk :] = in_lanes(share, lane, 0, lead).astype(BF)


def in_lanes(value, lane, start, keep):
    out = jnp.zeros(lane.shape, F32)
    for n, term in enumerate(split3(value)):
        out = jnp.where(keep & (lane == start + n), term, out)
    return out


def turn_kernel(own_ref, oth_ref, kept_ref, recv_ref, own_out, oth_out, w_out):
    own_out[0] = flat_rows(own_ref).T
    oth_out[0] = flat_rows(oth_ref).T
    sub = kept_ref.shape[2]
    w_out[0, :sub] = kept_ref[0].T
    w_out[0, sub:] = recv_ref[0].T


def weight_kernel(place_ref, own_ref, oth_ref, g_ref, share_ref, out_ref):
    step = pl.program_id(0)
    core = place_ref[0]
    zi = place_ref[1]
    kz = own_ref.shape[1] // HALF
    rows = NY * kz
    for ref, lead in ((own_ref, core), (oth_ref, 1 - core)):
        term = dot(ref[0], g_ref[...], 1, 0).astype(BF)
        place = pl.ds(pl.multiple_of(step * kz, kz), kz)
        for q in range(HALF):
            out_ref[lax.rem(lead * HALF + q - zi + NZ, NZ), place] = term[q * kz : (q + 1) * kz]

    @pl.when(step == 0)
    def _():
        row = lax.broadcasted_iota(jnp.int32, (STAT, out_ref.shape[2]), 0)
        lane = lax.broadcasted_iota(jnp.int32, (STAT, out_ref.shape[2]), 1)
        tail = in_lanes(share_ref[...], lane, 3 * zi, row == 0).astype(BF)
        for k in range(NZ):
            out_ref[k, rows:] = tail


def far_kernel(place_ref, own_ref, oth_ref, g_ref, share_ref, a_ref, b_ref):
    core = place_ref[0]
    zi = place_ref[1]
    kz = own_ref.shape[1]
    mine = 1 - zi // HALF == core
    block = jnp.where(mine, own_ref[...].astype(F32), oth_ref[...].astype(F32)).astype(BF)
    term = dot(block.reshape(NY * kz, own_ref.shape[2]), g_ref[...], 1, 0).astype(BF)
    a_ref[...] = term[: NY // 2 * kz]
    b_ref[: NY // 2 * kz] = term[NY // 2 * kz :]
    row = lax.broadcasted_iota(jnp.int32, (STAT, b_ref.shape[1]), 0)
    lane = lax.broadcasted_iota(jnp.int32, (STAT, b_ref.shape[1]), 1)
    b_ref[NY // 2 * kz :] = in_lanes(share_ref[...], lane, 3 * zi, row == 0).astype(BF)


def input_kernel(own_ref, oth_ref, w_ref, out_ref):
    sub = own_ref.shape[1]
    term = dot(own_ref[...], w_ref[0, :sub], 1, 0) + dot(oth_ref[...], w_ref[0, sub:], 1, 0)
    out_ref[0] = term.astype(BF)


def on_device(hidden_first, hidden_second, weight):
    core = lax.axis_index("c")
    place = jnp.stack([core, lax.axis_index("z")]).astype(jnp.int32)
    first = core == 0
    rows, kpart = hidden_first.shape
    kz, cols = weight.shape
    total_rows = rows * NX * NZ * 1.0
    full_width = cols * NY * NC * 1.0
    blk = rows * NX
    flat = 2 * blk
    sub = cols // NX
    hshape = (NX, NY, 2, rows, kpart)
    hblock = (NX, 1, 2, rows, kpart)
    smem = pl.BlockSpec(memory_space=SMEM)
    shape = jax.ShapeDtypeStruct

    w_parts = exchange(jnp.stack([weight[:, k * sub : (k + 1) * sub] for k in range(NX)]), "x")
    moved = copies(jnp.stack([hidden_first, hidden_second]), NX * NY)
    moved, w_parts = lax.optimization_barrier((moved, w_parts))
    h_own = exchange(moved, CHIPS).reshape(hshape)
    after, before, (far_a, far_b) = ring_blocks(w_parts)
    h_own, _, _ = lax.optimization_barrier((h_own, after[-1], before[0]))
    h_oth = swap_core(h_own)

    block_spec = at_dim((1, kz, sub), 0)
    w_kept, w_sent, cen, mine, theirs, stats = pl.pallas_call(
        views_kernel,
        grid=(NY,),
        in_specs=[smem, at_dim(hblock, 1), at_dim(hblock, 1)]
        + [block_spec] * 7
        + [
            pl.BlockSpec((1, kz, sub), lambda j: (jnp.minimum(j, NX // 2 - 1), 0, 0)),
            pl.BlockSpec((1, kz, sub), lambda j: (jnp.maximum(j - NX // 2, 0), 0, 0)),
        ],
        out_specs=[
            at_dim((1, kpart, sub), 0),
            at_dim((1, kpart, sub), 0),
            fixed((2, blk, sub)),
            fixed((blk + STAT, sub)),
            fixed((blk + STAT, sub)),
            fixed((8, sub)),
        ],
        out_shape=[
            shape((NY, kpart, sub), BF),
            shape((NY, kpart, sub), BF),
            shape((2, blk, sub), F32),
            shape((blk + STAT, sub), BF),
            shape((blk + STAT, sub), BF),
            shape((8, sub), F32),
        ],
        scratch_shapes=[pltpu.VMEM((NZ, kz, sub), BF), pltpu.VMEM((flat, sub), F32)],
        name="views",
    )(place, h_own, h_oth, w_parts, *after, *before, far_a, far_b)

    local = jnp.concatenate([mine, swap_core(theirs)], axis=1)
    got = ring_pieces(local[: STAT + blk // 2], local[STAT + blk // 2 :])

    w_recv = swap_core(w_sent)
    difference = cen[0] - cen[1] + (stats[0] - stats[1])[None, :]
    diff_share = (25.0 * jnp.sum(difference * difference) / (total_rows * full_width)).reshape(1, 1)

    wide = NZ * blk + 128
    flat_got = [piece for pair in got for piece in pair]
    whole = lambda s: pl.BlockSpec(s, lambda: (0,) * len(s))
    gathered, gram_part, view_stats = pl.pallas_call(
        functools.partial(gram_kernel, 1.0 / (full_width * NZ)),
        in_specs=[whole((1, 1))] + [whole(piece.shape) for piece in flat_got],
        out_specs=[whole((NZ * blk, 2 * sub)), whole((blk, wide)), whole((8, 2 * sub))],
        out_shape=[
            shape((NZ * blk, 2 * sub), BF),
            shape((blk, wide), BF),
            shape((8, 2 * sub), F32),
        ],
        name="gram",
    )(diff_share, *flat_got)

    stats_own = view_stats[:, :sub]
    stats_back = swap_core(view_stats[:, sub:])
    both_stats = jnp.stack(
        [jnp.where(first, stats_own, stats_back), jnp.where(first, stats_back, stats_own)]
    )
    variance = both_stats[:, 0]
    centered = cen + both_stats[:, 1][:, None, :]
    deviation = jnp.sqrt(variance + 0.0001)

    pieces = exchange(gram_part.reshape(NX * NY, blk // (NX * NY), wide), CHIPS)
    turned = (NY, kpart, flat)
    h_own, h_oth, w_turned = pl.pallas_call(
        turn_kernel,
        grid=(NY,),
        in_specs=[at_dim(hblock, 1), at_dim(hblock, 1)] + [at_dim((1, kpart, sub), 0)] * 2,
        out_specs=[at_dim((1, kpart, flat), 0)] * 2 + [at_dim((1, 2 * sub, kpart), 0)],
        out_shape=[shape(turned, BF), shape(turned, BF), shape((NY, 2 * sub, kpart), BF)],
        name="turn",
    )(h_own, h_oth, w_kept, w_recv)
    gram_rows = jnp.sum(pieces[:, :, : NZ * blk].astype(F32), axis=0).astype(BF)
    share = jnp.sum(pieces[:, :, NZ * blk :].astype(F32))
    gram_rows, share, variance, h_own, h_oth, w_turned = lax.optimization_barrier(
        (gram_rows, share, variance, h_own, h_oth, w_turned)
    )
    gram_half = exchange(copies(gram_rows, NX * NY), CHIPS).reshape(blk, NZ * blk)
    squares = gram_half.astype(F32)
    share = (share + jnp.sum(squares * squares) / ((total_rows - 1.0) ** 2 * full_width)).reshape(1, 1)
    spread_view = dot(gram_half, gathered, 1, 0)
    spread_own = spread_view[:, :sub]
    spread_back = swap_core(spread_view[:, sub:])
    spread = jnp.stack(
        [jnp.where(first, spread_own, spread_back), jnp.where(first, spread_back, spread_own)]
    )

    inv_grad = 50.0 / 256.0 * jnp.stack([difference, -difference])
    binding = (deviation < 1.0).astype(F32)
    hinge_grad = (
        -(25.0 * total_rows / (256.0 * (total_rows - 1.0)))
        * (binding / deviation)[:, None, :]
        * centered
    )
    cov_grad = (
        4.0
        * total_rows
        / 256.0
        * (spread / (total_rows - 1.0) ** 2 - variance[:, None, :] * centered / (total_rows - 1.0))
    )
    grad_views = (inv_grad + hinge_grad + cov_grad).astype(BF)
    grads = grad_views.reshape(2, NX, rows, sub).transpose(1, 0, 2, 3).reshape(flat, sub)

    far_block = pl.BlockSpec((NY, kz, flat), lambda j, place: (0, lax.rem(place[1], HALF), 0))
    held = lambda s: pl.BlockSpec(s, lambda j, place: (0,) * len(s))
    half = NX // 2 * kz
    far_right, far_left = pl.pallas_call(
        far_kernel,
        grid_spec=pltpu.PrefetchScalarGridSpec(
            num_scalar_prefetch=1,
            grid=(1,),
            in_specs=[far_block, far_block, held((flat, sub)), held((1, 1))],
            out_specs=[held((half, sub)), held((half + STAT, sub))],
        ),
        out_shape=[shape((half, sub), BF), shape((half + STAT, sub), BF)],
        name="far_terms",
    )(place, h_own, h_oth, grads, share)
    right = hop(far_right, 1)
    left = hop(far_left, -1)

    later, _, _ = lax.optimization_barrier((grads, far_right, far_left))
    input_part = pl.pallas_call(
        input_kernel,
        grid=(NY,),
        in_specs=[fixed((flat, sub)), fixed((flat, sub)), at_dim((1, 2 * sub, kpart), 0)],
        out_specs=at_dim((1, flat, kpart), 0),
        out_shape=shape((NY, flat, kpart), BF),
        name="input_terms",
    )(later, swap_core(grads), w_turned)
    input_parts = exchange(input_part.reshape(NX * NY, 2, rows, kpart), ("y", "x"))

    later, _ = lax.optimization_barrier((later, input_part))
    terms = NX * kz + STAT
    weight_part = pl.pallas_call(
        weight_kernel,
        grid=(NY,),
        in_specs=[smem] + [at_dim((1, kpart, flat), 0)] * 2 + [fixed((flat, sub)), fixed((1, 1))],
        out_specs=fixed((NZ, terms, sub)),
        out_shape=shape((NZ, terms, sub), BF),
        name="weight_terms",
    )(place, h_own, h_oth, later, share)

    weight_sum = ring_sum(weight_part, right, left)
    loss_rows = weight_sum[NX * kz :]
    weight_sum = weight_sum[: NX * kz].astype(BF).reshape(NX, kz, sub)
    weight_sum, loss_rows, input_parts = lax.optimization_barrier((weight_sum, loss_rows, input_parts))
    loss_part = jnp.sum(loss_rows).reshape(1, 1)
    blocks = exchange(weight_sum, "x")
    input_grads = jnp.sum(input_parts.astype(F32), axis=0).astype(BF)
    grad_weight = jnp.concatenate([blocks[k] for k in range(NX)], axis=1)
    total_loss = (loss_part + swap_core(loss_part))[0, 0]
    return (total_loss, grad_weight, input_grads[0], input_grads[1])


def solution(mesh):
    grid = Mesh(mesh.devices.reshape(NX, NZ, NY, NC), ("x", "z", "y", "c"))
    placed = P(("x", "z"), ("y", "c"))

    return jax.shard_map(
        on_device,
        mesh=grid,
        in_specs=(placed, placed, placed),
        out_specs=(P(), placed, placed, placed),
        check_vma=False,
    )
```

```python
import functools

import jax
import jax.numpy as jnp
from jax import lax
from jax.experimental import pallas as pl
from jax.experimental.pallas import tpu as pltpu
from jax.sharding import Mesh, PartitionSpec as P


BF = jnp.bfloat16
F32 = jnp.float32
NX, NZ, NY, NC = 4, 8, 4, 2
HALF = NZ // 2
CHIPS = ("x", "y")
SMEM = pltpu.SMEM
STAT = 16


def swap_core(v):
    return lax.ppermute(v, "c", [(0, 1), (1, 0)])


def hop(v, k):
    return lax.ppermute(v, "z", [(i, (i + k) % NZ) for i in range(NZ)])


def exchange(v, axes):
    return lax.all_to_all(v, axes, split_axis=0, concat_axis=0, tiled=True)


def copies(v, n):
    return jnp.broadcast_to(v[None], (n,) + v.shape)


def ring_blocks(v):
    right, left = [v], [v]
    for _ in range(1, HALF):
        right.append(hop(right[-1], 1))
        left.append(hop(left[-1], -1))
    half = v.shape[0] // 2
    far = (hop(right[-1][:half], 1), hop(left[-1][half:], -1))
    return left[1:], right[:0:-1], far


def ring_pieces(first, second):
    got = [[None, None] for _ in range(NZ)]
    got[0] = [first, second]
    for k in range(1, HALF + 1):
        for p in (0, 1):
            if k < HALF or p == 0:
                got[-k % NZ][p] = hop(got[(1 - k) % NZ][p], 1)
            if k < HALF or p == 1:
                got[k][p] = hop(got[k - 1][p], -1)
    return got


def ring_sum(terms, right, left):
    for d in range(HALF - 1, 0, -1):
        right, left = lax.optimization_barrier((right, left))
        right, left = right.astype(F32), left.astype(F32)
        if d == HALF - 1:
            low, high = jnp.zeros(left.shape, F32), jnp.zeros(right.shape, F32)
            right = jnp.concatenate([right, low], axis=0)
            left = jnp.concatenate([high, left], axis=0)
        right = hop((terms[d].astype(F32) + right).astype(BF), 1)
        left = hop((terms[NZ - d].astype(F32) + left).astype(BF), -1)
    return terms[0], right, left


def split3(v):
    hi = v.astype(BF).astype(F32)
    mid = (v - hi).astype(BF).astype(F32)
    return [hi, mid, v - hi - mid]


def dot(a, b, ca, cb):
    return lax.dot_general(a, b, (((ca,), (cb,)), ((), ())), preferred_element_type=F32)


def fixed(shape):
    return pl.BlockSpec(shape, lambda j: (0,) * len(shape))


def at_dim(shape, dim):
    return pl.BlockSpec(shape, lambda j: tuple(j if d == dim else 0 for d in range(len(shape))))


def flat_rows(ref, y=0):
    nx, _, nv, rows, width = ref.shape
    return ref[:, y].reshape(nx * nv * rows, width)


def views_kernel(place_ref, own_ref, oth_ref, *refs):
    w_refs, refs = refs[:7], refs[7:]
    far_a, far_b, kept_ref, sent_ref, cen_ref, mine_ref, theirs_ref, stat_ref, w_ref, acc = refs
    step = pl.program_id(0)
    core = place_ref[0]
    zi = place_ref[1]
    nx, _, nv, rows, kpart = own_ref.shape
    sub = acc.shape[1]
    for k, ref in zip((0, 1, 2, 3, 5, 6, 7), w_refs):
        w_ref[lax.rem(zi + k, NZ)] = ref[0]
    w_ref[lax.rem(zi + HALF, NZ)] = jnp.where(step < NY // 2, far_a[0], far_b[0])
    w_own = w_ref[pl.ds(core * HALF, HALF)].reshape(kpart, sub)
    w_oth = w_ref[pl.ds((1 - core) * HALF, HALF)].reshape(kpart, sub)
    kept_ref[0] = w_own
    sent_ref[0] = w_oth
    term = dot(flat_rows(own_ref), w_own, 1, 0) + dot(flat_rows(oth_ref), w_oth, 1, 0)

    @pl.when(step == 0)
    def _():
        acc[...] = term

    @pl.when(step > 0)
    def _():
        acc[...] += term

    @pl.when(step == pl.num_programs(0) - 1)
    def _():
        means, tails = [], []
        for v in range(nv):
            blocks = [acc[(a * nv + v) * rows : (a * nv + v + 1) * rows] for a in range(nx)]
            mean = sum(jnp.sum(block, axis=0, keepdims=True) for block in blocks) / (nx * rows * 1.0)
            means.append(mean)
            total = jnp.zeros_like(mean)
            for a in range(nx):
                block = blocks[a] - mean
                cen_ref[v, a * rows : (a + 1) * rows] = block
                total = total + jnp.sum(block * block, axis=0, keepdims=True)
            pad = jnp.zeros((STAT - 6, sub), F32)
            tails.append(jnp.concatenate(split3(mean) + split3(total) + [pad], axis=0).astype(BF))
        stat_ref[...] = jnp.concatenate(means + [jnp.zeros((6, sub), F32)], axis=0)
        data = [cen_ref[v].astype(BF) for v in range(nv)]
        for ref, same in ((mine_ref, core == 0), (theirs_ref, core == 1)):
            ref[:STAT] = jnp.where(same, tails[0], tails[1])
            ref[STAT:] = jnp.where(same, data[0], data[1])


def gram_kernel(scale_each, diff_ref, *refs):
    pieces, (all_ref, gram_ref, stat_ref) = refs[: 2 * NZ], refs[2 * NZ :]
    top = pieces[0].shape[0] - STAT
    blk = top + pieces[1].shape[0]
    stats = [pieces[2 * k][:STAT].astype(F32) for k in range(NZ)]
    means = [s[0:1] + s[1:2] + s[2:3] for s in stats]
    center = sum(means) / (NZ * 1.0)
    total = sum(s[3:4] + s[4:5] + s[5:6] for s in stats)
    for k in range(NZ):
        move = means[k] - center
        total = total + blk * (move * move)
        all_ref[k * blk : k * blk + top] = (pieces[2 * k][STAT:].astype(F32) + move).astype(BF)
        all_ref[k * blk + top : (k + 1) * blk] = (pieces[2 * k + 1][...].astype(F32) + move).astype(BF)
        gram_ref[:, k * blk : (k + 1) * blk] = dot(
            all_ref[:blk], all_ref[k * blk : (k + 1) * blk], 1, 1
        ).astype(BF)
    variance = total / (NZ * blk - 1.0)
    pad = jnp.zeros((6, total.shape[1]), F32)
    stat_ref[...] = jnp.concatenate([variance, means[0] - center, pad], axis=0)
    hinge = jnp.maximum(1.0 - jnp.sqrt(variance + 0.0001), 0.0)
    share = diff_ref[...] + scale_each * jnp.sum(25.0 * hinge - variance * variance, axis=1, keepdims=True)
    extra = gram_ref.shape[1] - NZ * blk
    row = lax.broadcasted_iota(jnp.int32, (blk, extra), 0)
    lane = lax.broadcasted_iota(jnp.int32, (blk, extra), 1)
    lead = lax.rem(row, blk // (NX * NY)) == 0
    gram_ref[:, NZ * blk :] = in_lanes(share, lane, 0, lead).astype(BF)


def in_lanes(value, lane, start, keep):
    out = jnp.zeros(lane.shape, F32)
    for n, term in enumerate(split3(value)):
        out = jnp.where(keep & (lane == start + n), term, out)
    return out


def turn_kernel(own_ref, oth_ref, kept_ref, recv_ref, own_out, oth_out, w_out):
    own_out[0] = flat_rows(own_ref).T
    oth_out[0] = flat_rows(oth_ref).T
    sub = kept_ref.shape[2]
    w_out[0, :sub] = kept_ref[0].T
    w_out[0, sub:] = recv_ref[0].T


def weight_kernel(place_ref, own_ref, oth_ref, g_ref, share_ref, out_ref):
    step = pl.program_id(0)
    core = place_ref[0]
    zi = place_ref[1]
    kz = own_ref.shape[1] // HALF
    rows = NY * kz
    for ref, lead in ((own_ref, core), (oth_ref, 1 - core)):
        term = dot(ref[0], g_ref[...], 1, 0).astype(BF)
        place = pl.ds(pl.multiple_of(step * kz, kz), kz)
        for q in range(HALF):
            out_ref[lax.rem(lead * HALF + q - zi + NZ, NZ), place] = term[q * kz : (q + 1) * kz]

    @pl.when(step == 0)
    def _():
        row = lax.broadcasted_iota(jnp.int32, (STAT, out_ref.shape[2]), 0)
        lane = lax.broadcasted_iota(jnp.int32, (STAT, out_ref.shape[2]), 1)
        tail = in_lanes(share_ref[...], lane, 3 * zi, row == 0).astype(BF)
        for k in range(NZ):
            out_ref[k, rows:] = tail


def far_kernel(place_ref, own_ref, oth_ref, g_ref, share_ref, a_ref, b_ref):
    core = place_ref[0]
    zi = place_ref[1]
    kz = own_ref.shape[1]
    mine = 1 - zi // HALF == core
    block = jnp.where(mine, own_ref[...].astype(F32), oth_ref[...].astype(F32)).astype(BF)
    term = dot(block.reshape(NY * kz, own_ref.shape[2]), g_ref[...], 1, 0).astype(BF)
    a_ref[...] = term[: NY // 2 * kz]
    b_ref[: NY // 2 * kz] = term[NY // 2 * kz :]
    row = lax.broadcasted_iota(jnp.int32, (STAT, b_ref.shape[1]), 0)
    lane = lax.broadcasted_iota(jnp.int32, (STAT, b_ref.shape[1]), 1)
    b_ref[NY // 2 * kz :] = in_lanes(share_ref[...], lane, 3 * zi, row == 0).astype(BF)


def input_kernel(own_ref, oth_ref, w_ref, out_ref):
    sub = own_ref.shape[1]
    term = dot(own_ref[...], w_ref[0, :sub], 1, 0) + dot(oth_ref[...], w_ref[0, sub:], 1, 0)
    out_ref[0] = term.astype(BF)


def on_device(hidden_first, hidden_second, weight):
    core = lax.axis_index("c")
    place = jnp.stack([core, lax.axis_index("z")]).astype(jnp.int32)
    first = core == 0
    rows, kpart = hidden_first.shape
    kz, cols = weight.shape
    total_rows = rows * NX * NZ * 1.0
    full_width = cols * NY * NC * 1.0
    blk = rows * NX
    flat = 2 * blk
    sub = cols // NX
    hshape = (NX, NY, 2, rows, kpart)
    hblock = (NX, 1, 2, rows, kpart)
    smem = pl.BlockSpec(memory_space=SMEM)
    shape = jax.ShapeDtypeStruct

    w_parts = exchange(jnp.stack([weight[:, k * sub : (k + 1) * sub] for k in range(NX)]), "x")
    moved = copies(jnp.stack([hidden_first, hidden_second]), NX * NY)
    moved, w_parts = lax.optimization_barrier((moved, w_parts))
    h_own = exchange(moved, CHIPS).reshape(hshape)
    after, before, (far_a, far_b) = ring_blocks(w_parts)
    h_own, _, _ = lax.optimization_barrier((h_own, after[-1], before[0]))
    h_oth = swap_core(h_own)

    block_spec = at_dim((1, kz, sub), 0)
    w_kept, w_sent, cen, mine, theirs, stats = pl.pallas_call(
        views_kernel,
        grid=(NY,),
        in_specs=[smem, at_dim(hblock, 1), at_dim(hblock, 1)]
        + [block_spec] * 7
        + [
            pl.BlockSpec((1, kz, sub), lambda j: (jnp.minimum(j, NX // 2 - 1), 0, 0)),
            pl.BlockSpec((1, kz, sub), lambda j: (jnp.maximum(j - NX // 2, 0), 0, 0)),
        ],
        out_specs=[
            at_dim((1, kpart, sub), 0),
            at_dim((1, kpart, sub), 0),
            fixed((2, blk, sub)),
            fixed((blk + STAT, sub)),
            fixed((blk + STAT, sub)),
            fixed((8, sub)),
        ],
        out_shape=[
            shape((NY, kpart, sub), BF),
            shape((NY, kpart, sub), BF),
            shape((2, blk, sub), F32),
            shape((blk + STAT, sub), BF),
            shape((blk + STAT, sub), BF),
            shape((8, sub), F32),
        ],
        scratch_shapes=[pltpu.VMEM((NZ, kz, sub), BF), pltpu.VMEM((flat, sub), F32)],
        name="views",
    )(place, h_own, h_oth, w_parts, *after, *before, far_a, far_b)

    local = jnp.concatenate([mine, swap_core(theirs)], axis=1)
    got = ring_pieces(local[: STAT + blk // 2], local[STAT + blk // 2 :])

    w_recv = swap_core(w_sent)
    difference = cen[0] - cen[1] + (stats[0] - stats[1])[None, :]
    diff_share = (25.0 * jnp.sum(difference * difference) / (total_rows * full_width)).reshape(1, 1)

    wide = NZ * blk + 128
    flat_got = [piece for pair in got for piece in pair]
    whole = lambda s: pl.BlockSpec(s, lambda: (0,) * len(s))
    gathered, gram_part, view_stats = pl.pallas_call(
        functools.partial(gram_kernel, 1.0 / (full_width * NZ)),
        in_specs=[whole((1, 1))] + [whole(piece.shape) for piece in flat_got],
        out_specs=[whole((NZ * blk, 2 * sub)), whole((blk, wide)), whole((8, 2 * sub))],
        out_shape=[
            shape((NZ * blk, 2 * sub), BF),
            shape((blk, wide), BF),
            shape((8, 2 * sub), F32),
        ],
        name="gram",
    )(diff_share, *flat_got)

    stats_own = view_stats[:, :sub]
    stats_back = swap_core(view_stats[:, sub:])
    both_stats = jnp.stack(
        [jnp.where(first, stats_own, stats_back), jnp.where(first, stats_back, stats_own)]
    )
    variance = both_stats[:, 0]
    centered = cen + both_stats[:, 1][:, None, :]
    deviation = jnp.sqrt(variance + 0.0001)

    pieces = exchange(gram_part.reshape(NX * NY, blk // (NX * NY), wide), CHIPS)
    turned = (NY, kpart, flat)
    h_own, h_oth, w_turned = pl.pallas_call(
        turn_kernel,
        grid=(NY,),
        in_specs=[at_dim(hblock, 1), at_dim(hblock, 1)] + [at_dim((1, kpart, sub), 0)] * 2,
        out_specs=[at_dim((1, kpart, flat), 0)] * 2 + [at_dim((1, 2 * sub, kpart), 0)],
        out_shape=[shape(turned, BF), shape(turned, BF), shape((NY, 2 * sub, kpart), BF)],
        name="turn",
    )(h_own, h_oth, w_kept, w_recv)
    gram_rows = jnp.sum(pieces[:, :, : NZ * blk].astype(F32), axis=0).astype(BF)
    share = jnp.sum(pieces[:, :, NZ * blk :].astype(F32))
    gram_rows, share, variance, h_own, h_oth, w_turned = lax.optimization_barrier(
        (gram_rows, share, variance, h_own, h_oth, w_turned)
    )
    gram_half = exchange(copies(gram_rows, NX * NY), CHIPS).reshape(blk, NZ * blk)
    squares = gram_half.astype(F32)
    squares = jnp.sum(squares * squares)
    share = (share + squares / ((total_rows - 1.0) ** 2 * full_width)).reshape(1, 1)
    spread_view = dot(gram_half, gathered, 1, 0)
    spread_own = spread_view[:, :sub]
    spread_back = swap_core(spread_view[:, sub:])
    spread = jnp.stack(
        [jnp.where(first, spread_own, spread_back), jnp.where(first, spread_back, spread_own)]
    )

    inv_grad = 50.0 / 256.0 * jnp.stack([difference, -difference])
    binding = (deviation < 1.0).astype(F32)
    hinge_grad = (
        -(25.0 * total_rows / (256.0 * (total_rows - 1.0)))
        * (binding / deviation)[:, None, :]
        * centered
    )
    cov_grad = (
        4.0
        * total_rows
        / 256.0
        * (spread / (total_rows - 1.0) ** 2 - variance[:, None, :] * centered / (total_rows - 1.0))
    )
    grad_views = (inv_grad + hinge_grad + cov_grad).astype(BF)
    grads = grad_views.reshape(2, NX, rows, sub).transpose(1, 0, 2, 3).reshape(flat, sub)

    far_block = pl.BlockSpec((NY, kz, flat), lambda j, place: (0, lax.rem(place[1], HALF), 0))
    held = lambda s: pl.BlockSpec(s, lambda j, place: (0,) * len(s))
    half = NX // 2 * kz
    far_right, far_left = pl.pallas_call(
        far_kernel,
        grid_spec=pltpu.PrefetchScalarGridSpec(
            num_scalar_prefetch=1,
            grid=(1,),
            in_specs=[far_block, far_block, held((flat, sub)), held((1, 1))],
            out_specs=[held((half, sub)), held((half + STAT, sub))],
        ),
        out_shape=[shape((half, sub), BF), shape((half + STAT, sub), BF)],
        name="far_terms",
    )(place, h_own, h_oth, grads, share)
    right = hop(far_right, 1)
    left = hop(far_left, -1)

    later, _, _ = lax.optimization_barrier((grads, far_right, far_left))
    input_part = pl.pallas_call(
        input_kernel,
        grid=(NY,),
        in_specs=[fixed((flat, sub)), fixed((flat, sub)), at_dim((1, 2 * sub, kpart), 0)],
        out_specs=at_dim((1, flat, kpart), 0),
        out_shape=shape((NY, flat, kpart), BF),
        name="input_terms",
    )(later, swap_core(grads), w_turned)
    input_parts = exchange(input_part.reshape(NX * NY, 2, rows, kpart), ("y", "x"))

    later, _ = lax.optimization_barrier((later, input_part))
    terms = NX * kz + STAT
    weight_part = pl.pallas_call(
        weight_kernel,
        grid=(NY,),
        in_specs=[smem] + [at_dim((1, kpart, flat), 0)] * 2 + [fixed((flat, sub)), fixed((1, 1))],
        out_specs=fixed((NZ, terms, sub)),
        out_shape=shape((NZ, terms, sub), BF),
        name="weight_terms",
    )(place, h_own, h_oth, later, share)

    arrived = ring_sum(weight_part, right, left)
    loss_rows = sum(v[NX * kz :].astype(F32) for v in arrived)
    weight_sum = sum(v[: NX * kz].astype(F32) for v in arrived).astype(BF).reshape(NX, kz, sub)
    weight_sum, loss_rows, input_parts = lax.optimization_barrier((weight_sum, loss_rows, input_parts))
    loss_part = jnp.sum(loss_rows).reshape(1, 1)
    blocks = exchange(weight_sum, "x")
    input_grads = jnp.sum(input_parts.astype(F32), axis=0).astype(BF)
    grad_weight = jnp.concatenate([blocks[k] for k in range(NX)], axis=1)
    total_loss = (loss_part + swap_core(loss_part))[0, 0]
    return (total_loss, grad_weight, input_grads[0], input_grads[1])


def solution(mesh):
    grid = Mesh(mesh.devices.reshape(NX, NZ, NY, NC), ("x", "z", "y", "c"))
    placed = P(("x", "z"), ("y", "c"))

    return jax.shard_map(
        on_device,
        mesh=grid,
        in_specs=(placed, placed, placed),
        out_specs=(P(), placed, placed, placed),
        check_vma=False,
    )
```

```python
import functools

import jax
import jax.numpy as jnp
from jax import lax
from jax.experimental import pallas as pl
from jax.experimental.pallas import tpu as pltpu
from jax.sharding import Mesh, PartitionSpec as P


BF = jnp.bfloat16
F32 = jnp.float32
NX, NZ, NY, NC = 4, 8, 4, 2
HALF = NZ // 2
CHIPS = ("x", "y")
SMEM = pltpu.SMEM
STAT = 16
PER = 2


def swap_core(v):
    return lax.ppermute(v, "c", [(0, 1), (1, 0)])


def hop(v, k):
    return lax.ppermute(v, "z", [(i, (i + k) % NZ) for i in range(NZ)])


def exchange(v, axes):
    return lax.all_to_all(v, axes, split_axis=0, concat_axis=0, tiled=True)


def copies(v, n):
    return jnp.broadcast_to(v[None], (n,) + v.shape)


def ring_blocks(v):
    right, left = [v], [v]
    for _ in range(1, HALF):
        right.append(hop(right[-1], 1))
        left.append(hop(left[-1], -1))
    half = v.shape[0] // 2
    far = (hop(right[-1][:half], 1), hop(left[-1][half:], -1))
    return left[1:], right[:0:-1], far


def ring_pieces(first, second):
    got = [[None, None] for _ in range(NZ)]
    got[0] = [first, second]
    for k in range(1, HALF + 1):
        for p in (0, 1):
            if k < HALF or p == 0:
                got[-k % NZ][p] = hop(got[(1 - k) % NZ][p], 1)
            if k < HALF or p == 1:
                got[k][p] = hop(got[k - 1][p], -1)
    return got


def ring_sum(terms, right, left):
    for d in range(HALF - 1, 0, -1):
        right, left = lax.optimization_barrier((right, left))
        right, left = right.astype(F32), left.astype(F32)
        if d == HALF - 1:
            low, high = jnp.zeros(left.shape, F32), jnp.zeros(right.shape, F32)
            right = jnp.concatenate([right, low], axis=0)
            left = jnp.concatenate([high, left], axis=0)
        right = hop((terms[d].astype(F32) + right).astype(BF), 1)
        left = hop((terms[NZ - d].astype(F32) + left).astype(BF), -1)
    return terms[0].astype(F32) + right.astype(F32) + left.astype(F32)


def split3(v):
    hi = v.astype(BF).astype(F32)
    mid = (v - hi).astype(BF).astype(F32)
    return [hi, mid, v - hi - mid]


def dot(a, b, ca, cb):
    return lax.dot_general(a, b, (((ca,), (cb,)), ((), ())), preferred_element_type=F32)


def fixed(shape):
    return pl.BlockSpec(shape, lambda j: (0,) * len(shape))


def at_dim(shape, dim):
    return pl.BlockSpec(shape, lambda j: tuple(j if d == dim else 0 for d in range(len(shape))))


def flat_rows(ref, y=0):
    nx, _, nv, rows, width = ref.shape
    return ref[:, y].reshape(nx * nv * rows, width)


def views_kernel(place_ref, own_ref, oth_ref, *refs):
    w_refs, refs = refs[:7], refs[7:]
    far_a, far_b, kept_ref, sent_ref, cen_ref, mine_ref, theirs_ref, stat_ref, w_ref, acc = refs
    step = pl.program_id(0)
    core = place_ref[0]
    zi = place_ref[1]
    nx, _, nv, rows, kpart = own_ref.shape
    sub = acc.shape[1]
    for k, ref in zip((0, 1, 2, 3, 5, 6, 7), w_refs):
        w_ref[lax.rem(zi + k, NZ)] = ref[0]
    w_ref[lax.rem(zi + HALF, NZ)] = jnp.where(step < NY // 2, far_a[0], far_b[0])
    w_own = w_ref[pl.ds(core * HALF, HALF)].reshape(kpart, sub)
    w_oth = w_ref[pl.ds((1 - core) * HALF, HALF)].reshape(kpart, sub)
    kept_ref[0] = w_own
    sent_ref[0] = w_oth
    term = dot(flat_rows(own_ref), w_own, 1, 0) + dot(flat_rows(oth_ref), w_oth, 1, 0)

    @pl.when(step == 0)
    def _():
        acc[...] = term

    @pl.when(step > 0)
    def _():
        acc[...] += term

    @pl.when(step == pl.num_programs(0) - 1)
    def _():
        means, tails = [], []
        for v in range(nv):
            blocks = [acc[(a * nv + v) * rows : (a * nv + v + 1) * rows] for a in range(nx)]
            mean = sum(jnp.sum(block, axis=0, keepdims=True) for block in blocks) / (nx * rows * 1.0)
            means.append(mean)
            total = jnp.zeros_like(mean)
            for a in range(nx):
                block = blocks[a] - mean
                cen_ref[v, a * rows : (a + 1) * rows] = block
                total = total + jnp.sum(block * block, axis=0, keepdims=True)
            pad = jnp.zeros((STAT - 6, sub), F32)
            tails.append(jnp.concatenate(split3(mean) + split3(total) + [pad], axis=0).astype(BF))
        stat_ref[...] = jnp.concatenate(means + [jnp.zeros((6, sub), F32)], axis=0)
        data = [cen_ref[v].astype(BF) for v in range(nv)]
        for ref, same in ((mine_ref, core == 0), (theirs_ref, core == 1)):
            ref[:STAT] = jnp.where(same, tails[0], tails[1])
            ref[STAT:] = jnp.where(same, data[0], data[1])


def gram_kernel(scale_each, diff_ref, *refs):
    pieces, (all_ref, gram_ref, stat_ref) = refs[: 2 * NZ], refs[2 * NZ :]
    top = pieces[0].shape[0] - STAT
    blk = top + pieces[1].shape[0]
    stats = [pieces[2 * k][:STAT].astype(F32) for k in range(NZ)]
    means = [s[0:1] + s[1:2] + s[2:3] for s in stats]
    center = sum(means) / (NZ * 1.0)
    total = sum(s[3:4] + s[4:5] + s[5:6] for s in stats)
    for k in range(NZ):
        move = means[k] - center
        total = total + blk * (move * move)
        all_ref[k * blk : k * blk + top] = (pieces[2 * k][STAT:].astype(F32) + move).astype(BF)
        all_ref[k * blk + top : (k + 1) * blk] = (pieces[2 * k + 1][...].astype(F32) + move).astype(BF)
        gram_ref[:, k * blk : (k + 1) * blk] = dot(
            all_ref[:blk], all_ref[k * blk : (k + 1) * blk], 1, 1
        ).astype(BF)
    variance = total / (NZ * blk - 1.0)
    pad = jnp.zeros((6, total.shape[1]), F32)
    stat_ref[...] = jnp.concatenate([variance, means[0] - center, pad], axis=0)
    hinge = jnp.maximum(1.0 - jnp.sqrt(variance + 0.0001), 0.0)
    share = diff_ref[...] + scale_each * jnp.sum(25.0 * hinge - variance * variance, axis=1, keepdims=True)
    extra = gram_ref.shape[1] - NZ * blk
    row = lax.broadcasted_iota(jnp.int32, (blk, extra), 0)
    lane = lax.broadcasted_iota(jnp.int32, (blk, extra), 1)
    lead = lax.rem(row, blk // (NX * NY)) == 0
    gram_ref[:, NZ * blk :] = in_lanes(share, lane, 0, lead).astype(BF)


def in_lanes(value, lane, start, keep):
    out = jnp.zeros(lane.shape, F32)
    for n, term in enumerate(split3(value)):
        out = jnp.where(keep & (lane == start + n), term, out)
    return out


def turn_kernel(own_ref, oth_ref, kept_ref, recv_ref, own_out, oth_out, w_out):
    own_out[0] = flat_rows(own_ref).T
    oth_out[0] = flat_rows(oth_ref).T
    sub = kept_ref.shape[2]
    w_out[0, :sub] = kept_ref[0].T
    w_out[0, sub:] = recv_ref[0].T


def weight_kernel(place_ref, own_ref, oth_ref, g_ref, share_ref, out_ref):
    step = pl.program_id(0)
    core = place_ref[0]
    zi = place_ref[1]
    kz = own_ref.shape[1] // HALF
    rows = NY * kz
    for ref, lead in ((own_ref, core), (oth_ref, 1 - core)):
        term = dot(ref[...].reshape(-1, ref.shape[2]), g_ref[...], 1, 0).astype(BF)
        for y in range(PER):
            place = pl.ds(pl.multiple_of((step * PER + y) * kz, kz), kz)
            for q in range(HALF):
                lo = (y * HALF + q) * kz
                out_ref[lax.rem(lead * HALF + q - zi + NZ, NZ), place] = term[lo : lo + kz]

    @pl.when(step == 0)
    def _():
        row = lax.broadcasted_iota(jnp.int32, (STAT, out_ref.shape[2]), 0)
        lane = lax.broadcasted_iota(jnp.int32, (STAT, out_ref.shape[2]), 1)
        tail = in_lanes(share_ref[...], lane, 3 * zi, row == 0).astype(BF)
        for k in range(NZ):
            out_ref[k, rows:] = tail


def far_kernel(place_ref, own_ref, oth_ref, g_ref, share_ref, a_ref, b_ref):
    core = place_ref[0]
    zi = place_ref[1]
    kz = own_ref.shape[1]
    mine = 1 - zi // HALF == core
    block = jnp.where(mine, own_ref[...].astype(F32), oth_ref[...].astype(F32)).astype(BF)
    term = dot(block.reshape(NY * kz, own_ref.shape[2]), g_ref[...], 1, 0).astype(BF)
    a_ref[...] = term[: NY // 2 * kz]
    b_ref[: NY // 2 * kz] = term[NY // 2 * kz :]
    row = lax.broadcasted_iota(jnp.int32, (STAT, b_ref.shape[1]), 0)
    lane = lax.broadcasted_iota(jnp.int32, (STAT, b_ref.shape[1]), 1)
    b_ref[NY // 2 * kz :] = in_lanes(share_ref[...], lane, 3 * zi, row == 0).astype(BF)


def input_kernel(own_ref, oth_ref, w_ref, out_ref):
    sub = own_ref.shape[1]
    term = dot(own_ref[...], w_ref[0, :sub], 1, 0) + dot(oth_ref[...], w_ref[0, sub:], 1, 0)
    out_ref[0] = term.astype(BF)


def on_device(hidden_first, hidden_second, weight):
    core = lax.axis_index("c")
    place = jnp.stack([core, lax.axis_index("z")]).astype(jnp.int32)
    first = core == 0
    rows, kpart = hidden_first.shape
    kz, cols = weight.shape
    total_rows = rows * NX * NZ * 1.0
    full_width = cols * NY * NC * 1.0
    blk = rows * NX
    flat = 2 * blk
    sub = cols // NX
    hshape = (NX, NY, 2, rows, kpart)
    hblock = (NX, 1, 2, rows, kpart)
    smem = pl.BlockSpec(memory_space=SMEM)
    shape = jax.ShapeDtypeStruct

    w_parts = exchange(jnp.stack([weight[:, k * sub : (k + 1) * sub] for k in range(NX)]), "x")
    moved = copies(jnp.stack([hidden_first, hidden_second]), NX * NY)
    moved, w_parts = lax.optimization_barrier((moved, w_parts))
    h_own = exchange(moved, CHIPS).reshape(hshape)
    after, before, (far_a, far_b) = ring_blocks(w_parts)
    h_own, _, _ = lax.optimization_barrier((h_own, after[-1], before[0]))
    h_oth = swap_core(h_own)

    block_spec = at_dim((1, kz, sub), 0)
    w_kept, w_sent, cen, mine, theirs, stats = pl.pallas_call(
        views_kernel,
        grid=(NY,),
        in_specs=[smem, at_dim(hblock, 1), at_dim(hblock, 1)]
        + [block_spec] * 7
        + [
            pl.BlockSpec((1, kz, sub), lambda j: (jnp.minimum(j, NX // 2 - 1), 0, 0)),
            pl.BlockSpec((1, kz, sub), lambda j: (jnp.maximum(j - NX // 2, 0), 0, 0)),
        ],
        out_specs=[
            at_dim((1, kpart, sub), 0),
            at_dim((1, kpart, sub), 0),
            fixed((2, blk, sub)),
            fixed((blk + STAT, sub)),
            fixed((blk + STAT, sub)),
            fixed((8, sub)),
        ],
        out_shape=[
            shape((NY, kpart, sub), BF),
            shape((NY, kpart, sub), BF),
            shape((2, blk, sub), F32),
            shape((blk + STAT, sub), BF),
            shape((blk + STAT, sub), BF),
            shape((8, sub), F32),
        ],
        scratch_shapes=[pltpu.VMEM((NZ, kz, sub), BF), pltpu.VMEM((flat, sub), F32)],
        name="views",
    )(place, h_own, h_oth, w_parts, *after, *before, far_a, far_b)

    local = jnp.concatenate([mine, swap_core(theirs)], axis=1)
    got = ring_pieces(local[: STAT + blk // 2], local[STAT + blk // 2 :])

    w_recv = swap_core(w_sent)
    difference = cen[0] - cen[1] + (stats[0] - stats[1])[None, :]
    diff_share = (25.0 * jnp.sum(difference * difference) / (total_rows * full_width)).reshape(1, 1)

    wide = NZ * blk + 128
    flat_got = [piece for pair in got for piece in pair]
    whole = lambda s: pl.BlockSpec(s, lambda: (0,) * len(s))
    gathered, gram_part, view_stats = pl.pallas_call(
        functools.partial(gram_kernel, 1.0 / (full_width * NZ)),
        in_specs=[whole((1, 1))] + [whole(piece.shape) for piece in flat_got],
        out_specs=[whole((NZ * blk, 2 * sub)), whole((blk, wide)), whole((8, 2 * sub))],
        out_shape=[
            shape((NZ * blk, 2 * sub), BF),
            shape((blk, wide), BF),
            shape((8, 2 * sub), F32),
        ],
        name="gram",
    )(diff_share, *flat_got)

    stats_own = view_stats[:, :sub]
    stats_back = swap_core(view_stats[:, sub:])
    both_stats = jnp.stack(
        [jnp.where(first, stats_own, stats_back), jnp.where(first, stats_back, stats_own)]
    )
    variance = both_stats[:, 0]
    centered = cen + both_stats[:, 1][:, None, :]
    deviation = jnp.sqrt(variance + 0.0001)

    pieces = exchange(gram_part.reshape(NX * NY, blk // (NX * NY), wide), CHIPS)
    turned = (NY, kpart, flat)
    h_own, h_oth, w_turned = pl.pallas_call(
        turn_kernel,
        grid=(NY,),
        in_specs=[at_dim(hblock, 1), at_dim(hblock, 1)] + [at_dim((1, kpart, sub), 0)] * 2,
        out_specs=[at_dim((1, kpart, flat), 0)] * 2 + [at_dim((1, 2 * sub, kpart), 0)],
        out_shape=[shape(turned, BF), shape(turned, BF), shape((NY, 2 * sub, kpart), BF)],
        name="turn",
    )(h_own, h_oth, w_kept, w_recv)
    gram_rows = jnp.sum(pieces[:, :, : NZ * blk].astype(F32), axis=0).astype(BF)
    share = jnp.sum(pieces[:, :, NZ * blk :].astype(F32))
    gram_rows, share, variance, h_own, h_oth, w_turned = lax.optimization_barrier(
        (gram_rows, share, variance, h_own, h_oth, w_turned)
    )
    gram_half = exchange(copies(gram_rows, NX * NY), CHIPS).reshape(blk, NZ * blk)
    squares = gram_half.astype(F32)
    share = (share + jnp.sum(squares * squares) / ((total_rows - 1.0) ** 2 * full_width)).reshape(1, 1)
    spread_view = dot(gram_half, gathered, 1, 0)
    spread_own = spread_view[:, :sub]
    spread_back = swap_core(spread_view[:, sub:])
    spread = jnp.stack(
        [jnp.where(first, spread_own, spread_back), jnp.where(first, spread_back, spread_own)]
    )

    inv_grad = 50.0 / 256.0 * jnp.stack([difference, -difference])
    binding = (deviation < 1.0).astype(F32)
    hinge_grad = (
        -(25.0 * total_rows / (256.0 * (total_rows - 1.0)))
        * (binding / deviation)[:, None, :]
        * centered
    )
    cov_grad = (
        4.0
        * total_rows
        / 256.0
        * (spread / (total_rows - 1.0) ** 2 - variance[:, None, :] * centered / (total_rows - 1.0))
    )
    grad_views = (inv_grad + hinge_grad + cov_grad).astype(BF)
    grads = grad_views.reshape(2, NX, rows, sub).transpose(1, 0, 2, 3).reshape(flat, sub)

    far_block = pl.BlockSpec((NY, kz, flat), lambda j, place: (0, lax.rem(place[1], HALF), 0))
    held = lambda s: pl.BlockSpec(s, lambda j, place: (0,) * len(s))
    half = NX // 2 * kz
    far_right, far_left = pl.pallas_call(
        far_kernel,
        grid_spec=pltpu.PrefetchScalarGridSpec(
            num_scalar_prefetch=1,
            grid=(1,),
            in_specs=[far_block, far_block, held((flat, sub)), held((1, 1))],
            out_specs=[held((half, sub)), held((half + STAT, sub))],
        ),
        out_shape=[shape((half, sub), BF), shape((half + STAT, sub), BF)],
        name="far_terms",
    )(place, h_own, h_oth, grads, share)
    right = hop(far_right, 1)
    left = hop(far_left, -1)

    later, _, _ = lax.optimization_barrier((grads, far_right, far_left))
    input_part = pl.pallas_call(
        input_kernel,
        grid=(NY,),
        in_specs=[fixed((flat, sub)), fixed((flat, sub)), at_dim((1, 2 * sub, kpart), 0)],
        out_specs=at_dim((1, flat, kpart), 0),
        out_shape=shape((NY, flat, kpart), BF),
        name="input_terms",
    )(later, swap_core(grads), w_turned)
    input_parts = exchange(input_part.reshape(NX * NY, 2, rows, kpart), ("y", "x"))

    later, _ = lax.optimization_barrier((later, input_part))
    terms = NX * kz + STAT
    weight_part = pl.pallas_call(
        weight_kernel,
        grid=(NY // PER,),
        in_specs=[smem] + [at_dim((PER, kpart, flat), 0)] * 2 + [fixed((flat, sub)), fixed((1, 1))],
        out_specs=fixed((NZ, terms, sub)),
        out_shape=shape((NZ, terms, sub), BF),
        name="weight_terms",
    )(place, h_own, h_oth, later, share)

    weight_sum = ring_sum(weight_part, right, left)
    loss_rows = weight_sum[NX * kz :]
    weight_sum = weight_sum[: NX * kz].astype(BF).reshape(NX, kz, sub)
    weight_sum, loss_rows, input_parts = lax.optimization_barrier((weight_sum, loss_rows, input_parts))
    loss_part = jnp.sum(loss_rows).reshape(1, 1)
    blocks = exchange(weight_sum, "x")
    input_grads = jnp.sum(input_parts.astype(F32), axis=0).astype(BF)
    grad_weight = jnp.concatenate([blocks[k] for k in range(NX)], axis=1)
    total_loss = (loss_part + swap_core(loss_part))[0, 0]
    return (total_loss, grad_weight, input_grads[0], input_grads[1])


def solution(mesh):
    grid = Mesh(mesh.devices.reshape(NX, NZ, NY, NC), ("x", "z", "y", "c"))
    placed = P(("x", "z"), ("y", "c"))

    return jax.shard_map(
        on_device,
        mesh=grid,
        in_specs=(placed, placed, placed),
        out_specs=(P(), placed, placed, placed),
        check_vma=False,
    )
```
